256 devices in a mesh: expert: 64 (over y, z_hi, x, core), hidden: 4 (over z_lo).
Axes of the slice: x: 4, y: 4, z: 8 (z_hi: 2, z_lo: 4; z = z_hi * 4 + z_lo), core: 2. Of those that a mesh axis runs over, the one named last changes fastest.
Arguments:
- tokens: bfloat16 [50176, 768], P(('expert', 'hidden')), may hold values from -512 to 512
- out_grad: bfloat16 [50176, 768], P(('expert', 'hidden')), may hold values from -12 to 12
- slot_router: bfloat16 [768, 256], replicated, may hold values from -0.5 to 0.5
- weight_in: bfloat16 [128, 768, 3072], P('expert', None, 'hidden'), may hold values from -0.21875 to 0.21875
- weight_out: bfloat16 [128, 3072, 768], P('expert', 'hidden'), may hold values from -0.109375 to 0.109375
Outputs:
- token_grad: bfloat16 [50176, 768], P(('expert', 'hidden'))
- router_grad: float32 [768, 256], P('hidden', 'expert')
- weight_in_grad: bfloat16 [128, 768, 3072], P('expert', None, 'hidden')
- weight_out_grad: bfloat16 [128, 3072, 768], P('expert', 'hidden')
The draws below stay inside these ranges and needn't reach their ends.
All inputs are finite; a program needn't handle non-finite values.
Results may differ from the reference program's by a relative error of at most 0.019.
Values may be sent and summed in bfloat16 or wider, within the bound.
A program may use at most 64 MiB of HBM per device.

```python
import jax
import jax.numpy as jnp
from jax import lax

D = 768
FF = 3072
SLOTS = 2
TOK = 196
EXPERTS = 128
IMAGES = 256
ROWS = 50176
N_HIDDEN = 4


def router_values(key):
    raw_values = jax.random.normal(jax.random.fold_in(key, 11), (D, EXPERTS * SLOTS), jnp.float32)
    return 0.08 * jnp.clip(raw_values, -6.0, 6.0)


def draw_slot_router(key, part):
    return router_values(key).astype(jnp.bfloat16)


def draw_tokens(key, part):
    base_values = jnp.clip(jax.random.normal(jax.random.fold_in(key, 21), (IMAGES, TOK, D), jnp.float32), -6.0, 6.0)
    return base_values.reshape(IMAGES * TOK, D).astype(jnp.bfloat16)


def levels(own_key, shape, split, low, top_value):
    def one(dim, blocks):
        draws = jax.random.uniform(jax.random.fold_in(jax.random.fold_in(own_key, 6), dim), (blocks,), jnp.float32, low / len(split), top_value / len(split))
        return jnp.repeat(jnp.exp(draws), shape[dim] // blocks).reshape((-1,) + (1,) * (len(shape) - dim - 1))

    gain = one(*split[0])
    for cut in split[1:]:
        gain = gain * one(*cut)
    return gain


def bell_draw(key, shape, scale, most, cuts=(), dtype=jnp.bfloat16):
    gain = levels(key, shape, cuts, -0.22, 0.18) if cuts else 1.0
    values = jax.random.normal(key, shape, jnp.float32) * scale * gain
    return jnp.minimum(jnp.maximum(values, -most), most).astype(dtype)


def setup_inputs(seed: int = 0) -> dict:
    key_of = jax.random.split(jax.random.key(seed), 6)
    tokens = draw_tokens(jax.random.fold_in(key_of[5], 71), 0)
    out_grad = bell_draw(key_of[1], (ROWS, D), 2.0, 12.0, ((0, 256),))
    slot_router = draw_slot_router(jax.random.fold_in(key_of[5], 71), 0)
    weight_in = bell_draw(key_of[3], (EXPERTS, D, FF), D ** -0.5, 0.21875, ((0, 64), (2, 4)))
    weight_out = bell_draw(key_of[4], (EXPERTS, FF, D), FF ** -0.5, 0.109375, ((0, 64), (1, 4)))
    return dict(tokens=tokens, out_grad=out_grad, slot_router=slot_router, weight_in=weight_in, weight_out=weight_out)


def gelu_value(values):
    return 0.5 * values * (1.0 + lax.erf(values * 0.7071067811865476))


def gelu_slope(values):
    return 0.5 * (1.0 + lax.erf(values * 0.7071067811865476)) + values * jnp.exp(-0.5 * values * values) * 0.3989422804014327


def reference(tokens, out_grad, slot_router, weight_in, weight_out):
    high = lax.Precision.HIGHEST
    images = tokens.shape[0] // TOK
    experts = weight_in.shape[0]
    inputs = tokens.reshape(images, TOK, D)
    out_grads = out_grad.reshape(images, TOK, D)
    inputs32 = inputs.astype(jnp.float32)
    out_grads32 = out_grads.astype(jnp.float32)
    router32 = slot_router.astype(jnp.float32)
    logits = jnp.einsum('btd,dc->btc', inputs32, router32, precision=high)
    dispatch = jax.nn.softmax(logits, axis=1)
    combine = jax.nn.softmax(logits, axis=2)
    dispatch16 = dispatch.astype(jnp.bfloat16)
    combine16 = combine.astype(jnp.bfloat16)
    slot_in = jnp.einsum('btc,btd->bcd', dispatch16.astype(jnp.float32), inputs32, precision=high).astype(jnp.bfloat16)
    slot_grad = jnp.einsum('btc,btd->bcd', combine16.astype(jnp.float32), out_grads32, precision=high).astype(jnp.bfloat16)

    def by_expert(values):
        return values.reshape(images, experts, SLOTS, D).transpose(1, 0, 2, 3).reshape(experts, images * SLOTS, D)

    def back_to_images(values):
        return values.reshape(experts, images, SLOTS, D).transpose(1, 0, 2, 3).reshape(images, experts * SLOTS, D)

    quarter = FF // N_HIDDEN

    def per_expert(items):
        slot_inputs, slot_grads, w_first, w_second = items
        row_count = slot_inputs.shape[0]
        pre_act = jnp.dot(slot_inputs, w_first, preferred_element_type=jnp.float32)
        activated = gelu_value(pre_act).astype(jnp.bfloat16)
        pieces = jnp.einsum('rqf,qfd->qrd', activated.reshape(row_count, N_HIDDEN, quarter).astype(jnp.float32),
                            w_second.reshape(N_HIDDEN, quarter, D).astype(jnp.float32), precision=high)
        slot_out = jnp.sum(pieces.astype(jnp.bfloat16).astype(jnp.float32), axis=0).astype(jnp.bfloat16)
        d_act = jnp.dot(slot_grads, w_second.T, preferred_element_type=jnp.float32)
        d_pre = (d_act * gelu_slope(pre_act)).astype(jnp.bfloat16)
        grad_second = jnp.dot(activated.T, slot_grads, preferred_element_type=jnp.float32).astype(jnp.bfloat16)
        grad_first = jnp.dot(slot_inputs.T, d_pre, preferred_element_type=jnp.float32).astype(jnp.bfloat16)
        back_pieces = jnp.einsum('rqf,dqf->qrd', d_pre.reshape(row_count, N_HIDDEN, quarter).astype(jnp.float32),
                                 w_first.reshape(D, N_HIDDEN, quarter).astype(jnp.float32), precision=high)
        slot_in_grad = jnp.sum(back_pieces.astype(jnp.bfloat16).astype(jnp.float32), axis=0).astype(jnp.bfloat16)
        return slot_out, slot_in_grad, grad_first, grad_second

    slot_out, slot_in_grad, weight_in_grad, weight_out_grad = lax.map(
        per_expert, (by_expert(slot_in), by_expert(slot_grad), weight_in, weight_out))
    slot_out = back_to_images(slot_out).astype(jnp.float32)
    slot_in_grad = back_to_images(slot_in_grad).astype(jnp.float32)
    d_combine = jnp.einsum('btd,bcd->btc', out_grads32, slot_out, precision=high)
    d_dispatch = jnp.einsum('btd,bcd->btc', inputs32, slot_in_grad, precision=high)
    from_combine = combine * (d_combine - jnp.sum(combine * d_combine, axis=2, keepdims=True))
    from_dispatch = dispatch * (d_dispatch - jnp.sum(dispatch * d_dispatch, axis=1, keepdims=True))
    d_logits = (from_combine + from_dispatch).astype(jnp.bfloat16).astype(jnp.float32)
    token_grad = (jnp.einsum('btc,bcd->btd', dispatch16.astype(jnp.float32), slot_in_grad, precision=high)
                  + jnp.einsum('btc,dc->btd', d_logits, router32, precision=high)).astype(jnp.bfloat16)
    router_grad = jnp.einsum('btd,btc->dc', inputs32, d_logits, precision=high)
    return token_grad.reshape(images * TOK, D), router_grad, weight_in_grad, weight_out_grad
```

```python
import functools

import jax
import jax.numpy as jnp
from jax import lax
from jax.experimental import pallas as pl
from jax.experimental.pallas import tpu as pltpu
from jax.sharding import PartitionSpec as P

D = 768
SLOTS = 2
TOK = 196
PLANE = 32
RING = 8
ROWS = 128
COLS = 256
PIECES = 6
LANES = 6
MESH = pl.DeviceIdType.MESH
BF = jnp.bfloat16
F32 = jnp.float32


def place():
    expert = lax.axis_index("expert")
    h = lax.axis_index("hidden")
    p = (expert // 16) * 8 + expert % 8
    zhi = (expert // 8) % 2
    return p, zhi, h


def plane_device(q, zhi, h):
    return ((q // 8) * 16 + zhi * 8 + q % 8, h)


def ring_device(p, z):
    return ((p // 8) * 16 + (z // 4) * 8 + p % 8, z % 4)


def remote(src, dst, send, recv, device):
    return pltpu.make_async_remote_copy(
        src_ref=src, dst_ref=dst, send_sem=send, recv_sem=recv, device_id=device, device_id_type=MESH
    )


def greet(p, zhi, h, ring_offsets):
    barrier = pltpu.get_barrier_semaphore()
    z = zhi * 4 + h

    def one(j, carry):
        pl.semaphore_signal(
            barrier, inc=1, device_id=plane_device((p + j) % PLANE, zhi, h), device_id_type=MESH
        )
        return carry

    lax.fori_loop(1, PLANE, one, 0)
    for offset in ring_offsets:
        pl.semaphore_signal(
            barrier, inc=1, device_id=ring_device(p, (z + offset) % RING), device_id_type=MESH
        )
    pl.semaphore_wait(barrier, PLANE - 1 + len(ring_offsets))


def exchange_kernel(
    sa, sb, win, wout,
    out_a, out_b, gin, gout,
    prcv, fs, rows, tout, ttr, part, rr, ofin, otr, psend, prcv2,
    w_in, w_out, g_in, g_out, act, slope, dpre, acc,
    w_sem, g_sem, ps_send, ps_recv, po_send, po_recv,
    in_send, in_recv, t_send, t_recv, out_send, out_recv, ot_send, ot_recv,
):
    p, zhi, h = place()
    z = zhi * 4 + h
    near = {1: ring_device(p, (z + 1) % RING), -1: ring_device(p, (z + RING - 1) % RING)}
    lam = {1: h, -1: 3 - h}

    def pos(d, j):
        return j if d == 1 else 3 - j

    w_copies = [
        pltpu.make_async_copy(win, w_in, w_sem.at[0]),
        pltpu.make_async_copy(wout, w_out, w_sem.at[1]),
    ]
    for copy in w_copies:
        copy.start()
    greet(p, zhi, h, (1, RING - 1))

    sends = (sa, sb)

    def plane_copy(t, j):
        q = (p + j) % PLANE
        return remote(
            sends[t].at[q], prcv.at[t, p], ps_send.at[t, q], ps_recv.at[t, p], plane_device(q, zhi, h)
        )

    def plane_arrival(t, j):
        q = (p + j) % PLANE
        return remote(
            sends[t].at[q], prcv.at[t, q], ps_send.at[t, q], ps_recv.at[t, q], plane_device(q, zhi, h)
        )

    def loop(body):
        def step(j, carry):
            body(j)
            return carry

        lax.fori_loop(1, PLANE, step, 0)

    for t in (0, 1):
        loop(lambda j, t=t: plane_copy(t, j).start())

    def gather(t):
        prcv[t, p] = sends[t][p]
        loop(lambda j: plane_arrival(t, j).wait_recv())
        for c in range(LANES):
            lanes = slice(c * 128, (c + 1) * 128)
            fs[c] = prcv[t, :, :, lanes].astype(F32).reshape(COLS, 128)
            for s in range(4):
                piece = slice(s * PLANE, (s + 1) * PLANE)
                mine = fs[c, pl.ds(zhi * 4 + s, PLANE, stride=8), :]
                rows[t, z, piece, lanes] = mine.astype(BF)
                other = fs[c, pl.ds((1 - zhi) * 4 + s, PLANE, stride=8), :]
                tout[t, piece, lanes] = other.astype(BF)


    def in_item(d, i):
        own = lam[d] - i
        far = 3 - (i - lam[d] - 1)
        own_z = zhi * 4 + pos(d, own)
        far_z = (1 - zhi) * 4 + pos(d, far)
        return jnp.where(i <= lam[d], own_z, far_z)

    def rows_copy(t, d, zs, k):
        return remote(
            rows.at[t, zs], rows.at[t, zs], in_send.at[t, (1 - d) // 2, k], in_recv.at[t, zs], near[d]
        )

    def in_step(t, k, start):
        for d in (1, -1):
            i = k - jnp.where(lam[d] == 2, 1, 0)
            valid = jnp.logical_and(lam[d] <= 2, jnp.logical_and(i >= 0, i <= lam[d] + 2))

            @pl.when(valid)
            def _(d=d, i=i):
                zs = in_item(d, i)
                copy = rows_copy(t, d, zs, k)
                if start:

                    @pl.when(i > 0)
                    def _():
                        copy.wait_recv()

                    copy.start()
                else:
                    copy.wait_send()

            if k == 0:

                @pl.when(lam[d] == 2)
                def _(d=d):
                    copy = remote(tout.at[t], ttr.at[t], t_send.at[t, 0], t_recv.at[t], near[d])
                    copy.start() if start else copy.wait_send()

                @pl.when(lam[d] == 3)
                def _(d=d):
                    copy = remote(tout.at[t], rows.at[t, z], t_send.at[t, 0], in_recv.at[t, z], near[d])
                    copy.start() if start else copy.wait_send()

            if k == 1:

                @pl.when(lam[d] == 3)
                def _(d=d):
                    zs = zhi * 4 + pos(d, 2)
                    if start:
                        remote(tout.at[t], ttr.at[t], t_send.at[t, 0], t_recv.at[t], near[d]).wait_recv()
                    copy = remote(ttr.at[t], rows.at[t, zs], t_send.at[t, 1], in_recv.at[t, zs], near[d])
                    copy.start() if start else copy.wait_send()

    def in_last(t):
        for d in (1, -1):

            @pl.when(lam[d] == 3)
            def _(d=d):
                for own in (2, 1, 0):
                    rows_copy(t, d, zhi * 4 + pos(d, own), 0).wait_recv()
                for far in (3, 2):
                    rows_copy(t, d, (1 - zhi) * 4 + pos(d, far), 0).wait_recv()


    def out_step(t, k, start):
        for d in (1, -1):
            i = k - (3 - lam[d])
            valid = jnp.logical_and(i >= 0, i <= lam[d] + 1)

            @pl.when(valid)
            def _(d=d, i=i):
                far_z = (1 - zhi) * 4 + pos(d, 2 + i)
                own_z = zhi * 4 + pos(d, i - 2)
                zs = jnp.where(i <= 1, far_z, own_z)
                sem = out_send.at[t, (1 - d) // 2, k]
                if start:

                    @pl.when(lam[d] < 3)
                    def _():
                        remote(part.at[t, zs], rr.at[t, zs], sem, out_recv.at[t, zs], near[-d]).wait_recv()
                        part[t, zs] = (part[t, zs].astype(F32) + rr[t, zs].astype(F32)).astype(BF)

                @pl.when(lam[d] > 0)
                def _():
                    slot = zs
                    if d == -1:
                        slot = jnp.where(i - 2 == lam[d] - 1, RING, zs)
                    copy = remote(part.at[t, zs], rr.at[t, slot], sem, out_recv.at[t, slot], near[-d])
                    copy.start() if start else copy.wait_send()

                @pl.when(jnp.logical_and(lam[d] == 0, i == 0))
                def _():
                    copy = remote(part.at[t, zs], otr.at[t], sem, ot_recv.at[t, 0], near[-d])
                    copy.start() if start else copy.wait_send()

                @pl.when(jnp.logical_and(lam[d] == 0, i == 1))
                def _():
                    copy = remote(part.at[t, zs], ofin.at[t], sem, ot_recv.at[t, 1], near[-d])
                    copy.start() if start else copy.wait_send()

            if k == 5:

                @pl.when(lam[d] == 3)
                def _(d=d):
                    copy = remote(otr.at[t], ofin.at[t], ot_send.at[t], ot_recv.at[t, 1], near[-d])
                    if start:
                        remote(otr.at[t], otr.at[t], ot_send.at[t], ot_recv.at[t, 0], near[-d]).wait_recv()
                        copy.start()
                    else:
                        copy.wait_send()

    def out_last(t):
        @pl.when(h < 3)
        def _():
            remote(part.at[t, z], rr.at[t, z], ot_send.at[t], out_recv.at[t, z], near[1]).wait_recv()
            part[t, z] = (part[t, z].astype(F32) + rr[t, z].astype(F32)).astype(BF)

        @pl.when(h > 0)
        def _():
            remote(part.at[t, z], rr.at[t, RING], ot_send.at[t], out_recv.at[t, RING], near[1]).wait_recv()
            part[t, z] = (part[t, z].astype(F32) + rr[t, RING].astype(F32)).astype(BF)

        remote(otr.at[t], ofin.at[t], ot_send.at[t], ot_recv.at[t, 1], near[1]).wait_recv()
        for c in range(LANES):
            lanes = slice(c * 128, (c + 1) * 128)
            for s in range(4):
                piece = slice(s * PLANE, (s + 1) * PLANE)
                fs[c, pl.ds(zhi * 4 + s, PLANE, stride=8), :] = part[t, z, piece, lanes].astype(F32)
                fs[c, pl.ds((1 - zhi) * 4 + s, PLANE, stride=8), :] = ofin[t, piece, lanes].astype(F32)
            psend[t, :, :, lanes] = fs[c].reshape(PLANE, 8, 128).astype(BF)
        loop(lambda j: back_copy(t, j).start())
        prcv2[t, p] = psend[t, p]

    def back_copy(t, j):
        q = (p + j) % PLANE
        return remote(
            psend.at[t, q], prcv2.at[t, p], po_send.at[t, q], po_recv.at[t, p], plane_device(q, zhi, h)
        )

    def back_arrival(t, j):
        q = (p + j) % PLANE
        return remote(
            psend.at[t, q], prcv2.at[t, q], po_send.at[t, q], po_recv.at[t, q], plane_device(q, zhi, h)
        )


    def expert_rows(t, e):
        return rows[t, :, e * 64 : (e + 1) * 64, :].reshape(RING * 64, D)

    def forward_piece(k):
        e, f = k // 3, k % 3
        span = slice(f * COLS, (f + 1) * COLS)
        pre = jnp.dot(expert_rows(0, e), w_in[e, :, span], preferred_element_type=F32)
        half = 0.5 * (1.0 + lax.erf(pre * 0.7071067811865476))
        value = (pre * half).astype(BF)
        act[e, :, span] = value
        slope[e, :, span] = half + pre * jnp.exp(-0.5 * pre * pre) * 0.3989422804014327
        more = jnp.dot(value, w_out[e, span, :], preferred_element_type=F32)
        collect(0, e, f, more)

    def collect(t, e, f, more):
        if f == 0:
            acc[...] = more
        elif f == 1:
            acc[...] += more
        else:
            total = (acc[...] + more).astype(BF)
            part[t, :, e * 64 : (e + 1) * 64, :] = total.reshape(RING, 64, D)

    def backward_piece(k):
        e, f = k // 3, k % 3
        span = slice(f * COLS, (f + 1) * COLS)
        d_act = lax.dot_general(
            expert_rows(1, e), w_out[e, span, :], (((1,), (1,)), ((), ())), preferred_element_type=F32
        )
        value = (d_act * slope[e, :, span]).astype(BF)
        dpre[e, :, span] = value
        more = lax.dot_general(
            value, w_in[e, :, span], (((1,), (1,)), ((), ())), preferred_element_type=F32
        )
        collect(1, e, f, more)

    def weight_piece(k):
        e, f = k // 3, k % 3
        span = slice(f * COLS, (f + 1) * COLS)
        g_out[e, span, :] = lax.dot_general(
            act[e, :, span], expert_rows(1, e), (((0,), (0,)), ((), ())), preferred_element_type=F32
        ).astype(BF)
        g_in[e, :, span] = lax.dot_general(
            expert_rows(0, e), dpre[e, :, span], (((0,), (0,)), ((), ())), preferred_element_type=F32
        ).astype(BF)

    gather(0)
    in_step(0, 0, True)
    gather(1)
    for k in range(1, PIECES):
        in_step(0, k, True)
    in_last(0)
    for copy in w_copies:
        copy.wait()
    for k in range(PIECES):
        in_step(1, k, True)
        forward_piece(k)
    in_last(1)
    for k in range(PIECES):
        out_step(0, k, True)
        backward_piece(k)
    out_last(0)
    for k in range(PIECES):
        out_step(1, k, True)
        weight_piece(k)
    g_copies = [
        pltpu.make_async_copy(g_in, gin, g_sem.at[0]),
        pltpu.make_async_copy(g_out, gout, g_sem.at[1]),
    ]
    for copy in g_copies:
        copy.start()
    out_last(1)
    loop(lambda j: back_arrival(0, j).wait_recv())
    out_a[...] = prcv2[0]
    loop(lambda j: back_arrival(1, j).wait_recv())
    out_b[...] = prcv2[1]
    for t in (0, 1):
        loop(lambda j, t=t: plane_copy(t, j).wait_send())
        loop(lambda j, t=t: back_copy(t, j).wait_send())
        for k in range(PIECES):
            in_step(t, k, False)
            out_step(t, k, False)
    for copy in g_copies:
        copy.wait()


def exchange(send_a, send_b, weight_in, weight_out):
    vmem = pl.BlockSpec(memory_space=pltpu.VMEM)
    anywhere = pl.BlockSpec(memory_space=pl.ANY)
    dma = pltpu.SemaphoreType.DMA
    experts = weight_in.shape[0]
    width = weight_in.shape[2]
    return pl.pallas_call(
        exchange_kernel,
        out_shape=(
            jax.ShapeDtypeStruct(send_a.shape, BF),
            jax.ShapeDtypeStruct(send_a.shape, BF),
            jax.ShapeDtypeStruct(weight_in.shape, BF),
            jax.ShapeDtypeStruct(weight_out.shape, BF),
        ),
        in_specs=[vmem, vmem, anywhere, anywhere],
        out_specs=(vmem, vmem, anywhere, anywhere),
        scratch_shapes=[
            pltpu.VMEM((2, PLANE, 8, D), BF),
            pltpu.VMEM((LANES, COLS, 128), F32),
            pltpu.VMEM((2, RING, ROWS, D), BF),
            pltpu.VMEM((2, ROWS, D), BF),
            pltpu.VMEM((2, ROWS, D), BF),
            pltpu.VMEM((2, RING, ROWS, D), BF),
            pltpu.VMEM((2, RING + 1, ROWS, D), BF),
            pltpu.VMEM((2, ROWS, D), BF),
            pltpu.VMEM((2, ROWS, D), BF),
            pltpu.VMEM((2, PLANE, 8, D), BF),
            pltpu.VMEM((2, PLANE, 8, D), BF),
            pltpu.VMEM(weight_in.shape, BF),
            pltpu.VMEM(weight_out.shape, BF),
            pltpu.VMEM(weight_in.shape, BF),
            pltpu.VMEM(weight_out.shape, BF),
            pltpu.VMEM((experts, RING * 64, width), BF),
            pltpu.VMEM((experts, RING * 64, width), F32),
            pltpu.VMEM((experts, RING * 64, width), BF),
            pltpu.VMEM((RING * 64, D), F32),
            dma((2,)),
            dma((2,)),
            dma((2, PLANE)),
            dma((2, PLANE)),
            dma((2, PLANE)),
            dma((2, PLANE)),
            dma((2, 2, PIECES)),
            dma((2, RING)),
            dma((2, 2)),
            dma((2,)),
            dma((2, 2, PIECES)),
            dma((2, RING + 1)),
            dma((2,)),
            dma((2, 2)),
        ],
        compiler_params=pltpu.CompilerParams(
            collective_id=0, has_side_effects=True, vmem_limit_bytes=56 * 1024 * 1024
        ),
        name="exchange",
    )(send_a, send_b, weight_in, weight_out)


def window(h):
    return pl.multiple_of((h + h // 2) * 128, 128)


def router_kernel(rp, out, prcv, zs, zr, ps_send, ps_recv, z_send, z_recv):
    p, zhi, h = place()
    z = zhi * 4 + h
    greet(p, zhi, h, tuple(range(1, RING)))

    def loop(body):
        def step(j, carry):
            body(j)
            return carry

        lax.fori_loop(1, PLANE, step, 0)

    def plane_copy(j, slot):
        q = (p + j) % PLANE
        slot = p if slot is None else q
        return remote(rp.at[q], prcv.at[slot], ps_send.at[q], ps_recv.at[slot], plane_device(q, zhi, h))

    loop(lambda j: plane_copy(j, None).start())
    prcv[p] = rp[p]
    loop(lambda j: plane_copy(j, 1).wait_recv())
    zs[...] = jnp.sum(prcv[...].astype(F32), axis=0)
    zr[z] = zs[:, pl.ds(window(h), COLS)]

    def ring_copy(j, slot):
        to = (z + j) % RING
        slot = z if slot is None else to
        return remote(
            zs.at[:, pl.ds(window(to % 4), COLS)], zr.at[slot], z_send.at[to], z_recv.at[slot], ring_device(p, to)
        )

    for j in range(1, RING):
        ring_copy(j, None).start()
    for j in range(1, RING):
        ring_copy(j, 1).wait_recv()
    out[...] = jnp.sum(zr[...], axis=0)
    loop(lambda j: plane_copy(j, None).wait_send())
    for j in range(1, RING):
        ring_copy(j, None).wait_send()


def router_reduce(partial):
    vmem = pl.BlockSpec(memory_space=pltpu.VMEM)
    dma = pltpu.SemaphoreType.DMA
    return pl.pallas_call(
        router_kernel,
        out_shape=jax.ShapeDtypeStruct((8, COLS), F32),
        in_specs=[vmem],
        out_specs=vmem,
        scratch_shapes=[
            pltpu.VMEM((PLANE, 8, D), BF),
            pltpu.VMEM((8, D), F32),
            pltpu.VMEM((RING, 8, COLS), F32),
            dma((PLANE,)),
            dma((PLANE,)),
            dma((RING,)),
            dma((RING,)),
        ],
        compiler_params=pltpu.CompilerParams(collective_id=1, has_side_effects=True),
        name="router",
    )(partial)


def per_device(tokens, out_grad, slot_router, weight_in, weight_out):
    router = slot_router.reshape(D, 4, 2, 8, 4).transpose(0, 1, 3, 2, 4).reshape(D, COLS)
    logits = jnp.dot(tokens, router, preferred_element_type=F32)
    dispatch = jax.nn.softmax(logits, axis=0)
    combine = jax.nn.softmax(logits, axis=1)
    dispatch16 = dispatch.astype(BF)
    combine16 = combine.astype(BF)
    slot_in = jnp.einsum("tc,td->cd", dispatch16, tokens, preferred_element_type=F32).astype(BF)
    slot_grad = jnp.einsum("tc,td->cd", combine16, out_grad, preferred_element_type=F32).astype(BF)
    slot_out, slot_in_grad, grad_first, grad_second = exchange(
        slot_in.reshape(PLANE, 8, D), slot_grad.reshape(PLANE, 8, D), weight_in, weight_out
    )
    slot_out = slot_out.reshape(COLS, D)
    slot_in_grad = slot_in_grad.reshape(COLS, D)
    d_combine = jnp.einsum("td,cd->tc", out_grad, slot_out, preferred_element_type=F32)
    d_dispatch = jnp.einsum("td,cd->tc", tokens, slot_in_grad, preferred_element_type=F32)
    from_combine = combine * (d_combine - jnp.sum(combine * d_combine, axis=1, keepdims=True))
    from_dispatch = dispatch * (d_dispatch - jnp.sum(dispatch * d_dispatch, axis=0, keepdims=True))
    d_logits = (from_combine + from_dispatch).astype(BF)
    router_term = jnp.einsum("tc,td->cd", d_logits, tokens, preferred_element_type=F32).astype(BF)
    router_sum = router_reduce(router_term.reshape(PLANE, 8, D))
    token_grad = (
        jnp.dot(dispatch16, slot_in_grad, preferred_element_type=F32)
        + jnp.einsum("tc,dc->td", d_logits, router, preferred_element_type=F32)
    ).astype(BF)
    _, zhi, h = place()
    router_grad = lax.dynamic_slice(router_sum, (zhi * 4, (h % 2) * 64), (4, 192)).T
    return (token_grad, router_grad, grad_first, grad_second)


def solution(mesh):
    return jax.shard_map(
        per_device,
        mesh=mesh,
        in_specs=(
            P(("expert", "hidden"), None),
            P(("expert", "hidden"), None),
            P(),
            P("expert", None, "hidden"),
            P("expert", "hidden", None),
        ),
        out_specs=(
            P(("expert", "hidden"), None),
            P("hidden", "expert"),
            P("expert", None, "hidden"),
            P("expert", "hidden", None),
        ),
        check_vma=False,
    )
```

```python
import functools

import jax
import jax.numpy as jnp
from jax import lax
from jax.experimental import pallas as pl
from jax.experimental.pallas import tpu as pltpu
from jax.sharding import PartitionSpec as P

D = 768
SLOTS = 2
TOK = 196
PLANE = 32
RING = 8
ROWS = 128
COLS = 256
HALF = 64
COPIES = 80
LANES = 6
MESH = pl.DeviceIdType.MESH
BF = jnp.bfloat16
F32 = jnp.float32


def place():
    expert = lax.axis_index("expert")
    h = lax.axis_index("hidden")
    p = lax.div(expert, 16) * 8 + lax.rem(expert, 8)
    zhi = lax.rem(lax.div(expert, 8), 2)
    return p, zhi, h


def plane_device(q, zhi, h):
    return (lax.div(q, 8) * 16 + zhi * 8 + lax.rem(q, 8), h)


def ring_device(p, z):
    return (lax.div(p, 8) * 16 + lax.div(z, 4) * 8 + lax.rem(p, 8), lax.rem(z, 4))


def remote(src, dst, send, recv, device):
    return pltpu.make_async_remote_copy(
        src_ref=src, dst_ref=dst, send_sem=send, recv_sem=recv, device_id=device, device_id_type=MESH
    )


def greet(p, zhi, h, ring_offsets):
    barrier = pltpu.get_barrier_semaphore()
    z = zhi * 4 + h

    def one(j, carry):
        pl.semaphore_signal(
            barrier, inc=1, device_id=plane_device(lax.rem(p + j, PLANE), zhi, h), device_id_type=MESH
        )
        return carry

    lax.fori_loop(1, PLANE, one, 0)
    for offset in ring_offsets:
        pl.semaphore_signal(
            barrier, inc=1, device_id=ring_device(p, (z + offset) % RING), device_id_type=MESH
        )
    pl.semaphore_wait(barrier, PLANE - 1 + len(ring_offsets))


EVENTS = (
    ("gather",),
    ("fwd", 0),
    ("fwd", 1),
    ("bwd", 0),
    ("wg", 0, 0),
    ("wg", 0, 1),
    ("wg", 0, 2),
    ("bwd", 1),
    ("wg", 1, 0),
    ("wg", 1, 1),
    ("wg", 1, 2),
    ("last", 0),
    ("last", 1),
)
EDGE = (
    (("io", 0, "l", 0), ("iO", 0, "h", 3), ("io", 1, "l", 0), ("iO", 1, "h", 3)),
    (("iX", 0, "l", 3), ("ix", 0, "h", 2), ("iX", 1, "l", 3), ("iO", 2, "h", 3), ("iX", 0, "l", 2), ("iO", 3, "h", 3), ("ix", 1, "h", 2), ("iX", 2, "l", 3), ("io", 2, "l", 0), ("iX", 1, "l", 2), ("iX", 3, "l", 3), ("io", 3, "l", 0)),
    (("oX", 0, "h", 2), ("oX", 0, "h", 3), ("oo", 0, "h", 0)),
    (("oo", 0, "h", 1), ("ix", 2, "h", 2), ("oo", 0, "h", 2), ("oX", 1, "h", 2), ("iX", 2, "l", 2), ("oX", 1, "h", 3), ("oo", 1, "h", 0), ("ix", 3, "h", 2), ("oo", 1, "h", 1), ("oo", 1, "h", 2), ("oX", 0, "l", 2), ("iX", 3, "l", 2), ("oX", 0, "l", 3), ("oT", 0, "h", 2)),
    (("oX", 2, "h", 2),),
    (("oX", 2, "h", 3),),
    (("oo", 2, "h", 0),),
    (("oo", 2, "h", 1),),
    (("oo", 2, "h", 2),),
    (("oX", 3, "h", 2), ("oX", 1, "l", 2)),
    (("oX", 3, "h", 3), ("oX", 1, "l", 3)),
    (("oT", 1, "h", 2), ("oo", 3, "h", 0)),
    (("oX", 2, "l", 2), ("oo", 3, "h", 1), ("oX", 2, "l", 3), ("oT", 2, "h", 2), ("oo", 3, "h", 2), ("oX", 3, "l", 2), ("oX", 3, "l", 3), ("oT", 3, "h", 2)),
    (),
)
INNER = (
    (("io", 0, "l", 1), ("iy", 0, "h", 2), ("io", 0, "h", 2), ("io", 1, "l", 1)),
    (("io", 0, "h", 1), ("io", 0, "l", 0), ("io", 1, "l", 0), ("iy", 1, "h", 2), ("io", 0, "h", 0), ("iX", 0, "l", 3), ("io", 1, "h", 0), ("iX", 1, "l", 3), ("iX", 0, "h", 3), ("iX", 0, "l", 2), ("iX", 1, "h", 3), ("iX", 2, "l", 3)),
    (("iX", 0, "h", 2), ("io", 2, "l", 0), ("io", 1, "h", 1), ("iX", 1, "l", 2), ("io", 1, "h", 2), ("io", 2, "l", 1)),
    (("iX", 1, "h", 2), ("iX", 3, "l", 3), ("iy", 2, "h", 2), ("io", 3, "l", 0), ("oX", 0, "h", 2), ("iX", 2, "h", 3), ("oX", 0, "h", 3), ("io", 2, "h", 0), ("io", 2, "h", 1), ("io", 3, "l", 1), ("oo", 0, "h", 0), ("io", 2, "h", 2), ("oo", 0, "h", 1), ("iy", 3, "h", 2), ("oX", 1, "h", 2), ("iX", 3, "h", 3), ("oX", 0, "l", 2), ("iX", 2, "l", 2), ("oX", 0, "l", 3), ("oX", 1, "h", 3)),
    (("oo", 1, "h", 0), ("iX", 2, "h", 2), ("oo", 1, "h", 1), ("io", 3, "h", 0)),
    (("io", 3, "h", 1), ("iX", 3, "l", 2)),
    (("io", 3, "h", 2),),
    (),
    (("iX", 3, "h", 2), ("oX", 2, "h", 2), ("oo", 0, "l", 0), ("oX", 2, "h", 3)),
    (("oX", 1, "l", 2),),
    (("oo", 2, "h", 0), ("oX", 1, "l", 3)),
    (("oo", 2, "h", 1), ("oo", 1, "l", 0), ("oX", 2, "l", 2), ("oX", 3, "h", 2), ("oX", 2, "l", 3), ("oX", 3, "h", 3), ("oo", 2, "l", 0)),
    (("oX", 3, "l", 2), ("oo", 3, "h", 0), ("oX", 3, "l", 3), ("oo", 3, "h", 1), ("oo", 3, "l", 0)),
    (),
)

class Chains:
    def __init__(self, edge, at, refs):
        self.lam = {"h": 3, "l": 0} if edge else {"h": 2, "l": 1}
        self.at = at
        self.refs = refs
        self.sent = 0
        self.seen = set()

    def zpos(self, d, j, own):
        up, zhi = self.at["up"], self.at["zhi"]
        towards = up if d == "h" else 1 - up
        return (zhi if own else 1 - zhi) * 4 + jnp.where(towards == 1, j, 3 - j)

    def last_slot(self, d):
        towards = self.at["up"] if d == "h" else 1 - self.at["up"]
        return jnp.where(towards == 1, self.at["z"], RING)

    def block(self, name, q, slot=None):
        t, e = q // 2, q % 2
        rows = pl.ds(e * HALF, HALF)
        ref = self.refs[name]
        return ref.at[t, rows] if slot is None else ref.at[t, slot, rows]

    def copy(self, src, dst, recv, device):
        remote(src, dst, self.refs["z_send"].at[self.sent], recv, device).start()
        self.sent += 1

    def drain(self):
        for n in range(self.sent):
            one = self.block("tout", 0)
            remote(one, one, self.refs["z_send"].at[n], self.refs["t_recv"].at[0], self.at["h"]).wait_send()

    def arrive(self, dst, recv):
        remote(dst, dst, self.refs["z_send"].at[0], recv, self.at["h"]).wait_recv()

    def arrive_rows(self, q, d, j, own):
        if (q, d, j, own) in self.seen:
            return
        self.seen.add((q, d, j, own))
        zs = self.zpos(d, j, own)
        self.arrive(self.block("rows", q, zs), self.refs["in_recv"].at[q, zs])

    def all_rows(self, q):
        for d in ("h", "l"):
            for j in range(self.lam[d] - 1, -1, -1):
                self.arrive_rows(q, d, j, True)
            for j in (3, 2):
                self.arrive_rows(q, d, j, False)

    def add(self, q, zs, slot):
        self.arrive(self.block("rr", q, slot), self.refs["out_recv"].at[q, slot])
        part, rr = self.block("part", q, zs), self.block("rr", q, slot)
        part[...] = (part[...].astype(F32) + rr[...].astype(F32)).astype(BF)

    def finish(self, q):
        for d in ("h", "l"):
            if self.lam[d] < 3:
                self.add(q, self.at["z"], self.last_slot(d))
        self.arrive(self.block("ofin", q), self.refs["ot_recv"].at[q, 1])

    def emit(self, code, q, d, j):
        lam = self.lam[d]
        other = "l" if d == "h" else "h"
        in_recv, out_recv = self.refs["in_recv"], self.refs["out_recv"]
        if code in ("io", "iX"):
            own = code == "io"
            zs = self.zpos(d, j, own)
            if not own or j < lam:
                self.arrive_rows(q, d, j, own)
            rows = self.block("rows", q, zs)
            self.copy(rows, rows, in_recv.at[q, zs], self.at[d])
        elif code == "iO":
            z = self.at["z"]
            self.copy(self.block("tout", q), self.block("rows", q, z), in_recv.at[q, z], self.at[d])
        elif code == "iy":
            self.copy(self.block("tout", q), self.block("ttr", q), self.refs["t_recv"].at[q], self.at[d])
        elif code == "ix":
            ttr = self.block("ttr", q)
            self.arrive(ttr, self.refs["t_recv"].at[q])
            zs = self.zpos(d, 2, True)
            self.copy(ttr, self.block("rows", q, zs), in_recv.at[q, zs], self.at[d])
        elif code in ("oo", "oX"):
            own = code == "oo"
            zs = self.zpos(d, j, own)
            if lam < 3:
                self.add(q, zs, zs)
            part = self.block("part", q, zs)
            if lam > 0:
                slot = self.last_slot_of(d, zs) if own and j == lam - 1 else zs
                self.copy(part, self.block("rr", q, slot), out_recv.at[q, slot], self.at[other])
            elif j == 2:
                self.copy(part, self.block("otr", q), self.refs["ot_recv"].at[q, 0], self.at[other])
            else:
                self.copy(part, self.block("ofin", q), self.refs["ot_recv"].at[q, 1], self.at[other])
        else:
            otr = self.block("otr", q)
            self.arrive(otr, self.refs["ot_recv"].at[q, 0])
            self.copy(otr, self.block("ofin", q), self.refs["ot_recv"].at[q, 1], self.at[other])

    def last_slot_of(self, d, zs):
        towards = self.at["up"] if d == "h" else 1 - self.at["up"]
        return jnp.where(towards == 1, zs, RING)


def exchange_kernel(
    sa, sb, win, wout,
    out_a, out_b, gin, gout,
    prcv, fs, rows, tout, ttr, part, rr, ofin, otr, psend, prcv2,
    w_in, w_out, g_in, g_out, act, slope, dpre, acc,
    w_sem, g_sem, ps_send, ps_recv, po_send, po_recv,
    z_send, in_recv, t_recv, out_recv, ot_recv,
):
    p, zhi, h = place()
    z = zhi * 4 + h
    up = jnp.where(h >= 2, 1, 0)
    step = 2 * up - 1
    at = {
        "z": z,
        "zhi": zhi,
        "up": up,
        "h": ring_device(p, (z + step + RING) % RING),
        "l": ring_device(p, (z - step + RING) % RING),
    }
    refs = {
        "rows": rows, "tout": tout, "ttr": ttr, "part": part, "rr": rr, "ofin": ofin, "otr": otr,
        "z_send": z_send, "in_recv": in_recv, "t_recv": t_recv, "out_recv": out_recv, "ot_recv": ot_recv,
    }
    edge, inner = Chains(True, at, refs), Chains(False, at, refs)
    at_edge = jnp.logical_or(h == 0, h == 3)

    def both(body):
        @pl.when(at_edge)
        def _():
            body(edge, EDGE)

        @pl.when(jnp.logical_not(at_edge))
        def _():
            body(inner, INNER)

    w_copies = [
        pltpu.make_async_copy(win, w_in, w_sem.at[0]),
        pltpu.make_async_copy(wout, w_out, w_sem.at[1]),
    ]
    for copy in w_copies:
        copy.start()
    greet(p, zhi, h, (1, RING - 1))
    sends = (sa, sb)
    for t in (0, 1):
        plane_start(p, zhi, h, sends[t], prcv.at[t], ps_send.at[t], ps_recv.at[t])

    def gather(t):
        plane_arrived(prcv.at[t], ps_recv.at[t])
        prcv[t, p] = sends[t][p]
        for c in range(LANES):
            lanes = slice(c * 128, (c + 1) * 128)
            fs[c] = prcv[t, :, :, lanes].astype(F32).reshape(COLS, 128)
            for s in range(4):
                piece = slice(s * PLANE, (s + 1) * PLANE)
                mine = fs[c, pl.ds(zhi * 4 + s, PLANE, stride=8), :]
                rows[t, z, piece, lanes] = mine.astype(BF)
                other = fs[c, pl.ds((1 - zhi) * 4 + s, PLANE, stride=8), :]
                tout[t, piece, lanes] = other.astype(BF)

    def out_last(t):
        def finish(chains, table):
            for e in (0, 1):
                chains.finish(2 * t + e)

        both(finish)
        for c in range(LANES):
            lanes = slice(c * 128, (c + 1) * 128)
            for s in range(4):
                piece = slice(s * PLANE, (s + 1) * PLANE)
                fs[c, pl.ds(zhi * 4 + s, PLANE, stride=8), :] = part[t, z, piece, lanes].astype(F32)
                fs[c, pl.ds((1 - zhi) * 4 + s, PLANE, stride=8), :] = ofin[t, piece, lanes].astype(F32)
            psend[t, :, :, lanes] = fs[c].reshape(PLANE, 8, 128).astype(BF)
        plane_start(p, zhi, h, psend.at[t], prcv2.at[t], po_send.at[t], po_recv.at[t])


    def expert_rows(t, e):
        return rows[t, :, e * HALF : (e + 1) * HALF, :].reshape(RING * HALF, D)

    def collect(t, e, f, more):
        if f == 0:
            acc[...] = more
        elif f == 1:
            acc[...] += more
        else:
            total = (acc[...] + more).astype(BF)
            part[t, :, e * HALF : (e + 1) * HALF, :] = total.reshape(RING, HALF, D)

    def forward_piece(e, f):
        span = slice(f * COLS, (f + 1) * COLS)
        pre = jnp.dot(expert_rows(0, e), w_in[e, :, span], preferred_element_type=F32)
        half = 0.5 * (1.0 + lax.erf(pre * 0.7071067811865476))
        value = (pre * half).astype(BF)
        act[e, :, span] = value
        slope[e, :, span] = half + pre * jnp.exp(-0.5 * pre * pre) * 0.3989422804014327
        more = jnp.dot(value, w_out[e, span, :], preferred_element_type=F32)
        collect(0, e, f, more)

    def backward_piece(e, f):
        span = slice(f * COLS, (f + 1) * COLS)
        d_act = lax.dot_general(
            expert_rows(1, e), w_out[e, span, :], (((1,), (1,)), ((), ())), preferred_element_type=F32
        )
        value = (d_act * slope[e, :, span]).astype(BF)
        dpre[e, :, span] = value
        more = lax.dot_general(
            value, w_in[e, :, span], (((1,), (1,)), ((), ())), preferred_element_type=F32
        )
        collect(1, e, f, more)

    def weight_piece(e, f):
        span = slice(f * COLS, (f + 1) * COLS)
        g_out[e, span, :] = lax.dot_general(
            act[e, :, span], expert_rows(1, e), (((0,), (0,)), ((), ())), preferred_element_type=F32
        ).astype(BF)
        g_in[e, :, span] = lax.dot_general(
            expert_rows(0, e), dpre[e, :, span], (((0,), (0,)), ((), ())), preferred_element_type=F32
        ).astype(BF)

    g_copies = [
        pltpu.make_async_copy(g_in, gin, g_sem.at[0]),
        pltpu.make_async_copy(g_out, gout, g_sem.at[1]),
    ]

    def segment(n):
        def body(chains, table):
            for item in table[n]:
                chains.emit(*item)

        both(body)

    gather(0)
    for n, event in enumerate(EVENTS):
        segment(n)
        kind, which = event[0], event[1:]
        if kind == "gather":
            gather(1)
        elif kind in ("fwd", "bwd"):
            (e,) = which
            q = e if kind == "fwd" else 2 + e
            both(lambda chains, table, q=q: chains.all_rows(q))
            if q == 0:
                for copy in w_copies:
                    copy.wait()
            for f in range(3):
                (forward_piece if kind == "fwd" else backward_piece)(e, f)
        elif kind == "wg":
            weight_piece(*which)
            if which == (1, 2):
                for copy in g_copies:
                    copy.start()
        else:
            out_last(which[0])
    segment(len(EVENTS))
    plane_arrived(prcv2.at[0], po_recv.at[0])
    prcv2[0, p] = psend[0, p]
    out_a[...] = prcv2[0]
    plane_arrived(prcv2.at[1], po_recv.at[1])
    prcv2[1, p] = psend[1, p]
    out_b[...] = prcv2[1]
    for t in (0, 1):
        plane_sent(prcv.at[t], ps_send.at[t])
        plane_sent(psend.at[t], po_send.at[t])

    both(lambda chains, table: chains.drain())
    for copy in g_copies:
        copy.wait()


def plane_start(p, zhi, h, src, dst, send, recv):
    def step(j, carry):
        q = lax.rem(p + j, PLANE)
        remote(src.at[q], dst.at[p], send, recv, plane_device(q, zhi, h)).start()
        return carry

    lax.fori_loop(1, PLANE, step, 0)


def plane_arrived(dst, recv):
    many = dst.at[pl.ds(0, PLANE - 1)]
    pltpu.make_async_copy(many, many, recv).wait()


def plane_sent(src, send):
    many = src.at[pl.ds(0, PLANE - 1)]
    pltpu.make_async_copy(many, many, send).wait()


def exchange(send_a, send_b, weight_in, weight_out):
    vmem = pl.BlockSpec(memory_space=pltpu.VMEM)
    anywhere = pl.BlockSpec(memory_space=pl.ANY)
    dma = pltpu.SemaphoreType.DMA
    experts = weight_in.shape[0]
    width = weight_in.shape[2]
    return pl.pallas_call(
        exchange_kernel,
        out_shape=(
            jax.ShapeDtypeStruct(send_a.shape, BF),
            jax.ShapeDtypeStruct(send_a.shape, BF),
            jax.ShapeDtypeStruct(weight_in.shape, BF),
            jax.ShapeDtypeStruct(weight_out.shape, BF),
        ),
        in_specs=[vmem, vmem, anywhere, anywhere],
        out_specs=(vmem, vmem, anywhere, anywhere),
        scratch_shapes=[
            pltpu.VMEM((2, PLANE, 8, D), BF),
            pltpu.VMEM((LANES, COLS, 128), F32),
            pltpu.VMEM((2, RING, ROWS, D), BF),
            pltpu.VMEM((2, ROWS, D), BF),
            pltpu.VMEM((2, ROWS, D), BF),
            pltpu.VMEM((2, RING, ROWS, D), BF),
            pltpu.VMEM((2, RING + 1, ROWS, D), BF),
            pltpu.VMEM((2, ROWS, D), BF),
            pltpu.VMEM((2, ROWS, D), BF),
            pltpu.VMEM((2, PLANE, 8, D), BF),
            pltpu.VMEM((2, PLANE, 8, D), BF),
            pltpu.VMEM(weight_in.shape, BF),
            pltpu.VMEM(weight_out.shape, BF),
            pltpu.VMEM(weight_in.shape, BF),
            pltpu.VMEM(weight_out.shape, BF),
            pltpu.VMEM((experts, RING * 64, width), BF),
            pltpu.VMEM((experts, RING * 64, width), F32),
            pltpu.VMEM((experts, RING * 64, width), BF),
            pltpu.VMEM((RING * 64, D), F32),
            dma((2,)),
            dma((2,)),
            dma((2,)),
            dma((2,)),
            dma((2,)),
            dma((2,)),
            dma((COPIES,)),
            dma((4, RING)),
            dma((4,)),
            dma((4, RING + 1)),
            dma((4, 2)),
        ],
        compiler_params=pltpu.CompilerParams(
            collective_id=0, has_side_effects=True, vmem_limit_bytes=56 * 1024 * 1024
        ),
        name="exchange",
    )(send_a, send_b, weight_in, weight_out)


def window(h):
    return pl.multiple_of((h + h // 2) * 128, 128)


def router_kernel(rp, out, prcv, zs, zr, ps_send, ps_recv, z_send, z_recv):
    p, zhi, h = place()
    z = zhi * 4 + h
    greet(p, zhi, h, tuple(range(1, RING)))

    plane_start(p, zhi, h, rp, prcv, ps_send, ps_recv)
    plane_arrived(prcv, ps_recv)
    prcv[p] = rp[p]
    zs[...] = jnp.sum(prcv[...].astype(F32), axis=0)
    zr[z] = zs[:, pl.ds(window(h), COLS)]

    def ring_copy(j, slot):
        to = lax.rem(z + j, RING)
        slot = z if slot is None else to
        return remote(
            zs.at[:, pl.ds(window(lax.rem(to, 4)), COLS)],
            zr.at[slot],
            z_send.at[to],
            z_recv.at[slot],
            ring_device(p, to),
        )

    for j in range(1, RING):
        ring_copy(j, None).start()
    for j in range(1, RING):
        ring_copy(j, 1).wait_recv()
    out[...] = jnp.sum(zr[...], axis=0)
    plane_sent(rp, ps_send)
    for j in range(1, RING):
        ring_copy(j, None).wait_send()


def router_reduce(partial):
    vmem = pl.BlockSpec(memory_space=pltpu.VMEM)
    dma = pltpu.SemaphoreType.DMA
    return pl.pallas_call(
        router_kernel,
        out_shape=jax.ShapeDtypeStruct((8, COLS), F32),
        in_specs=[vmem],
        out_specs=vmem,
        scratch_shapes=[
            pltpu.VMEM((PLANE, 8, D), BF),
            pltpu.VMEM((8, D), F32),
            pltpu.VMEM((RING, 8, COLS), F32),
            dma(()),
            dma(()),
            dma((RING,)),
            dma((RING,)),
        ],
        compiler_params=pltpu.CompilerParams(collective_id=1, has_side_effects=True),
        name="router",
    )(partial)


def per_device(tokens, out_grad, slot_router, weight_in, weight_out):
    router = slot_router.reshape(D, 4, 2, 8, 4).transpose(0, 1, 3, 2, 4).reshape(D, COLS)
    logits = jnp.dot(tokens, router, preferred_element_type=F32)
    dispatch = jax.nn.softmax(logits, axis=0)
    combine = jax.nn.softmax(logits, axis=1)
    dispatch16 = dispatch.astype(BF)
    combine16 = combine.astype(BF)
    slot_in = jnp.einsum("tc,td->cd", dispatch16, tokens, preferred_element_type=F32).astype(BF)
    slot_grad = jnp.einsum("tc,td->cd", combine16, out_grad, preferred_element_type=F32).astype(BF)
    slot_out, slot_in_grad, grad_first, grad_second = exchange(
        slot_in.reshape(PLANE, 8, D), slot_grad.reshape(PLANE, 8, D), weight_in, weight_out
    )
    slot_out = slot_out.reshape(COLS, D)
    slot_in_grad = slot_in_grad.reshape(COLS, D)
    d_combine = jnp.einsum("td,cd->tc", out_grad, slot_out, preferred_element_type=F32)
    d_dispatch = jnp.einsum("td,cd->tc", tokens, slot_in_grad, preferred_element_type=F32)
    from_combine = combine * (d_combine - jnp.sum(combine * d_combine, axis=1, keepdims=True))
    from_dispatch = dispatch * (d_dispatch - jnp.sum(dispatch * d_dispatch, axis=0, keepdims=True))
    d_logits = (from_combine + from_dispatch).astype(BF)
    router_term = jnp.einsum("tc,td->cd", d_logits, tokens, preferred_element_type=F32).astype(BF)
    router_sum = router_reduce(router_term.reshape(PLANE, 8, D))
    token_grad = (
        jnp.dot(dispatch16, slot_in_grad, preferred_element_type=F32)
        + jnp.einsum("tc,dc->td", d_logits, router, preferred_element_type=F32)
    ).astype(BF)
    _, zhi, h = place()
    router_grad = lax.dynamic_slice(router_sum, (zhi * 4, (h % 2) * 64), (4, 192)).T
    return (token_grad, router_grad, grad_first, grad_second)


def solution(mesh):
    return jax.shard_map(
        per_device,
        mesh=mesh,
        in_specs=(
            P(("expert", "hidden"), None),
            P(("expert", "hidden"), None),
            P(),
            P("expert", None, "hidden"),
            P("expert", "hidden", None),
        ),
        out_specs=(
            P(("expert", "hidden"), None),
            P("hidden", "expert"),
            P("expert", None, "hidden"),
            P("expert", "hidden", None),
        ),
        check_vma=False,
    )
```

```python
import jax
import jax.numpy as jnp
from jax import lax
from jax.experimental import pallas as pl
from jax.experimental.pallas import tpu as pltpu
from jax.sharding import PartitionSpec as P

D = 768
TOK = 196
PLANE = 32
RING = 8
ROWS = 128
COLS = 256
HALF = 64
COPIES = 80
LANES = 6
MESH = pl.DeviceIdType.MESH
BF = jnp.bfloat16
F32 = jnp.float32


def place():
    expert = lax.axis_index("expert")
    h = lax.axis_index("hidden")
    p = lax.div(expert, 16) * 8 + lax.rem(expert, 8)
    zhi = lax.rem(lax.div(expert, 8), 2)
    return p, zhi, h


def plane_device(q, zhi, h):
    return (lax.div(q, 8) * 16 + zhi * 8 + lax.rem(q, 8), h)


def ring_device(p, z):
    return (lax.div(p, 8) * 16 + lax.div(z, 4) * 8 + lax.rem(p, 8), lax.rem(z, 4))


def met():
    pl.semaphore_wait(pltpu.get_barrier_semaphore(), PLANE + RING - 2)


def remote(src, dst, send, recv, device):
    return pltpu.make_async_remote_copy(
        src_ref=src, dst_ref=dst, send_sem=send, recv_sem=recv, device_id=device, device_id_type=MESH
    )


def greet(p, zhi, h, ring_offsets):
    barrier = pltpu.get_barrier_semaphore()
    z = zhi * 4 + h

    def one(j, carry):
        pl.semaphore_signal(
            barrier, inc=1, device_id=plane_device(lax.rem(p + j, PLANE), zhi, h), device_id_type=MESH
        )
        return carry

    lax.fori_loop(1, PLANE, one, 0)
    for offset in ring_offsets:
        pl.semaphore_signal(
            barrier, inc=1, device_id=ring_device(p, lax.rem(z + offset, RING)), device_id_type=MESH
        )


EVENTS = (
    ("gather",),
    ("fwd", 0),
    ("fwd", 1),
    ("bwd", 0),
    ("wg", 0, 0),
    ("wg", 0, 1),
    ("wg", 0, 2),
    ("bwd", 1),
    ("wg", 1, 0),
    ("wg", 1, 1),
    ("wg", 1, 2),
    ("last", 0),
    ("last", 1),
)
EDGE = (
    (("io", 0, "l", 0), ("iO", 0, "h", 3), ("io", 1, "l", 0), ("iO", 1, "h", 3)),
    (("iX", 0, "l", 3), ("ix", 0, "h", 2), ("iX", 1, "l", 3), ("iO", 2, "h", 3), ("iX", 0, "l", 2), ("iO", 3, "h", 3), ("ix", 1, "h", 2), ("iX", 2, "l", 3), ("io", 2, "l", 0), ("iX", 1, "l", 2), ("iX", 3, "l", 3), ("io", 3, "l", 0)),
    (("oX", 0, "h", 2), ("oX", 0, "h", 3), ("oo", 0, "h", 0)),
    (("oo", 0, "h", 1), ("ix", 2, "h", 2), ("oo", 0, "h", 2), ("oX", 1, "h", 2), ("iX", 2, "l", 2), ("oX", 1, "h", 3), ("oo", 1, "h", 0), ("ix", 3, "h", 2), ("oo", 1, "h", 1), ("oo", 1, "h", 2), ("oX", 0, "l", 2), ("iX", 3, "l", 2), ("oX", 0, "l", 3), ("oT", 0, "h", 2)),
    (("oX", 2, "h", 2),),
    (("oX", 2, "h", 3),),
    (("oo", 2, "h", 0),),
    (("oo", 2, "h", 1),),
    (("oo", 2, "h", 2),),
    (("oX", 3, "h", 2), ("oX", 1, "l", 2)),
    (("oX", 3, "h", 3), ("oX", 1, "l", 3)),
    (("oT", 1, "h", 2), ("oo", 3, "h", 0)),
    (("oX", 2, "l", 2), ("oo", 3, "h", 1), ("oX", 2, "l", 3), ("oT", 2, "h", 2), ("oo", 3, "h", 2), ("oX", 3, "l", 2), ("oX", 3, "l", 3), ("oT", 3, "h", 2)),
    (),
)
INNER = (
    (("io", 0, "l", 1), ("iy", 0, "h", 2), ("io", 0, "h", 2), ("io", 1, "l", 1)),
    (("io", 0, "h", 1), ("io", 0, "l", 0), ("io", 1, "l", 0), ("iy", 1, "h", 2), ("io", 0, "h", 0), ("iX", 0, "l", 3), ("io", 1, "h", 0), ("iX", 1, "l", 3), ("iX", 0, "h", 3), ("iX", 0, "l", 2), ("iX", 1, "h", 3), ("iX", 2, "l", 3)),
    (("iX", 0, "h", 2), ("io", 2, "l", 0), ("io", 1, "h", 1), ("iX", 1, "l", 2), ("io", 1, "h", 2), ("io", 2, "l", 1)),
    (("iX", 1, "h", 2), ("iX", 3, "l", 3), ("iy", 2, "h", 2), ("io", 3, "l", 0), ("oX", 0, "h", 2), ("iX", 2, "h", 3), ("oX", 0, "h", 3), ("io", 2, "h", 0), ("io", 2, "h", 1), ("io", 3, "l", 1), ("oo", 0, "h", 0), ("io", 2, "h", 2), ("oo", 0, "h", 1), ("iy", 3, "h", 2), ("oX", 1, "h", 2), ("iX", 3, "h", 3), ("oX", 0, "l", 2), ("iX", 2, "l", 2), ("oX", 0, "l", 3), ("oX", 1, "h", 3)),
    (("oo", 1, "h", 0), ("iX", 2, "h", 2), ("oo", 1, "h", 1), ("io", 3, "h", 0)),
    (("io", 3, "h", 1), ("iX", 3, "l", 2)),
    (("io", 3, "h", 2),),
    (),
    (("iX", 3, "h", 2), ("oX", 2, "h", 2), ("oo", 0, "l", 0), ("oX", 2, "h", 3)),
    (("oX", 1, "l", 2),),
    (("oo", 2, "h", 0), ("oX", 1, "l", 3)),
    (("oo", 2, "h", 1), ("oo", 1, "l", 0), ("oX", 2, "l", 2), ("oX", 3, "h", 2), ("oX", 2, "l", 3), ("oX", 3, "h", 3), ("oo", 2, "l", 0)),
    (("oX", 3, "l", 2), ("oo", 3, "h", 0), ("oX", 3, "l", 3), ("oo", 3, "h", 1), ("oo", 3, "l", 0)),
    (),
)

class Chains:
    def __init__(self, edge, at, refs):
        self.lam = {"h": 3, "l": 0} if edge else {"h": 2, "l": 1}
        self.at = at
        self.refs = refs
        self.sent = 0
        self.seen = set()

    def zpos(self, d, j, own):
        up, zhi = self.at["up"], self.at["zhi"]
        towards = up if d == "h" else 1 - up
        return (zhi if own else 1 - zhi) * 4 + jnp.where(towards == 1, j, 3 - j)

    def last_slot(self, d):
        towards = self.at["up"] if d == "h" else 1 - self.at["up"]
        return jnp.where(towards == 1, self.at["z"], RING)

    def block(self, name, q, slot=None):
        t, e = q // 2, q % 2
        rows = pl.ds(e * HALF, HALF)
        ref = self.refs[name]
        return ref.at[t, rows] if slot is None else ref.at[t, slot, rows]

    def copy(self, src, dst, recv, device):
        remote(src, dst, self.refs["z_send"].at[self.sent], recv, device).start()
        self.sent += 1

    def drain(self):
        for n in range(self.sent):
            one = self.block("tout", 0)
            remote(one, one, self.refs["z_send"].at[n], self.refs["t_recv"].at[0], self.at["h"]).wait_send()

    def arrive(self, dst, recv):
        remote(dst, dst, self.refs["z_send"].at[0], recv, self.at["h"]).wait_recv()

    def arrive_rows(self, q, d, j, own):
        if (q, d, j, own) in self.seen:
            return
        self.seen.add((q, d, j, own))
        zs = self.zpos(d, j, own)
        self.arrive(self.block("rows", q, zs), self.refs["in_recv"].at[q, zs])

    def all_rows(self, q):
        for d in ("h", "l"):
            for j in range(self.lam[d] - 1, -1, -1):
                self.arrive_rows(q, d, j, True)
            for j in (3, 2):
                self.arrive_rows(q, d, j, False)

    def add(self, q, zs, slot):
        self.arrive(self.block("rr", q, slot), self.refs["out_recv"].at[q, slot])
        part, rr = self.block("part", q, zs), self.block("rr", q, slot)
        part[...] = (part[...].astype(F32) + rr[...].astype(F32)).astype(BF)

    def finish(self, q):
        for d in ("h", "l"):
            if self.lam[d] < 3:
                self.add(q, self.at["z"], self.last_slot(d))
        self.arrive(self.block("ofin", q), self.refs["ot_recv"].at[q, 1])

    def emit(self, code, q, d, j):
        lam = self.lam[d]
        other = "l" if d == "h" else "h"
        in_recv, out_recv = self.refs["in_recv"], self.refs["out_recv"]
        if code in ("io", "iX"):
            own = code == "io"
            zs = self.zpos(d, j, own)
            if not own or j < lam:
                self.arrive_rows(q, d, j, own)
            rows = self.block("rows", q, zs)
            self.copy(rows, rows, in_recv.at[q, zs], self.at[d])
        elif code == "iO":
            z = self.at["z"]
            self.copy(self.block("tout", q), self.block("rows", q, z), in_recv.at[q, z], self.at[d])
        elif code == "iy":
            self.copy(self.block("tout", q), self.block("ttr", q), self.refs["t_recv"].at[q], self.at[d])
        elif code == "ix":
            ttr = self.block("ttr", q)
            self.arrive(ttr, self.refs["t_recv"].at[q])
            zs = self.zpos(d, 2, True)
            self.copy(ttr, self.block("rows", q, zs), in_recv.at[q, zs], self.at[d])
        elif code in ("oo", "oX"):
            own = code == "oo"
            zs = self.zpos(d, j, own)
            if lam < 3:
                self.add(q, zs, zs)
            part = self.block("part", q, zs)
            if lam > 0:
                slot = self.last_slot_of(d, zs) if own and j == lam - 1 else zs
                self.copy(part, self.block("rr", q, slot), out_recv.at[q, slot], self.at[other])
            elif j == 2:
                self.copy(part, self.block("otr", q), self.refs["ot_recv"].at[q, 0], self.at[other])
            else:
                self.copy(part, self.block("ofin", q), self.refs["ot_recv"].at[q, 1], self.at[other])
        else:
            otr = self.block("otr", q)
            self.arrive(otr, self.refs["ot_recv"].at[q, 0])
            self.copy(otr, self.block("ofin", q), self.refs["ot_recv"].at[q, 1], self.at[other])

    def last_slot_of(self, d, zs):
        towards = self.at["up"] if d == "h" else 1 - self.at["up"]
        return jnp.where(towards == 1, zs, RING)


def exchange_kernel(
    tokens, out_grad, router, win, wout,
    token_grad, router_out, gin, gout,
    rt, disp, comb, d_log, sa, sb, rs, rrcv, zs, zr,
    prcv, fs, rows, tout, ttr, part, rr, ofin, otr, psend, prcv2,
    w_in, w_out, g_in, g_out, act, slope, dpre, acc,
    w_sem, g_sem, ps_send, ps_recv, po_send, po_recv,
    z_send, in_recv, t_recv, out_recv, ot_recv,
    pr_send, pr_recv, rz_send, rz_recv,
):
    p, zhi, h = place()
    z = zhi * 4 + h
    up = jnp.where(h >= 2, 1, 0)
    step = 2 * up - 1
    at = {
        "z": z,
        "zhi": zhi,
        "up": up,
        "h": ring_device(p, lax.rem(z + step + RING, RING)),
        "l": ring_device(p, lax.rem(z - step + RING, RING)),
    }
    refs = {
        "rows": rows, "tout": tout, "ttr": ttr, "part": part, "rr": rr, "ofin": ofin, "otr": otr,
        "z_send": z_send, "in_recv": in_recv, "t_recv": t_recv, "out_recv": out_recv, "ot_recv": ot_recv,
    }
    edge, inner = Chains(True, at, refs), Chains(False, at, refs)
    at_edge = jnp.logical_or(h == 0, h == 3)

    def both(body):
        @pl.when(at_edge)
        def _():
            body(edge, EDGE)

        @pl.when(jnp.logical_not(at_edge))
        def _():
            body(inner, INNER)

    w_copies = [
        pltpu.make_async_copy(win, w_in, w_sem.at[0]),
        pltpu.make_async_copy(wout, w_out, w_sem.at[1]),
    ]
    for copy in w_copies:
        copy.start()
    greet(p, zhi, h, tuple(range(1, RING)))

    natural = lax.broadcasted_iota(jnp.int32, (COLS, COLS), 0)
    placed = lax.broadcasted_iota(jnp.int32, (COLS, COLS), 1)
    source = (placed & 192) + ((placed & 4) << 3) + ((placed & 56) >> 1) + (placed & 3)
    pick = jnp.where(natural == source, 1.0, 0.0).astype(BF)
    rt[...] = jnp.dot(router[...], pick, preferred_element_type=F32).astype(BF)
    logits = jnp.dot(tokens[...], rt[...], preferred_element_type=F32)
    above = jnp.exp(logits - jnp.max(logits, axis=0, keepdims=True))
    disp[...] = above / jnp.sum(above, axis=0, keepdims=True)
    sa[...] = rounded_slots(disp[...].astype(BF), tokens[...])
    met()
    sends = (sa, sb)
    plane_start(p, zhi, h, sa, prcv.at[0], ps_send.at[0], ps_recv.at[0])
    above = jnp.exp(logits - jnp.max(logits, axis=1, keepdims=True))
    comb[...] = above / jnp.sum(above, axis=1, keepdims=True)
    sb[...] = rounded_slots(comb[...].astype(BF), out_grad[...])
    plane_start(p, zhi, h, sb, prcv.at[1], ps_send.at[1], ps_recv.at[1])

    def gather(t):
        plane_arrived(prcv.at[t], ps_recv.at[t])
        prcv[t, p] = sends[t][p]
        for c in range(LANES):
            lanes = slice(c * 128, (c + 1) * 128)
            fs[c] = prcv[t, :, :, lanes].astype(F32).reshape(COLS, 128)
            for s in range(4):
                piece = slice(s * PLANE, (s + 1) * PLANE)
                mine = fs[c, pl.ds(zhi * 4 + s, PLANE, stride=8), :]
                rows[t, z, piece, lanes] = mine.astype(BF)
                other = fs[c, pl.ds((1 - zhi) * 4 + s, PLANE, stride=8), :]
                tout[t, piece, lanes] = other.astype(BF)

    def out_last(t):
        def finish(chains, table):
            for e in (0, 1):
                chains.finish(2 * t + e)

        both(finish)
        for c in range(LANES):
            lanes = slice(c * 128, (c + 1) * 128)
            for s in range(4):
                piece = slice(s * PLANE, (s + 1) * PLANE)
                fs[c, pl.ds(zhi * 4 + s, PLANE, stride=8), :] = part[t, z, piece, lanes].astype(F32)
                fs[c, pl.ds((1 - zhi) * 4 + s, PLANE, stride=8), :] = ofin[t, piece, lanes].astype(F32)
            psend[t, :, :, lanes] = fs[c].reshape(PLANE, 8, 128).astype(BF)
        plane_start(p, zhi, h, psend.at[t], prcv2.at[t], po_send.at[t], po_recv.at[t])


    def expert_rows(t, e):
        return rows[t, :, e * HALF : (e + 1) * HALF, :].reshape(RING * HALF, D)

    def collect(t, e, f, more):
        if f == 0:
            acc[...] = more
        elif f == 1:
            acc[...] += more
        else:
            total = (acc[...] + more).astype(BF)
            part[t, :, e * HALF : (e + 1) * HALF, :] = total.reshape(RING, HALF, D)

    def forward_piece(e, f):
        span = slice(f * COLS, (f + 1) * COLS)
        pre = jnp.dot(expert_rows(0, e), w_in[e, :, span], preferred_element_type=F32)
        half = 0.5 * (1.0 + lax.erf(pre * 0.7071067811865476))
        value = (pre * half).astype(BF)
        act[e, :, span] = value
        slope[e, :, span] = half + pre * jnp.exp(-0.5 * pre * pre) * 0.3989422804014327
        more = jnp.dot(value, w_out[e, span, :], preferred_element_type=F32)
        collect(0, e, f, more)

    def backward_piece(e, f):
        span = slice(f * COLS, (f + 1) * COLS)
        d_act = lax.dot_general(
            expert_rows(1, e), w_out[e, span, :], (((1,), (1,)), ((), ())), preferred_element_type=F32
        )
        value = (d_act * slope[e, :, span]).astype(BF)
        dpre[e, :, span] = value
        more = lax.dot_general(
            value, w_in[e, :, span], (((1,), (1,)), ((), ())), preferred_element_type=F32
        )
        collect(1, e, f, more)

    def weight_piece(e, f):
        span = slice(f * COLS, (f + 1) * COLS)
        g_out[e, span, :] = lax.dot_general(
            act[e, :, span], expert_rows(1, e), (((0,), (0,)), ((), ())), preferred_element_type=F32
        ).astype(BF)
        g_in[e, :, span] = lax.dot_general(
            expert_rows(0, e), dpre[e, :, span], (((0,), (0,)), ((), ())), preferred_element_type=F32
        ).astype(BF)

    g_copies = [
        pltpu.make_async_copy(g_in, gin, g_sem.at[0]),
        pltpu.make_async_copy(g_out, gout, g_sem.at[1]),
    ]

    def segment(n):
        def body(chains, table):
            for item in table[n]:
                chains.emit(*item)

        both(body)

    gather(0)
    for n, event in enumerate(EVENTS):
        segment(n)
        kind, which = event[0], event[1:]
        if kind == "gather":
            gather(1)
        elif kind in ("fwd", "bwd"):
            (e,) = which
            q = e if kind == "fwd" else 2 + e
            both(lambda chains, table, q=q: chains.all_rows(q))
            if q == 0:
                for copy in w_copies:
                    copy.wait()
            for f in range(3):
                (forward_piece if kind == "fwd" else backward_piece)(e, f)
        elif kind == "wg":
            weight_piece(*which)
            if which == (1, 2):
                for copy in g_copies:
                    copy.start()
        else:
            out_last(which[0])
    segment(len(EVENTS))
    plane_arrived(prcv2.at[0], po_recv.at[0])
    prcv2[0, p] = psend[0, p]
    slot_out = prcv2[0].astype(F32).reshape(COLS, D).astype(BF)
    d_combine = across(out_grad[...], slot_out)
    mixed = comb[...] * d_combine
    d_log[...] = mixed - comb[...] * jnp.sum(mixed, axis=1, keepdims=True)
    plane_arrived(prcv2.at[1], po_recv.at[1])
    prcv2[1, p] = psend[1, p]
    slot_in_grad = prcv2[1].astype(F32).reshape(COLS, D).astype(BF)
    d_dispatch = across(tokens[...], slot_in_grad)
    mixed = disp[...] * d_dispatch
    d_logits = (d_log[...] + (mixed - disp[...] * jnp.sum(mixed, axis=0, keepdims=True))).astype(BF)
    rs[...] = rounded_slots(d_logits, tokens[...])
    plane_start(p, zhi, h, rs, rrcv, pr_send, pr_recv)
    token_grad[...] = (
        jnp.dot(disp[...].astype(BF), slot_in_grad, preferred_element_type=F32) + across(d_logits, rt[...])
    ).astype(BF)
    plane_arrived(rrcv, pr_recv)
    rrcv[p] = rs[p]
    zs[...] = jnp.sum(rrcv[...].astype(F32), axis=0)
    zr[z] = zs[:, pl.ds(window(h), COLS)]

    def ring_copy(j, arrival):
        to = lax.rem(z + j, RING)
        slot = to if arrival else z
        return remote(
            zs.at[:, pl.ds(window(lax.rem(to, 4)), COLS)],
            zr.at[slot],
            rz_send.at[to],
            rz_recv.at[slot],
            ring_device(p, to),
        )

    for j in range(1, RING):
        ring_copy(j, False).start()
    for j in range(1, RING):
        ring_copy(j, True).wait_recv()
    total = jnp.sum(zr[...], axis=0)
    total = jnp.where(zhi == 0, total[:4], total[4:])
    router_out[...] = jnp.where(lax.rem(h, 2) == 0, total[:, :192], total[:, 64:])

    for t in (0, 1):
        plane_sent(prcv.at[t], ps_send.at[t])
        plane_sent(psend.at[t], po_send.at[t])
    plane_sent(rrcv, pr_send)
    for j in range(1, RING):
        ring_copy(j, False).wait_send()

    both(lambda chains, table: chains.drain())
    for copy in g_copies:
        copy.wait()


def rounded_slots(weights, values):
    sums = lax.dot_general(weights, values, (((0,), (0,)), ((), ())), preferred_element_type=F32)
    return sums.reshape(PLANE, 8, D).astype(BF)


def across(left, right):
    return lax.dot_general(left, right, (((1,), (1,)), ((), ())), preferred_element_type=F32)


def window(h):
    return pl.multiple_of((h + lax.div(h, 2)) * 128, 128)


def plane_start(p, zhi, h, src, dst, send, recv):
    def step(j, carry):
        q = lax.rem(p + j, PLANE)
        remote(src.at[q], dst.at[p], send, recv, plane_device(q, zhi, h)).start()
        return carry

    lax.fori_loop(1, PLANE, step, 0)


def plane_arrived(dst, recv):
    many = dst.at[pl.ds(0, PLANE - 1)]
    pltpu.make_async_copy(many, many, recv).wait()


def plane_sent(src, send):
    many = src.at[pl.ds(0, PLANE - 1)]
    pltpu.make_async_copy(many, many, send).wait()


def layer(tokens, out_grad, slot_router, weight_in, weight_out):
    vmem = pl.BlockSpec(memory_space=pltpu.VMEM)
    anywhere = pl.BlockSpec(memory_space=pl.ANY)
    dma = pltpu.SemaphoreType.DMA
    experts = weight_in.shape[0]
    width = weight_in.shape[2]
    return pl.pallas_call(
        exchange_kernel,
        out_shape=(
            jax.ShapeDtypeStruct(tokens.shape, BF),
            jax.ShapeDtypeStruct((4, 192), F32),
            jax.ShapeDtypeStruct(weight_in.shape, BF),
            jax.ShapeDtypeStruct(weight_out.shape, BF),
        ),
        in_specs=[vmem, vmem, vmem, anywhere, anywhere],
        out_specs=(vmem, vmem, anywhere, anywhere),
        scratch_shapes=[
            pltpu.VMEM(slot_router.shape, BF),
            pltpu.VMEM((TOK, COLS), F32),
            pltpu.VMEM((TOK, COLS), F32),
            pltpu.VMEM((TOK, COLS), F32),
            pltpu.VMEM((PLANE, 8, D), BF),
            pltpu.VMEM((PLANE, 8, D), BF),
            pltpu.VMEM((PLANE, 8, D), BF),
            pltpu.VMEM((PLANE, 8, D), BF),
            pltpu.VMEM((8, D), F32),
            pltpu.VMEM((RING, 8, COLS), F32),
            pltpu.VMEM((2, PLANE, 8, D), BF),
            pltpu.VMEM((LANES, COLS, 128), F32),
            pltpu.VMEM((2, RING, ROWS, D), BF),
            pltpu.VMEM((2, ROWS, D), BF),
            pltpu.VMEM((2, ROWS, D), BF),
            pltpu.VMEM((2, RING, ROWS, D), BF),
            pltpu.VMEM((2, RING + 1, ROWS, D), BF),
            pltpu.VMEM((2, ROWS, D), BF),
            pltpu.VMEM((2, ROWS, D), BF),
            pltpu.VMEM((2, PLANE, 8, D), BF),
            pltpu.VMEM((2, PLANE, 8, D), BF),
            pltpu.VMEM(weight_in.shape, BF),
            pltpu.VMEM(weight_out.shape, BF),
            pltpu.VMEM(weight_in.shape, BF),
            pltpu.VMEM(weight_out.shape, BF),
            pltpu.VMEM((experts, RING * HALF, width), BF),
            pltpu.VMEM((experts, RING * HALF, width), F32),
            pltpu.VMEM((experts, RING * HALF, width), BF),
            pltpu.VMEM((RING * HALF, D), F32),
            dma((2,)),
            dma((2,)),
            dma((2,)),
            dma((2,)),
            dma((2,)),
            dma((2,)),
            dma((COPIES,)),
            dma((4, RING)),
            dma((4,)),
            dma((4, RING + 1)),
            dma((4, 2)),
            dma(()),
            dma(()),
            dma((RING,)),
            dma((RING,)),
        ],
        compiler_params=pltpu.CompilerParams(
            collective_id=0, has_side_effects=True, vmem_limit_bytes=58 * 1024 * 1024
        ),
        name="layer",
    )(tokens, out_grad, slot_router, weight_in, weight_out)


def per_device(tokens, out_grad, slot_router, weight_in, weight_out):
    token_grad, router_grad, grad_first, grad_second = layer(
        tokens, out_grad, slot_router, weight_in, weight_out
    )
    return (token_grad, router_grad.T, grad_first, grad_second)


def solution(mesh):
    return jax.shard_map(
        per_device,
        mesh=mesh,
        in_specs=(
            P(("expert", "hidden"), None),
            P(("expert", "hidden"), None),
            P(),
            P("expert", None, "hidden"),
            P("expert", "hidden", None),
        ),
        out_specs=(
            P(("expert", "hidden"), None),
            P("hidden", "expert"),
            P("expert", None, "hidden"),
            P("expert", "hidden", None),
        ),
        check_vma=False,
    )
```

```python
import jax
import jax.numpy as jnp
from jax import lax
from jax.experimental import pallas as pl
from jax.experimental.pallas import tpu as pltpu
from jax.sharding import PartitionSpec as P

D = 768
TOK = 196
PLANE = 32
RING = 8
ROWS = 128
COLS = 256
HALF = 64
COPIES = 80
LANES = 6
MESH = pl.DeviceIdType.MESH
BF = jnp.bfloat16
F32 = jnp.float32


def place():
    expert = lax.axis_index("expert")
    h = lax.axis_index("hidden")
    p = lax.div(expert, 16) * 8 + lax.rem(expert, 8)
    zhi = lax.rem(lax.div(expert, 8), 2)
    return p, zhi, h


def plane_device(q, zhi, h):
    return (lax.div(q, 8) * 16 + zhi * 8 + lax.rem(q, 8), h)


def ring_device(p, z):
    return (lax.div(p, 8) * 16 + lax.div(z, 4) * 8 + lax.rem(p, 8), lax.rem(z, 4))


def met():
    pl.semaphore_wait(pltpu.get_barrier_semaphore(), PLANE + RING - 2)


def remote(src, dst, send, recv, device):
    return pltpu.make_async_remote_copy(
        src_ref=src, dst_ref=dst, send_sem=send, recv_sem=recv, device_id=device, device_id_type=MESH
    )


def greet(p, zhi, h, ring_offsets):
    barrier = pltpu.get_barrier_semaphore()
    z = zhi * 4 + h

    def one(j, carry):
        pl.semaphore_signal(
            barrier, inc=1, device_id=plane_device(lax.rem(p + j, PLANE), zhi, h), device_id_type=MESH
        )
        return carry

    lax.fori_loop(1, PLANE, one, 0)
    for offset in ring_offsets:
        pl.semaphore_signal(
            barrier, inc=1, device_id=ring_device(p, lax.rem(z + offset, RING)), device_id_type=MESH
        )


EVENTS = (
    ("gather",),
    ("fwd", 0),
    ("fwd", 1),
    ("bwd", 0),
    ("wg", 0, 0),
    ("wg", 0, 1),
    ("wg", 0, 2),
    ("bwd", 1),
    ("wg", 1, 0),
    ("wg", 1, 1),
    ("wg", 1, 2),
    ("last", 0),
    ("last", 1),
)
EDGE = (
    (("io", 0, "l", 0), ("iO", 0, "h", 3), ("io", 1, "l", 0), ("iO", 1, "h", 3)),
    (("iX", 0, "l", 3), ("ix", 0, "h", 2), ("iX", 1, "l", 3), ("iO", 2, "h", 3), ("iX", 0, "l", 2), ("iO", 3, "h", 3), ("ix", 1, "h", 2), ("iX", 2, "l", 3), ("io", 2, "l", 0), ("iX", 1, "l", 2), ("iX", 3, "l", 3), ("io", 3, "l", 0)),
    (("oX", 0, "h", 2), ("oX", 0, "h", 3), ("oo", 0, "h", 0)),
    (("oo", 0, "h", 1), ("ix", 2, "h", 2), ("oo", 0, "h", 2), ("oX", 1, "h", 2), ("iX", 2, "l", 2), ("oX", 1, "h", 3), ("oo", 1, "h", 0), ("ix", 3, "h", 2), ("oo", 1, "h", 1), ("oo", 1, "h", 2), ("oX", 0, "l", 2), ("iX", 3, "l", 2), ("oX", 0, "l", 3), ("oT", 0, "h", 2)),
    (("oX", 2, "h", 2),),
    (("oX", 2, "h", 3),),
    (("oo", 2, "h", 0),),
    (("oo", 2, "h", 1),),
    (("oo", 2, "h", 2),),
    (("oX", 3, "h", 2), ("oX", 1, "l", 2)),
    (("oX", 3, "h", 3), ("oX", 1, "l", 3)),
    (("oT", 1, "h", 2), ("oo", 3, "h", 0)),
    (("oX", 2, "l", 2), ("oo", 3, "h", 1), ("oX", 2, "l", 3), ("oT", 2, "h", 2), ("oo", 3, "h", 2), ("oX", 3, "l", 2), ("oX", 3, "l", 3), ("oT", 3, "h", 2)),
    (),
)
INNER = (
    (("io", 0, "l", 1), ("iy", 0, "h", 2), ("io", 0, "h", 2), ("io", 1, "l", 1)),
    (("io", 0, "h", 1), ("io", 0, "l", 0), ("io", 1, "l", 0), ("iy", 1, "h", 2), ("io", 0, "h", 0), ("iX", 0, "l", 3), ("io", 1, "h", 0), ("iX", 1, "l", 3), ("iX", 0, "h", 3), ("iX", 0, "l", 2), ("iX", 1, "h", 3), ("iX", 2, "l", 3)),
    (("iX", 0, "h", 2), ("io", 2, "l", 0), ("io", 1, "h", 1), ("iX", 1, "l", 2), ("io", 1, "h", 2), ("io", 2, "l", 1)),
    (("iX", 1, "h", 2), ("iX", 3, "l", 3), ("iy", 2, "h", 2), ("io", 3, "l", 0), ("oX", 0, "h", 2), ("iX", 2, "h", 3), ("oX", 0, "h", 3), ("io", 2, "h", 0), ("io", 2, "h", 1), ("io", 3, "l", 1), ("oo", 0, "h", 0), ("io", 2, "h", 2), ("oo", 0, "h", 1), ("iy", 3, "h", 2), ("oX", 1, "h", 2), ("iX", 3, "h", 3), ("oX", 0, "l", 2), ("iX", 2, "l", 2), ("oX", 0, "l", 3), ("oX", 1, "h", 3)),
    (("oo", 1, "h", 0), ("iX", 2, "h", 2), ("oo", 1, "h", 1), ("io", 3, "h", 0)),
    (("io", 3, "h", 1), ("iX", 3, "l", 2)),
    (("io", 3, "h", 2),),
    (),
    (("iX", 3, "h", 2), ("oX", 2, "h", 2), ("oo", 0, "l", 0), ("oX", 2, "h", 3)),
    (("oX", 1, "l", 2),),
    (("oo", 2, "h", 0), ("oX", 1, "l", 3)),
    (("oo", 2, "h", 1), ("oo", 1, "l", 0), ("oX", 2, "l", 2), ("oX", 3, "h", 2), ("oX", 2, "l", 3), ("oX", 3, "h", 3), ("oo", 2, "l", 0)),
    (("oX", 3, "l", 2), ("oo", 3, "h", 0), ("oX", 3, "l", 3), ("oo", 3, "h", 1), ("oo", 3, "l", 0)),
    (),
)

class Chains:
    def __init__(self, edge, at, refs):
        self.lam = {"h": 3, "l": 0} if edge else {"h": 2, "l": 1}
        self.at = at
        self.refs = refs
        self.sent = 0
        self.seen = set()

    def zpos(self, d, j, own):
        up, zhi = self.at["up"], self.at["zhi"]
        towards = up if d == "h" else 1 - up
        return (zhi if own else 1 - zhi) * 4 + jnp.where(towards == 1, j, 3 - j)

    def last_slot(self, d):
        towards = self.at["up"] if d == "h" else 1 - self.at["up"]
        return jnp.where(towards == 1, self.at["z"], RING)

    def block(self, name, q, slot=None):
        t, e = q // 2, q % 2
        rows = pl.ds(e * HALF, HALF)
        ref = self.refs[name]
        return ref.at[t, rows] if slot is None else ref.at[t, slot, rows]

    def copy(self, src, dst, recv, device):
        remote(src, dst, self.refs["z_send"].at[self.sent], recv, device).start()
        self.sent += 1

    def drain(self):
        for n in range(self.sent):
            one = self.block("tout", 0)
            remote(one, one, self.refs["z_send"].at[n], self.refs["t_recv"].at[0], self.at["h"]).wait_send()

    def arrive(self, dst, recv):
        remote(dst, dst, self.refs["z_send"].at[0], recv, self.at["h"]).wait_recv()

    def arrive_rows(self, q, d, j, own):
        if (q, d, j, own) in self.seen:
            return
        self.seen.add((q, d, j, own))
        zs = self.zpos(d, j, own)
        self.arrive(self.block("rows", q, zs), self.refs["in_recv"].at[q, zs])

    def all_rows(self, q):
        for d in ("h", "l"):
            for j in range(self.lam[d] - 1, -1, -1):
                self.arrive_rows(q, d, j, True)
            for j in (3, 2):
                self.arrive_rows(q, d, j, False)

    def add(self, q, zs, slot):
        self.arrive(self.block("rr", q, slot), self.refs["out_recv"].at[q, slot])
        part, rr = self.block("part", q, zs), self.block("rr", q, slot)
        part[...] = (part[...].astype(F32) + rr[...].astype(F32)).astype(BF)

    def finish(self, q):
        for d in ("h", "l"):
            if self.lam[d] < 3:
                self.add(q, self.at["z"], self.last_slot(d))
        self.arrive(self.block("ofin", q), self.refs["ot_recv"].at[q, 1])

    def emit(self, code, q, d, j):
        lam = self.lam[d]
        other = "l" if d == "h" else "h"
        in_recv, out_recv = self.refs["in_recv"], self.refs["out_recv"]
        if code in ("io", "iX"):
            own = code == "io"
            zs = self.zpos(d, j, own)
            if not own or j < lam:
                self.arrive_rows(q, d, j, own)
            rows = self.block("rows", q, zs)
            self.copy(rows, rows, in_recv.at[q, zs], self.at[d])
        elif code == "iO":
            z = self.at["z"]
            self.copy(self.block("tout", q), self.block("rows", q, z), in_recv.at[q, z], self.at[d])
        elif code == "iy":
            self.copy(self.block("tout", q), self.block("ttr", q), self.refs["t_recv"].at[q], self.at[d])
        elif code == "ix":
            ttr = self.block("ttr", q)
            self.arrive(ttr, self.refs["t_recv"].at[q])
            zs = self.zpos(d, 2, True)
            self.copy(ttr, self.block("rows", q, zs), in_recv.at[q, zs], self.at[d])
        elif code in ("oo", "oX"):
            own = code == "oo"
            zs = self.zpos(d, j, own)
            if lam < 3:
                self.add(q, zs, zs)
            part = self.block("part", q, zs)
            if lam > 0:
                slot = self.last_slot_of(d, zs) if own and j == lam - 1 else zs
                self.copy(part, self.block("rr", q, slot), out_recv.at[q, slot], self.at[other])
            elif j == 2:
                self.copy(part, self.block("otr", q), self.refs["ot_recv"].at[q, 0], self.at[other])
            else:
                self.copy(part, self.block("ofin", q), self.refs["ot_recv"].at[q, 1], self.at[other])
        else:
            otr = self.block("otr", q)
            self.arrive(otr, self.refs["ot_recv"].at[q, 0])
            self.copy(otr, self.block("ofin", q), self.refs["ot_recv"].at[q, 1], self.at[other])

    def last_slot_of(self, d, zs):
        towards = self.at["up"] if d == "h" else 1 - self.at["up"]
        return jnp.where(towards == 1, zs, RING)


def exchange_kernel(
    tokens_in, out_grad_in, router_in, win, wout,
    token_grad, router_out, g_in, g_out,
    tokens, out_grad, router,
    rt, disp, comb, d_log, sa, sb, rs, rrcv, zs, zr,
    prcv, fs, rows, tout, ttr, part, rr, ofin, otr, psend, prcv2,
    w_in, w_out, act, slope, dpre, acc,
    a_sem, w_sem, ps_send, ps_recv, po_send, po_recv,
    z_send, in_recv, t_recv, out_recv, ot_recv,
    pr_send, pr_recv, rz_send, rz_recv,
):
    p, zhi, h = place()
    z = zhi * 4 + h
    up = jnp.where(h >= 2, 1, 0)
    step = 2 * up - 1
    at = {
        "z": z,
        "zhi": zhi,
        "up": up,
        "h": ring_device(p, lax.rem(z + step + RING, RING)),
        "l": ring_device(p, lax.rem(z - step + RING, RING)),
    }
    refs = {
        "rows": rows, "tout": tout, "ttr": ttr, "part": part, "rr": rr, "ofin": ofin, "otr": otr,
        "z_send": z_send, "in_recv": in_recv, "t_recv": t_recv, "out_recv": out_recv, "ot_recv": ot_recv,
    }
    edge, inner = Chains(True, at, refs), Chains(False, at, refs)
    at_edge = jnp.logical_or(h == 0, h == 3)

    def both(body):
        @pl.when(at_edge)
        def _():
            body(edge, EDGE)

        @pl.when(jnp.logical_not(at_edge))
        def _():
            body(inner, INNER)

    a_copies = [
        pltpu.make_async_copy(src, dst, a_sem.at[n])
        for n, (src, dst) in enumerate(
            ((router_in, router), (tokens_in, tokens), (out_grad_in, out_grad))
        )
    ]
    for copy in a_copies:
        copy.start()
    w_copies = [
        pltpu.make_async_copy(win, w_in, w_sem.at[0]),
        pltpu.make_async_copy(wout, w_out, w_sem.at[1]),
    ]
    for copy in w_copies:
        copy.start()
    greet(p, zhi, h, tuple(range(1, RING)))

    natural = lax.broadcasted_iota(jnp.int32, (COLS, COLS), 0)
    placed = lax.broadcasted_iota(jnp.int32, (COLS, COLS), 1)
    source = (placed & 192) + ((placed & 4) << 3) + ((placed & 56) >> 1) + (placed & 3)
    pick = jnp.where(natural == source, 1.0, 0.0).astype(BF)
    a_copies[0].wait()
    rt[...] = jnp.dot(router[...], pick, preferred_element_type=F32).astype(BF)
    a_copies[1].wait()
    logits = jnp.dot(tokens[...], rt[...], preferred_element_type=F32)
    above = jnp.exp(logits - jnp.max(logits, axis=0, keepdims=True))
    disp[...] = above / jnp.sum(above, axis=0, keepdims=True)
    sa[...] = rounded_slots(disp[...].astype(BF), tokens[...])
    met()
    sends = (sa, sb)
    plane_start(p, zhi, h, sa, prcv.at[0], ps_send.at[0], ps_recv.at[0])
    a_copies[2].wait()
    above = jnp.exp(logits - jnp.max(logits, axis=1, keepdims=True))
    comb[...] = above / jnp.sum(above, axis=1, keepdims=True)
    sb[...] = rounded_slots(comb[...].astype(BF), out_grad[...])
    plane_start(p, zhi, h, sb, prcv.at[1], ps_send.at[1], ps_recv.at[1])

    def gather(t):
        plane_arrived(prcv.at[t], ps_recv.at[t])
        prcv[t, p] = sends[t][p]
        for c in range(LANES):
            lanes = slice(c * 128, (c + 1) * 128)
            fs[c] = prcv[t, :, :, lanes].astype(F32).reshape(COLS, 128)
            for s in range(4):
                piece = slice(s * PLANE, (s + 1) * PLANE)
                mine = fs[c, pl.ds(zhi * 4 + s, PLANE, stride=8), :]
                rows[t, z, piece, lanes] = mine.astype(BF)
                other = fs[c, pl.ds((1 - zhi) * 4 + s, PLANE, stride=8), :]
                tout[t, piece, lanes] = other.astype(BF)

    def out_last(t):
        def finish(chains, table):
            for e in (0, 1):
                chains.finish(2 * t + e)

        both(finish)
        for c in range(LANES):
            lanes = slice(c * 128, (c + 1) * 128)
            for s in range(4):
                piece = slice(s * PLANE, (s + 1) * PLANE)
                fs[c, pl.ds(zhi * 4 + s, PLANE, stride=8), :] = part[t, z, piece, lanes].astype(F32)
                fs[c, pl.ds((1 - zhi) * 4 + s, PLANE, stride=8), :] = ofin[t, piece, lanes].astype(F32)
            psend[t, :, :, lanes] = fs[c].reshape(PLANE, 8, 128).astype(BF)
        plane_start(p, zhi, h, psend.at[t], prcv2.at[t], po_send.at[t], po_recv.at[t])


    def expert_rows(t, e):
        return rows[t, :, e * HALF : (e + 1) * HALF, :].reshape(RING * HALF, D)

    def collect(t, e, f, more):
        if f == 0:
            acc[...] = more
        elif f == 1:
            acc[...] += more
        else:
            total = (acc[...] + more).astype(BF)
            part[t, :, e * HALF : (e + 1) * HALF, :] = total.reshape(RING, HALF, D)

    def forward_piece(e, f):
        span = slice(f * COLS, (f + 1) * COLS)
        pre = jnp.dot(expert_rows(0, e), w_in[e, :, span], preferred_element_type=F32)
        half = 0.5 * (1.0 + lax.erf(pre * 0.7071067811865476))
        value = (pre * half).astype(BF)
        act[e, :, span] = value
        slope[e, :, span] = half + pre * jnp.exp(-0.5 * pre * pre) * 0.3989422804014327
        more = jnp.dot(value, w_out[e, span, :], preferred_element_type=F32)
        collect(0, e, f, more)

    def backward_piece(e, f):
        span = slice(f * COLS, (f + 1) * COLS)
        d_act = lax.dot_general(
            expert_rows(1, e), w_out[e, span, :], (((1,), (1,)), ((), ())), preferred_element_type=F32
        )
        value = (d_act * slope[e, :, span]).astype(BF)
        dpre[e, :, span] = value
        more = lax.dot_general(
            value, w_in[e, :, span], (((1,), (1,)), ((), ())), preferred_element_type=F32
        )
        collect(1, e, f, more)

    def weight_piece(e, f):
        span = slice(f * COLS, (f + 1) * COLS)
        g_out[e, span, :] = lax.dot_general(
            act[e, :, span], expert_rows(1, e), (((0,), (0,)), ((), ())), preferred_element_type=F32
        ).astype(BF)
        g_in[e, :, span] = lax.dot_general(
            expert_rows(0, e), dpre[e, :, span], (((0,), (0,)), ((), ())), preferred_element_type=F32
        ).astype(BF)

    def segment(n):
        def body(chains, table):
            for item in table[n]:
                chains.emit(*item)

        both(body)

    gather(0)
    for n, event in enumerate(EVENTS):
        segment(n)
        kind, which = event[0], event[1:]
        if kind == "gather":
            gather(1)
        elif kind in ("fwd", "bwd"):
            (e,) = which
            q = e if kind == "fwd" else 2 + e
            both(lambda chains, table, q=q: chains.all_rows(q))
            if q == 0:
                for copy in w_copies:
                    copy.wait()
            for f in range(3):
                (forward_piece if kind == "fwd" else backward_piece)(e, f)
        elif kind == "wg":
            weight_piece(*which)
        else:
            out_last(which[0])
    segment(len(EVENTS))
    plane_arrived(prcv2.at[0], po_recv.at[0])
    prcv2[0, p] = psend[0, p]
    slot_out = prcv2[0].astype(F32).reshape(COLS, D).astype(BF)
    d_combine = across(out_grad[...], slot_out)
    mixed = comb[...] * d_combine
    d_log[...] = mixed - comb[...] * jnp.sum(mixed, axis=1, keepdims=True)
    plane_arrived(prcv2.at[1], po_recv.at[1])
    prcv2[1, p] = psend[1, p]
    slot_in_grad = prcv2[1].astype(F32).reshape(COLS, D).astype(BF)
    d_dispatch = across(tokens[...], slot_in_grad)
    mixed = disp[...] * d_dispatch
    d_logits = (d_log[...] + (mixed - disp[...] * jnp.sum(mixed, axis=0, keepdims=True))).astype(BF)
    rs[...] = rounded_slots(d_logits, tokens[...])
    plane_start(p, zhi, h, rs, rrcv, pr_send, pr_recv)
    token_grad[...] = (
        jnp.dot(disp[...].astype(BF), slot_in_grad, preferred_element_type=F32) + across(d_logits, rt[...])
    ).astype(BF)
    plane_arrived(rrcv, pr_recv)
    rrcv[p] = rs[p]
    zs[...] = jnp.sum(rrcv[...].astype(F32), axis=0)
    zr[z] = zs[:, pl.ds(window(h), COLS)]

    def ring_copy(j, arrival):
        to = lax.rem(z + j, RING)
        slot = to if arrival else z
        return remote(
            zs.at[:, pl.ds(window(lax.rem(to, 4)), COLS)],
            zr.at[slot],
            rz_send.at[to],
            rz_recv.at[slot],
            ring_device(p, to),
        )

    for j in range(1, RING):
        ring_copy(j, False).start()
    for j in range(1, RING):
        ring_copy(j, True).wait_recv()
    total = jnp.sum(zr[...], axis=0)
    total = jnp.where(zhi == 0, total[:4], total[4:])
    router_out[...] = jnp.where(lax.rem(h, 2) == 0, total[:, :192], total[:, 64:])

    for t in (0, 1):
        plane_sent(prcv.at[t], ps_send.at[t])
        plane_sent(psend.at[t], po_send.at[t])
    plane_sent(rrcv, pr_send)
    for j in range(1, RING):
        ring_copy(j, False).wait_send()

    both(lambda chains, table: chains.drain())


def rounded_slots(weights, values):
    sums = lax.dot_general(weights, values, (((0,), (0,)), ((), ())), preferred_element_type=F32)
    return sums.reshape(PLANE, 8, D).astype(BF)


def across(left, right):
    return lax.dot_general(left, right, (((1,), (1,)), ((), ())), preferred_element_type=F32)


def window(h):
    return pl.multiple_of((h + lax.div(h, 2)) * 128, 128)


def plane_start(p, zhi, h, src, dst, send, recv):
    def step(j, carry):
        q = lax.rem(p + j, PLANE)
        remote(src.at[q], dst.at[p], send, recv, plane_device(q, zhi, h)).start()
        return carry

    lax.fori_loop(1, PLANE, step, 0)


def plane_arrived(dst, recv):
    many = dst.at[pl.ds(0, PLANE - 1)]
    pltpu.make_async_copy(many, many, recv).wait()


def plane_sent(src, send):
    many = src.at[pl.ds(0, PLANE - 1)]
    pltpu.make_async_copy(many, many, send).wait()


def layer(tokens, out_grad, slot_router, weight_in, weight_out):
    vmem = pl.BlockSpec(memory_space=pltpu.VMEM)
    dma = pltpu.SemaphoreType.DMA
    experts = weight_in.shape[0]
    width = weight_in.shape[2]
    return pl.pallas_call(
        exchange_kernel,
        out_shape=(
            pltpu.VMEM(tokens.shape, BF),
            pltpu.VMEM((4, 192), F32),
            pltpu.VMEM(weight_in.shape, BF),
            pltpu.VMEM(weight_out.shape, BF),
        ),
        in_specs=[pl.BlockSpec(memory_space=pltpu.HBM)] * 5,
        out_specs=(vmem,) * 4,
        scratch_shapes=[
            pltpu.VMEM(tokens.shape, BF),
            pltpu.VMEM(out_grad.shape, BF),
            pltpu.VMEM(slot_router.shape, BF),
            pltpu.VMEM(slot_router.shape, BF),
            pltpu.VMEM((TOK, COLS), F32),
            pltpu.VMEM((TOK, COLS), F32),
            pltpu.VMEM((TOK, COLS), F32),
            pltpu.VMEM((PLANE, 8, D), BF),
            pltpu.VMEM((PLANE, 8, D), BF),
            pltpu.VMEM((PLANE, 8, D), BF),
            pltpu.VMEM((PLANE, 8, D), BF),
            pltpu.VMEM((8, D), F32),
            pltpu.VMEM((RING, 8, COLS), F32),
            pltpu.VMEM((2, PLANE, 8, D), BF),
            pltpu.VMEM((LANES, COLS, 128), F32),
            pltpu.VMEM((2, RING, ROWS, D), BF),
            pltpu.VMEM((2, ROWS, D), BF),
            pltpu.VMEM((2, ROWS, D), BF),
            pltpu.VMEM((2, RING, ROWS, D), BF),
            pltpu.VMEM((2, RING + 1, ROWS, D), BF),
            pltpu.VMEM((2, ROWS, D), BF),
            pltpu.VMEM((2, ROWS, D), BF),
            pltpu.VMEM((2, PLANE, 8, D), BF),
            pltpu.VMEM((2, PLANE, 8, D), BF),
            pltpu.VMEM(weight_in.shape, BF),
            pltpu.VMEM(weight_out.shape, BF),
            pltpu.VMEM((experts, RING * HALF, width), BF),
            pltpu.VMEM((experts, RING * HALF, width), F32),
            pltpu.VMEM((experts, RING * HALF, width), BF),
            pltpu.VMEM((RING * HALF, D), F32),
            dma((3,)),
            dma((2,)),
            dma((2,)),
            dma((2,)),
            dma((2,)),
            dma((2,)),
            dma((COPIES,)),
            dma((4, RING)),
            dma((4,)),
            dma((4, RING + 1)),
            dma((4, 2)),
            dma(()),
            dma(()),
            dma((RING,)),
            dma((RING,)),
        ],
        compiler_params=pltpu.CompilerParams(
            collective_id=0, has_side_effects=True, vmem_limit_bytes=61900000
        ),
        name="layer",
    )(tokens, out_grad, slot_router, weight_in, weight_out)


def store_kernel(*refs):
    count = len(refs) // 2
    sems = refs[-1]
    copies = [
        pltpu.make_async_copy(refs[n], refs[count + n], sems.at[n]) for n in range(count)
    ]
    for copy in copies:
        copy.start()
    for copy in copies:
        copy.wait()


def store(*arrays):
    return pl.pallas_call(
        store_kernel,
        out_shape=tuple(jax.ShapeDtypeStruct(a.shape, a.dtype) for a in arrays),
        in_specs=[pl.BlockSpec(memory_space=pl.ANY)] * len(arrays),
        out_specs=(pl.BlockSpec(memory_space=pltpu.HBM),) * len(arrays),
        scratch_shapes=[pltpu.SemaphoreType.DMA((len(arrays),))],
        compiler_params=pltpu.CompilerParams(vmem_limit_bytes=1024 * 1024),
        name="store",
    )(*arrays)


def per_device(tokens, out_grad, slot_router, weight_in, weight_out):
    token_grad, router_grad, grad_first, grad_second = store(
        *layer(tokens, out_grad, slot_router, weight_in, weight_out)
    )
    return (token_grad, router_grad.T, grad_first, grad_second)


def solution(mesh):
    return jax.shard_map(
        per_device,
        mesh=mesh,
        in_specs=(
            P(("expert", "hidden"), None),
            P(("expert", "hidden"), None),
            P(),
            P("expert", None, "hidden"),
            P("expert", "hidden", None),
        ),
        out_specs=(
            P(("expert", "hidden"), None),
            P("hidden", "expert"),
            P("expert", None, "hidden"),
            P("expert", "hidden", None),
        ),
        check_vma=False,
    )
```

```python
import jax
import jax.numpy as jnp
from jax import lax
from jax.experimental import pallas as pl
from jax.experimental.pallas import tpu as pltpu
from jax.sharding import PartitionSpec as P

D = 768
TOK = 196
PLANE = 32
RING = 8
ROWS = 128
COLS = 256
HALF = 64
COPIES = 80
LANES = 6
MESH = pl.DeviceIdType.MESH
BF = jnp.bfloat16
F32 = jnp.float32


def place():
    expert = lax.axis_index("expert")
    h = lax.axis_index("hidden")
    p = lax.div(expert, 16) * 8 + lax.rem(expert, 8)
    zhi = lax.rem(lax.div(expert, 8), 2)
    return p, zhi, h


def plane_device(q, zhi, h):
    return (lax.div(q, 8) * 16 + zhi * 8 + lax.rem(q, 8), h)


def ring_device(p, z):
    return (lax.div(p, 8) * 16 + lax.div(z, 4) * 8 + lax.rem(p, 8), lax.rem(z, 4))


def met():
    pl.semaphore_wait(pltpu.get_barrier_semaphore(), PLANE + RING - 2)


def remote(src, dst, send, recv, device):
    return pltpu.make_async_remote_copy(
        src_ref=src, dst_ref=dst, send_sem=send, recv_sem=recv, device_id=device, device_id_type=MESH
    )


def greet(p, zhi, h, ring_offsets):
    barrier = pltpu.get_barrier_semaphore()
    z = zhi * 4 + h

    def one(j, carry):
        pl.semaphore_signal(
            barrier, inc=1, device_id=plane_device(lax.rem(p + j, PLANE), zhi, h), device_id_type=MESH
        )
        return carry

    lax.fori_loop(1, PLANE, one, 0)
    for offset in ring_offsets:
        pl.semaphore_signal(
            barrier, inc=1, device_id=ring_device(p, lax.rem(z + offset, RING)), device_id_type=MESH
        )


EVENTS = (
    ("gather",),
    ("fwd", 0, 0),
    ("fwd", 0, 1),
    ("fwd", 0, 2),
    ("fwd", 1, 0),
    ("fwd", 1, 1),
    ("fwd", 1, 2),
    ("bwd", 0, 0),
    ("bwd", 0, 1),
    ("bwd", 0, 2),
    ("wg", 0, 0),
    ("wg", 0, 1),
    ("wg", 0, 2),
    ("bwd", 1, 0),
    ("bwd", 1, 1),
    ("bwd", 1, 2),
    ("wg", 1, 0),
    ("wg", 1, 1),
    ("wg", 1, 2),
    ("last", 0),
    ("last", 1),
)
EDGE = (
    (("io", 0, "l", 0), ("io", 1, "l", 0), ("iO", 0, "h", 3), ("iO", 1, "h", 3), ("ix", 0, "h", 2), ("iX", 0, "l", 3)),
    (("iX", 1, "l", 3), ("iO", 2, "h", 3), ("iX", 0, "l", 2), ("iO", 3, "h", 3), ("ix", 1, "h", 2), ("iX", 2, "l", 3), ("io", 3, "l", 0), ("iX", 1, "l", 2), ("io", 2, "l", 0), ("iX", 3, "l", 3)),
    (),
    (),
    (("oo", 0, "h", 0), ("oX", 0, "h", 2), ("ix", 2, "h", 2), ("iX", 2, "l", 2), ("oX", 0, "h", 3), ("ix", 3, "h", 2), ("iX", 3, "l", 2), ("oo", 0, "h", 1)),
    (),
    (("oo", 0, "h", 2),),
    (("oX", 1, "h", 2), ("oo", 1, "h", 1), ("oX", 1, "h", 3)),
    (),
    (),
    (("oo", 1, "h", 2), ("oo", 1, "h", 0), ("oo", 2, "h", 0)),
    (),
    (("oX", 2, "h", 2),),
    (("oX", 2, "h", 3),),
    (),
    (),
    (("oX", 3, "h", 2), ("oX", 0, "l", 3), ("oo", 3, "h", 0), ("oX", 0, "l", 2), ("oX", 3, "h", 3)),
    (("oo", 2, "h", 2), ("oX", 1, "l", 2), ("oX", 1, "l", 3)),
    (("oT", 0, "h", 2), ("oT", 1, "h", 2)),
    (("oo", 2, "h", 1),),
    (("oX", 2, "l", 2), ("oo", 3, "h", 1), ("oo", 3, "h", 2), ("oX", 3, "l", 2), ("oX", 2, "l", 3), ("oT", 2, "h", 2), ("oX", 3, "l", 3), ("oT", 3, "h", 2)),
    (),
)
INNER = (
    (("iy", 0, "h", 2), ("iy", 1, "h", 2), ("io", 0, "l", 1), ("io", 0, "h", 2), ("io", 1, "l", 1), ("io", 0, "l", 0), ("io", 0, "h", 1), ("io", 1, "l", 0), ("io", 0, "h", 0), ("iX", 0, "l", 3), ("io", 1, "h", 0), ("iX", 1, "l", 3), ("iX", 0, "l", 2), ("iX", 0, "h", 3)),
    (("iX", 1, "h", 3), ("iX", 0, "h", 2), ("iy", 2, "h", 2), ("io", 1, "h", 2), ("iy", 3, "h", 2), ("io", 3, "l", 1), ("iX", 1, "l", 2), ("io", 2, "l", 0), ("io", 1, "h", 1)),
    (("iX", 2, "l", 3),),
    (),
    (("io", 3, "l", 0), ("io", 2, "l", 1), ("iX", 1, "h", 2)),
    (("io", 2, "h", 0),),
    (("io", 2, "h", 2), ("io", 2, "h", 1), ("iX", 2, "l", 2), ("iX", 2, "h", 3), ("iX", 3, "l", 3)),
    (("oX", 0, "h", 2), ("iX", 2, "h", 2), ("oo", 0, "h", 0)),
    (("iX", 3, "h", 3), ("iX", 3, "l", 2), ("oX", 0, "h", 3), ("io", 3, "h", 0), ("io", 3, "h", 1), ("iX", 3, "h", 2), ("oX", 1, "h", 2)),
    (("io", 3, "h", 2), ("oo", 1, "h", 1), ("oX", 1, "h", 3)),
    (),
    (("oX", 0, "l", 3),),
    (),
    (),
    (("oX", 0, "l", 2),),
    (("oo", 1, "h", 0), ("oX", 1, "l", 2), ("oX", 1, "l", 3), ("oX", 2, "h", 2)),
    (("oo", 1, "l", 0), ("oo", 0, "l", 0)),
    (("oo", 0, "h", 1), ("oX", 2, "h", 3), ("oX", 3, "h", 2), ("oX", 3, "h", 3), ("oX", 2, "l", 2)),
    (("oX", 3, "l", 2), ("oo", 2, "h", 0)),
    (("oo", 3, "h", 0), ("oX", 2, "l", 3), ("oX", 3, "l", 3)),
    (("oo", 2, "l", 0), ("oo", 2, "h", 1), ("oo", 3, "l", 0), ("oo", 3, "h", 1)),
    (),
)

class Chains:
    def __init__(self, edge, at, refs):
        self.lam = {"h": 3, "l": 0} if edge else {"h": 2, "l": 1}
        self.at = at
        self.refs = refs
        self.sent = 0
        self.seen = set()

    def zpos(self, d, j, own):
        up, zhi = self.at["up"], self.at["zhi"]
        towards = up if d == "h" else 1 - up
        return (zhi if own else 1 - zhi) * 4 + jnp.where(towards == 1, j, 3 - j)

    def last_slot(self, d):
        towards = self.at["up"] if d == "h" else 1 - self.at["up"]
        return jnp.where(towards == 1, self.at["z"], RING)

    def block(self, name, q, slot=None):
        t, e = q // 2, q % 2
        rows = pl.ds(e * HALF, HALF)
        ref = self.refs[name]
        return ref.at[t, rows] if slot is None else ref.at[t, slot, rows]

    def copy(self, src, dst, recv, device):
        remote(src, dst, self.refs["z_send"].at[self.sent], recv, device).start()
        self.sent += 1

    def drain(self):
        for n in range(self.sent):
            one = self.block("tout", 0)
            remote(one, one, self.refs["z_send"].at[n], self.refs["t_recv"].at[0], self.at["h"]).wait_send()

    def arrive(self, dst, recv):
        remote(dst, dst, self.refs["z_send"].at[0], recv, self.at["h"]).wait_recv()

    def arrive_rows(self, q, d, j, own):
        if (q, d, j, own) in self.seen:
            return
        self.seen.add((q, d, j, own))
        zs = self.zpos(d, j, own)
        self.arrive(self.block("rows", q, zs), self.refs["in_recv"].at[q, zs])

    def all_rows(self, q):
        for d in ("h", "l"):
            for j in range(self.lam[d] - 1, -1, -1):
                self.arrive_rows(q, d, j, True)
            for j in (3, 2):
                self.arrive_rows(q, d, j, False)

    def add(self, q, zs, slot):
        self.arrive(self.block("rr", q, slot), self.refs["out_recv"].at[q, slot])
        part, rr = self.block("part", q, zs), self.block("rr", q, slot)
        part[...] = (part[...].astype(F32) + rr[...].astype(F32)).astype(BF)

    def finish(self, q):
        for d in ("h", "l"):
            if self.lam[d] < 3:
                self.add(q, self.at["z"], self.last_slot(d))
        self.arrive(self.block("ofin", q), self.refs["ot_recv"].at[q, 1])

    def emit(self, code, q, d, j):
        lam = self.lam[d]
        other = "l" if d == "h" else "h"
        in_recv, out_recv = self.refs["in_recv"], self.refs["out_recv"]
        if code in ("io", "iX"):
            own = code == "io"
            zs = self.zpos(d, j, own)
            if not own or j < lam:
                self.arrive_rows(q, d, j, own)
            rows = self.block("rows", q, zs)
            self.copy(rows, rows, in_recv.at[q, zs], self.at[d])
        elif code == "iO":
            z = self.at["z"]
            self.copy(self.block("tout", q), self.block("rows", q, z), in_recv.at[q, z], self.at[d])
        elif code == "iy":
            self.copy(self.block("tout", q), self.block("ttr", q), self.refs["t_recv"].at[q], self.at[d])
        elif code == "ix":
            ttr = self.block("ttr", q)
            self.arrive(ttr, self.refs["t_recv"].at[q])
            zs = self.zpos(d, 2, True)
            self.copy(ttr, self.block("rows", q, zs), in_recv.at[q, zs], self.at[d])
        elif code in ("oo", "oX"):
            own = code == "oo"
            zs = self.zpos(d, j, own)
            if lam < 3:
                self.add(q, zs, zs)
            part = self.block("part", q, zs)
            if lam > 0:
                slot = self.last_slot_of(d, zs) if own and j == lam - 1 else zs
                self.copy(part, self.block("rr", q, slot), out_recv.at[q, slot], self.at[other])
            elif j == 2:
                self.copy(part, self.block("otr", q), self.refs["ot_recv"].at[q, 0], self.at[other])
            else:
                self.copy(part, self.block("ofin", q), self.refs["ot_recv"].at[q, 1], self.at[other])
        else:
            otr = self.block("otr", q)
            self.arrive(otr, self.refs["ot_recv"].at[q, 0])
            self.copy(otr, self.block("ofin", q), self.refs["ot_recv"].at[q, 1], self.at[other])

    def last_slot_of(self, d, zs):
        towards = self.at["up"] if d == "h" else 1 - self.at["up"]
        return jnp.where(towards == 1, zs, RING)


def exchange_kernel(
    tokens_in, out_grad_in, router_in, win, wout,
    token_grad, router_out, g_in, g_out,
    tokens, out_grad, router,
    rt, disp, comb, d_log, sa, sb, rs, rrcv, zs, zr,
    prcv, fs, rows, tout, ttr, part, rr, ofin, otr, psend, prcv2,
    w_in, w_out, act, slope, dpre, acc,
    a_sem, w_sem, ps_send, ps_recv, po_send, po_recv,
    z_send, in_recv, t_recv, out_recv, ot_recv,
    pr_send, pr_recv, rz_send, rz_recv,
):
    p, zhi, h = place()
    z = zhi * 4 + h
    up = jnp.where(h >= 2, 1, 0)
    step = 2 * up - 1
    at = {
        "z": z,
        "zhi": zhi,
        "up": up,
        "h": ring_device(p, lax.rem(z + step + RING, RING)),
        "l": ring_device(p, lax.rem(z - step + RING, RING)),
    }
    refs = {
        "rows": rows, "tout": tout, "ttr": ttr, "part": part, "rr": rr, "ofin": ofin, "otr": otr,
        "z_send": z_send, "in_recv": in_recv, "t_recv": t_recv, "out_recv": out_recv, "ot_recv": ot_recv,
    }
    edge, inner = Chains(True, at, refs), Chains(False, at, refs)
    at_edge = jnp.logical_or(h == 0, h == 3)

    def both(body):
        @pl.when(at_edge)
        def _():
            body(edge, EDGE)

        @pl.when(jnp.logical_not(at_edge))
        def _():
            body(inner, INNER)

    a_copies = [
        pltpu.make_async_copy(src, dst, a_sem.at[n])
        for n, (src, dst) in enumerate(
            ((router_in, router), (tokens_in, tokens), (out_grad_in, out_grad))
        )
    ]
    for copy in a_copies:
        copy.start()
    w_copies = [
        pltpu.make_async_copy(win, w_in, w_sem.at[0]),
        pltpu.make_async_copy(wout, w_out, w_sem.at[1]),
    ]
    for copy in w_copies:
        copy.start()
    greet(p, zhi, h, tuple(range(1, RING)))

    natural = lax.broadcasted_iota(jnp.int32, (COLS, COLS), 0)
    placed = lax.broadcasted_iota(jnp.int32, (COLS, COLS), 1)
    source = (placed & 192) + ((placed & 4) << 3) + ((placed & 56) >> 1) + (placed & 3)
    pick = jnp.where(natural == source, 1.0, 0.0).astype(BF)
    a_copies[0].wait()
    rt[...] = jnp.dot(router[...], pick, preferred_element_type=F32).astype(BF)
    a_copies[1].wait()
    logits = jnp.dot(tokens[...], rt[...], preferred_element_type=F32)
    above = jnp.exp(logits - jnp.max(logits, axis=0, keepdims=True))
    disp[...] = above / jnp.sum(above, axis=0, keepdims=True)
    sa[...] = rounded_slots(disp[...].astype(BF), tokens[...])
    met()
    sends = (sa, sb)
    plane_start(p, zhi, h, sa, prcv.at[0], ps_send.at[0], ps_recv.at[0])
    a_copies[2].wait()
    above = jnp.exp(logits - jnp.max(logits, axis=1, keepdims=True))
    comb[...] = above / jnp.sum(above, axis=1, keepdims=True)
    sb[...] = rounded_slots(comb[...].astype(BF), out_grad[...])
    plane_start(p, zhi, h, sb, prcv.at[1], ps_send.at[1], ps_recv.at[1])

    def gather(t):
        plane_arrived(prcv.at[t], ps_recv.at[t])
        prcv[t, p] = sends[t][p]
        for c in range(LANES):
            lanes = slice(c * 128, (c + 1) * 128)
            fs[c] = prcv[t, :, :, lanes].astype(F32).reshape(COLS, 128)
            for s in range(4):
                piece = slice(s * PLANE, (s + 1) * PLANE)
                mine = fs[c, pl.ds(zhi * 4 + s, PLANE, stride=8), :]
                rows[t, z, piece, lanes] = mine.astype(BF)
                other = fs[c, pl.ds((1 - zhi) * 4 + s, PLANE, stride=8), :]
                tout[t, piece, lanes] = other.astype(BF)

    def out_last(t):
        def finish(chains, table):
            for e in (0, 1):
                chains.finish(2 * t + e)

        both(finish)
        for c in range(LANES):
            lanes = slice(c * 128, (c + 1) * 128)
            for s in range(4):
                piece = slice(s * PLANE, (s + 1) * PLANE)
                fs[c, pl.ds(zhi * 4 + s, PLANE, stride=8), :] = part[t, z, piece, lanes].astype(F32)
                fs[c, pl.ds((1 - zhi) * 4 + s, PLANE, stride=8), :] = ofin[t, piece, lanes].astype(F32)
            psend[t, :, :, lanes] = fs[c].reshape(PLANE, 8, 128).astype(BF)
        plane_start(p, zhi, h, psend.at[t], prcv2.at[t], po_send.at[t], po_recv.at[t])


    def expert_rows(t, e):
        return rows[t, :, e * HALF : (e + 1) * HALF, :].reshape(RING * HALF, D)

    def collect(t, e, f, more):
        if f == 0:
            acc[...] = more
        elif f == 1:
            acc[...] += more
        else:
            total = (acc[...] + more).astype(BF)
            part[t, :, e * HALF : (e + 1) * HALF, :] = total.reshape(RING, HALF, D)

    def forward_piece(e, f):
        span = slice(f * COLS, (f + 1) * COLS)
        pre = jnp.dot(expert_rows(0, e), w_in[e, :, span], preferred_element_type=F32)
        half = 0.5 * (1.0 + lax.erf(pre * 0.7071067811865476))
        value = (pre * half).astype(BF)
        act[e, :, span] = value
        slope[e, :, span] = half + pre * jnp.exp(-0.5 * pre * pre) * 0.3989422804014327
        more = jnp.dot(value, w_out[e, span, :], preferred_element_type=F32)
        collect(0, e, f, more)

    def backward_piece(e, f):
        span = slice(f * COLS, (f + 1) * COLS)
        d_act = lax.dot_general(
            expert_rows(1, e), w_out[e, span, :], (((1,), (1,)), ((), ())), preferred_element_type=F32
        )
        value = (d_act * slope[e, :, span]).astype(BF)
        dpre[e, :, span] = value
        more = lax.dot_general(
            value, w_in[e, :, span], (((1,), (1,)), ((), ())), preferred_element_type=F32
        )
        collect(1, e, f, more)

    def weight_piece(e, f):
        span = slice(f * COLS, (f + 1) * COLS)
        g_out[e, span, :] = lax.dot_general(
            act[e, :, span], expert_rows(1, e), (((0,), (0,)), ((), ())), preferred_element_type=F32
        ).astype(BF)
        g_in[e, :, span] = lax.dot_general(
            expert_rows(0, e), dpre[e, :, span], (((0,), (0,)), ((), ())), preferred_element_type=F32
        ).astype(BF)

    def segment(n):
        def body(chains, table):
            for item in table[n]:
                chains.emit(*item)

        both(body)

    gather(0)
    for n, event in enumerate(EVENTS):
        segment(n)
        kind, which = event[0], event[1:]
        if kind == "gather":
            gather(1)
        elif kind in ("fwd", "bwd"):
            e, f = which
            q = e if kind == "fwd" else 2 + e
            if f == 0:
                both(lambda chains, table, q=q: chains.all_rows(q))
            if (q, f) == (0, 0):
                for copy in w_copies:
                    copy.wait()
            (forward_piece if kind == "fwd" else backward_piece)(e, f)
        elif kind == "wg":
            weight_piece(*which)
        else:
            out_last(which[0])
    segment(len(EVENTS))
    plane_arrived(prcv2.at[0], po_recv.at[0])
    prcv2[0, p] = psend[0, p]
    slot_out = prcv2[0].astype(F32).reshape(COLS, D).astype(BF)
    d_combine = across(out_grad[...], slot_out)
    mixed = comb[...] * d_combine
    d_log[...] = mixed - comb[...] * jnp.sum(mixed, axis=1, keepdims=True)
    plane_arrived(prcv2.at[1], po_recv.at[1])
    prcv2[1, p] = psend[1, p]
    slot_in_grad = prcv2[1].astype(F32).reshape(COLS, D).astype(BF)
    d_dispatch = across(tokens[...], slot_in_grad)
    mixed = disp[...] * d_dispatch
    d_logits = (d_log[...] + (mixed - disp[...] * jnp.sum(mixed, axis=0, keepdims=True))).astype(BF)
    rs[...] = rounded_slots(d_logits, tokens[...])
    plane_start(p, zhi, h, rs, rrcv, pr_send, pr_recv)
    token_grad[...] = (
        jnp.dot(disp[...].astype(BF), slot_in_grad, preferred_element_type=F32) + across(d_logits, rt[...])
    ).astype(BF)
    plane_arrived(rrcv, pr_recv)
    rrcv[p] = rs[p]
    zs[...] = jnp.sum(rrcv[...].astype(F32), axis=0)
    zr[z] = zs[:, pl.ds(window(h), COLS)]

    def ring_copy(j, arrival):
        to = lax.rem(z + j, RING)
        slot = to if arrival else z
        return remote(
            zs.at[:, pl.ds(window(lax.rem(to, 4)), COLS)],
            zr.at[slot],
            rz_send.at[to],
            rz_recv.at[slot],
            ring_device(p, to),
        )

    for j in range(1, RING):
        ring_copy(j, False).start()
    for j in range(1, RING):
        ring_copy(j, True).wait_recv()
    total = jnp.sum(zr[...], axis=0)
    total = jnp.where(zhi == 0, total[:4], total[4:])
    router_out[...] = jnp.where(lax.rem(h, 2) == 0, total[:, :192], total[:, 64:])

    for t in (0, 1):
        plane_sent(prcv.at[t], ps_send.at[t])
        plane_sent(psend.at[t], po_send.at[t])
    plane_sent(rrcv, pr_send)
    for j in range(1, RING):
        ring_copy(j, False).wait_send()

    both(lambda chains, table: chains.drain())


def rounded_slots(weights, values):
    sums = lax.dot_general(weights, values, (((0,), (0,)), ((), ())), preferred_element_type=F32)
    return sums.reshape(PLANE, 8, D).astype(BF)


def across(left, right):
    return lax.dot_general(left, right, (((1,), (1,)), ((), ())), preferred_element_type=F32)


def window(h):
    return pl.multiple_of((h + lax.div(h, 2)) * 128, 128)


def plane_start(p, zhi, h, src, dst, send, recv):
    def step(j, carry):
        q = lax.rem(p + j, PLANE)
        remote(src.at[q], dst.at[p], send, recv, plane_device(q, zhi, h)).start()
        return carry

    lax.fori_loop(1, PLANE, step, 0)


def plane_arrived(dst, recv):
    many = dst.at[pl.ds(0, PLANE - 1)]
    pltpu.make_async_copy(many, many, recv).wait()


def plane_sent(src, send):
    many = src.at[pl.ds(0, PLANE - 1)]
    pltpu.make_async_copy(many, many, send).wait()


def layer(tokens, out_grad, slot_router, weight_in, weight_out):
    vmem = pl.BlockSpec(memory_space=pltpu.VMEM)
    dma = pltpu.SemaphoreType.DMA
    experts = weight_in.shape[0]
    width = weight_in.shape[2]
    return pl.pallas_call(
        exchange_kernel,
        out_shape=(
            pltpu.VMEM(tokens.shape, BF),
            pltpu.VMEM((4, 192), F32),
            pltpu.VMEM(weight_in.shape, BF),
            pltpu.VMEM(weight_out.shape, BF),
        ),
        in_specs=[pl.BlockSpec(memory_space=pltpu.HBM)] * 5,
        out_specs=(vmem,) * 4,
        scratch_shapes=[
            pltpu.VMEM(tokens.shape, BF),
            pltpu.VMEM(out_grad.shape, BF),
            pltpu.VMEM(slot_router.shape, BF),
            pltpu.VMEM(slot_router.shape, BF),
            pltpu.VMEM((TOK, COLS), F32),
            pltpu.VMEM((TOK, COLS), F32),
            pltpu.VMEM((TOK, COLS), F32),
            pltpu.VMEM((PLANE, 8, D), BF),
            pltpu.VMEM((PLANE, 8, D), BF),
            pltpu.VMEM((PLANE, 8, D), BF),
            pltpu.VMEM((PLANE, 8, D), BF),
            pltpu.VMEM((8, D), F32),
            pltpu.VMEM((RING, 8, COLS), F32),
            pltpu.VMEM((2, PLANE, 8, D), BF),
            pltpu.VMEM((LANES, COLS, 128), F32),
            pltpu.VMEM((2, RING, ROWS, D), BF),
            pltpu.VMEM((2, ROWS, D), BF),
            pltpu.VMEM((2, ROWS, D), BF),
            pltpu.VMEM((2, RING, ROWS, D), BF),
            pltpu.VMEM((2, RING + 1, ROWS, D), BF),
            pltpu.VMEM((2, ROWS, D), BF),
            pltpu.VMEM((2, ROWS, D), BF),
            pltpu.VMEM((2, PLANE, 8, D), BF),
            pltpu.VMEM((2, PLANE, 8, D), BF),
            pltpu.VMEM(weight_in.shape, BF),
            pltpu.VMEM(weight_out.shape, BF),
            pltpu.VMEM((experts, RING * HALF, width), BF),
            pltpu.VMEM((experts, RING * HALF, width), F32),
            pltpu.VMEM((experts, RING * HALF, width), BF),
            pltpu.VMEM((RING * HALF, D), F32),
            dma((3,)),
            dma((2,)),
            dma((2,)),
            dma((2,)),
            dma((2,)),
            dma((2,)),
            dma((COPIES,)),
            dma((4, RING)),
            dma((4,)),
            dma((4, RING + 1)),
            dma((4, 2)),
            dma(()),
            dma(()),
            dma((RING,)),
            dma((RING,)),
        ],
        compiler_params=pltpu.CompilerParams(
            collective_id=0, has_side_effects=True, vmem_limit_bytes=61900000
        ),
        name="layer",
    )(tokens, out_grad, slot_router, weight_in, weight_out)


def store_kernel(*refs):
    count = len(refs) // 2
    sems = refs[-1]
    copies = [
        pltpu.make_async_copy(refs[n], refs[count + n], sems.at[n]) for n in range(count)
    ]
    for copy in copies:
        copy.start()
    for copy in copies:
        copy.wait()


def store(*arrays):
    return pl.pallas_call(
        store_kernel,
        out_shape=tuple(jax.ShapeDtypeStruct(a.shape, a.dtype) for a in arrays),
        in_specs=[pl.BlockSpec(memory_space=pl.ANY)] * len(arrays),
        out_specs=(pl.BlockSpec(memory_space=pltpu.HBM),) * len(arrays),
        scratch_shapes=[pltpu.SemaphoreType.DMA((len(arrays),))],
        compiler_params=pltpu.CompilerParams(vmem_limit_bytes=1024 * 1024),
        name="store",
    )(*arrays)


def per_device(tokens, out_grad, slot_router, weight_in, weight_out):
    token_grad, router_grad, grad_first, grad_second = store(
        *layer(tokens, out_grad, slot_router, weight_in, weight_out)
    )
    return (token_grad, router_grad.T, grad_first, grad_second)


def solution(mesh):
    return jax.shard_map(
        per_device,
        mesh=mesh,
        in_specs=(
            P(("expert", "hidden"), None),
            P(("expert", "hidden"), None),
            P(),
            P("expert", None, "hidden"),
            P("expert", "hidden", None),
        ),
        out_specs=(
            P(("expert", "hidden"), None),
            P("hidden", "expert"),
            P("expert", None, "hidden"),
            P("expert", "hidden", None),
        ),
        check_vma=False,
    )
```

```python
import jax
import jax.numpy as jnp
from jax import lax
from jax.experimental import pallas as pl
from jax.experimental.pallas import tpu as pltpu
from jax.sharding import PartitionSpec as P

D = 768
TOK = 196
PLANE = 32
RING = 8
ROWS = 128
COLS = 256
HALF = 64
COPIES = 80
LANES = 6
MESH = pl.DeviceIdType.MESH
BF = jnp.bfloat16
F32 = jnp.float32


def place():
    expert = lax.axis_index("expert")
    h = lax.axis_index("hidden")
    p = lax.div(expert, 16) * 8 + lax.rem(expert, 8)
    zhi = lax.rem(lax.div(expert, 8), 2)
    return p, zhi, h


def plane_device(q, zhi, h):
    return (lax.div(q, 8) * 16 + zhi * 8 + lax.rem(q, 8), h)


def ring_device(p, z):
    return (lax.div(p, 8) * 16 + lax.div(z, 4) * 8 + lax.rem(p, 8), lax.rem(z, 4))


def met():
    pl.semaphore_wait(pltpu.get_barrier_semaphore(), PLANE + RING - 2)


def remote(src, dst, send, recv, device):
    return pltpu.make_async_remote_copy(
        src_ref=src, dst_ref=dst, send_sem=send, recv_sem=recv, device_id=device, device_id_type=MESH
    )


def greet(p, zhi, h, ring_offsets):
    barrier = pltpu.get_barrier_semaphore()
    z = zhi * 4 + h

    def one(j, carry):
        pl.semaphore_signal(
            barrier, inc=1, device_id=plane_device(lax.rem(p + j, PLANE), zhi, h), device_id_type=MESH
        )
        return carry

    lax.fori_loop(1, PLANE, one, 0)
    for offset in ring_offsets:
        pl.semaphore_signal(
            barrier, inc=1, device_id=ring_device(p, lax.rem(z + offset, RING)), device_id_type=MESH
        )


EVENTS = (
    ("gather",),
    ("fwd", 0, 0),
    ("fwd", 0, 1),
    ("fwd", 0, 2),
    ("fwd", 1, 0),
    ("fwd", 1, 1),
    ("fwd", 1, 2),
    ("bwd", 0, 0),
    ("bwd", 0, 1),
    ("bwd", 0, 2),
    ("wg", 0, 0),
    ("wg", 0, 1),
    ("wg", 0, 2),
    ("bwd", 1, 0),
    ("bwd", 1, 1),
    ("bwd", 1, 2),
    ("wg", 1, 0),
    ("wg", 1, 1),
    ("wg", 1, 2),
    ("last", 0),
    ("last", 1),
)
EDGE = (
    (("io", 0, "l", 0), ("io", 1, "l", 0), ("iO", 0, "h", 3), ("iO", 1, "h", 3), ("ix", 0, "h", 2), ("iX", 0, "l", 3), ("ix", 1, "h", 2), ("iX", 1, "l", 3), ("iX", 0, "l", 2)),
    (("iO", 2, "h", 3), ("io", 3, "l", 0), ("iX", 1, "l", 2), ("iO", 3, "h", 3), ("ix", 2, "h", 2), ("io", 2, "l", 0), ("iX", 2, "l", 3), ("iX", 2, "l", 2), ("iX", 3, "l", 3)),
    (),
    (),
    (("oX", 0, "h", 3), ("oo", 0, "h", 2), ("ix", 3, "h", 2), ("oX", 0, "h", 2), ("iX", 3, "l", 2), ("oo", 0, "h", 0)),
    (("oo", 0, "h", 1),),
    (),
    (("oX", 1, "h", 2), ("oo", 1, "h", 1), ("oo", 1, "h", 0), ("oX", 1, "h", 3)),
    (),
    (),
    (("oX", 2, "h", 3), ("oo", 2, "h", 0)),
    (("oX", 0, "l", 2), ("oX", 2, "h", 2)),
    (("oo", 1, "h", 2), ("oo", 2, "h", 1)),
    (("oT", 0, "h", 2),),
    (),
    (),
    (("oX", 3, "h", 2),),
    (("oX", 3, "h", 3), ("oX", 1, "l", 2), ("oo", 3, "h", 0)),
    (("oX", 1, "l", 3), ("oX", 0, "l", 3), ("oT", 1, "h", 2), ("oo", 2, "h", 2), ("oo", 3, "h", 2), ("oX", 2, "l", 2), ("oo", 3, "h", 1), ("oX", 2, "l", 3), ("oX", 3, "l", 2)),
    (("oT", 2, "h", 2), ("oX", 3, "l", 3), ("oT", 3, "h", 2)),
    (),
    (),
)
INNER = (
    (("iy", 0, "h", 2), ("iy", 1, "h", 2), ("io", 0, "l", 1), ("io", 0, "l", 0), ("io", 1, "h", 2), ("io", 0, "h", 2), ("io", 1, "l", 0), ("io", 1, "l", 1)),
    (("io", 0, "h", 1), ("iy", 2, "h", 2), ("iX", 0, "l", 3), ("io", 0, "h", 0), ("iX", 0, "l", 2), ("io", 3, "l", 1), ("iX", 0, "h", 3), ("io", 2, "l", 1), ("iX", 0, "h", 2)),
    (("iy", 3, "h", 2), ("iX", 1, "l", 2), ("iX", 1, "l", 3)),
    (("io", 2, "l", 0), ("io", 1, "h", 1), ("iX", 2, "l", 3)),
    (("iX", 1, "h", 2), ("iX", 2, "l", 2), ("io", 1, "h", 0), ("iX", 1, "h", 3), ("io", 2, "h", 2)),
    (("io", 3, "l", 0),),
    (("io", 2, "h", 1), ("oX", 0, "h", 3)),
    (("io", 2, "h", 0), ("iX", 2, "h", 3), ("iX", 3, "l", 2), ("oX", 0, "h", 2), ("oo", 0, "h", 0), ("iX", 3, "l", 3), ("iX", 2, "h", 2), ("io", 3, "h", 0), ("oX", 0, "l", 2)),
    (("oX", 1, "h", 2), ("oo", 0, "h", 1)),
    (("io", 3, "h", 1),),
    (("iX", 3, "h", 2), ("iX", 3, "h", 3)),
    (("oX", 1, "h", 3),),
    (("io", 3, "h", 2), ("oo", 1, "h", 0), ("oX", 2, "h", 3), ("oX", 1, "l", 2)),
    (("oX", 2, "h", 2), ("oX", 1, "l", 3)),
    (("oo", 2, "h", 0), ("oX", 0, "l", 3), ("oo", 2, "h", 1), ("oX", 2, "l", 2), ("oo", 1, "h", 1)),
    (),
    (),
    (("oX", 2, "l", 3), ("oX", 3, "h", 2)),
    (("oo", 0, "l", 0), ("oX", 3, "h", 3), ("oX", 3, "l", 2), ("oo", 3, "h", 0)),
    (("oX", 3, "l", 3), ("oo", 1, "l", 0)),
    (("oo", 3, "l", 0), ("oo", 2, "l", 0), ("oo", 3, "h", 1)),
    (),
)

class Chains:
    def __init__(self, edge, at, refs):
        self.lam = {"h": 3, "l": 0} if edge else {"h": 2, "l": 1}
        self.at = at
        self.refs = refs
        self.sent = 0
        self.seen = set()

    def zpos(self, d, j, own):
        up, zhi = self.at["up"], self.at["zhi"]
        towards = up if d == "h" else 1 - up
        return (zhi if own else 1 - zhi) * 4 + jnp.where(towards == 1, j, 3 - j)

    def last_slot(self, d):
        towards = self.at["up"] if d == "h" else 1 - self.at["up"]
        return jnp.where(towards == 1, self.at["z"], RING)

    def block(self, name, q, slot=None):
        t, e = q // 2, q % 2
        rows = pl.ds(e * HALF, HALF)
        ref = self.refs[name]
        return ref.at[t, rows] if slot is None else ref.at[t, slot, rows]

    def copy(self, src, dst, recv, device):
        remote(src, dst, self.refs["z_send"].at[self.sent], recv, device).start()
        self.sent += 1

    def drain(self):
        for n in range(self.sent):
            one = self.block("tout", 0)
            remote(one, one, self.refs["z_send"].at[n], self.refs["t_recv"].at[0], self.at["h"]).wait_send()

    def arrive(self, dst, recv):
        remote(dst, dst, self.refs["z_send"].at[0], recv, self.at["h"]).wait_recv()

    def arrive_rows(self, q, d, j, own):
        if (q, d, j, own) in self.seen:
            return
        self.seen.add((q, d, j, own))
        zs = self.zpos(d, j, own)
        self.arrive(self.block("rows", q, zs), self.refs["in_recv"].at[q, zs])

    def all_rows(self, q):
        for d in ("h", "l"):
            for j in range(self.lam[d] - 1, -1, -1):
                self.arrive_rows(q, d, j, True)
            for j in (3, 2):
                self.arrive_rows(q, d, j, False)

    def add(self, q, zs, slot):
        self.arrive(self.block("rr", q, slot), self.refs["out_recv"].at[q, slot])
        part, rr = self.block("part", q, zs), self.block("rr", q, slot)
        part[...] = (part[...].astype(F32) + rr[...].astype(F32)).astype(BF)

    def finish(self, q):
        for d in ("h", "l"):
            if self.lam[d] < 3:
                self.add(q, self.at["z"], self.last_slot(d))
        self.arrive(self.block("ofin", q), self.refs["ot_recv"].at[q, 1])

    def emit(self, code, q, d, j):
        lam = self.lam[d]
        other = "l" if d == "h" else "h"
        in_recv, out_recv = self.refs["in_recv"], self.refs["out_recv"]
        if code in ("io", "iX"):
            own = code == "io"
            zs = self.zpos(d, j, own)
            if not own or j < lam:
                self.arrive_rows(q, d, j, own)
            rows = self.block("rows", q, zs)
            self.copy(rows, rows, in_recv.at[q, zs], self.at[d])
        elif code == "iO":
            z = self.at["z"]
            self.copy(self.block("tout", q), self.block("rows", q, z), in_recv.at[q, z], self.at[d])
        elif code == "iy":
            self.copy(self.block("tout", q), self.block("ttr", q), self.refs["t_recv"].at[q], self.at[d])
        elif code == "ix":
            ttr = self.block("ttr", q)
            self.arrive(ttr, self.refs["t_recv"].at[q])
            zs = self.zpos(d, 2, True)
            self.copy(ttr, self.block("rows", q, zs), in_recv.at[q, zs], self.at[d])
        elif code in ("oo", "oX"):
            own = code == "oo"
            zs = self.zpos(d, j, own)
            if lam < 3:
                self.add(q, zs, zs)
            part = self.block("part", q, zs)
            if lam > 0:
                slot = self.last_slot_of(d, zs) if own and j == lam - 1 else zs
                self.copy(part, self.block("rr", q, slot), out_recv.at[q, slot], self.at[other])
            elif j == 2:
                self.copy(part, self.block("otr", q), self.refs["ot_recv"].at[q, 0], self.at[other])
            else:
                self.copy(part, self.block("ofin", q), self.refs["ot_recv"].at[q, 1], self.at[other])
        else:
            otr = self.block("otr", q)
            self.arrive(otr, self.refs["ot_recv"].at[q, 0])
            self.copy(otr, self.block("ofin", q), self.refs["ot_recv"].at[q, 1], self.at[other])

    def last_slot_of(self, d, zs):
        towards = self.at["up"] if d == "h" else 1 - self.at["up"]
        return jnp.where(towards == 1, zs, RING)


def exchange_kernel(
    tokens_in, out_grad_in, router_in, win, wout,
    token_grad, router_out, g_in, g_out,
    tokens, out_grad, router,
    rt, disp, comb, d_log, sa, sb, rs, rrcv, zs, zr,
    prcv, fs, rows, tout, ttr, part, rr, ofin, otr, psend, prcv2,
    w_in, w_out, act, slope, dpre, acc,
    a_sem, w_sem, ps_send, ps_recv, po_send, po_recv,
    z_send, in_recv, t_recv, out_recv, ot_recv,
    pr_send, pr_recv, rz_send, rz_recv,
):
    p, zhi, h = place()
    z = zhi * 4 + h
    up = jnp.where(h >= 2, 1, 0)
    step = 2 * up - 1
    at = {
        "z": z,
        "zhi": zhi,
        "up": up,
        "h": ring_device(p, lax.rem(z + step + RING, RING)),
        "l": ring_device(p, lax.rem(z - step + RING, RING)),
    }
    refs = {
        "rows": rows, "tout": tout, "ttr": ttr, "part": part, "rr": rr, "ofin": ofin, "otr": otr,
        "z_send": z_send, "in_recv": in_recv, "t_recv": t_recv, "out_recv": out_recv, "ot_recv": ot_recv,
    }
    edge, inner = Chains(True, at, refs), Chains(False, at, refs)
    at_edge = jnp.logical_or(h == 0, h == 3)

    def both(body):
        @pl.when(at_edge)
        def _():
            body(edge, EDGE)

        @pl.when(jnp.logical_not(at_edge))
        def _():
            body(inner, INNER)

    a_copies = [
        pltpu.make_async_copy(src, dst, a_sem.at[n])
        for n, (src, dst) in enumerate(
            ((router_in, router), (tokens_in, tokens), (out_grad_in, out_grad))
        )
    ]
    for copy in a_copies:
        copy.start()
    w_copies = [
        pltpu.make_async_copy(win, w_in, w_sem.at[0]),
        pltpu.make_async_copy(wout, w_out, w_sem.at[1]),
    ]
    for copy in w_copies:
        copy.start()
    greet(p, zhi, h, tuple(range(1, RING)))

    natural = lax.broadcasted_iota(jnp.int32, (COLS, COLS), 0)
    placed = lax.broadcasted_iota(jnp.int32, (COLS, COLS), 1)
    source = (placed & 192) + ((placed & 4) << 3) + ((placed & 56) >> 1) + (placed & 3)
    pick = jnp.where(natural == source, 1.0, 0.0).astype(BF)
    a_copies[0].wait()
    rt[...] = jnp.dot(router[...], pick, preferred_element_type=F32).astype(BF)
    a_copies[1].wait()
    logits = jnp.dot(tokens[...], rt[...], preferred_element_type=F32)
    above = jnp.exp(logits - jnp.max(logits, axis=0, keepdims=True))
    disp[...] = above / jnp.sum(above, axis=0, keepdims=True)
    sa[...] = rounded_slots(disp[...].astype(BF), tokens[...])
    met()
    sends = (sa, sb)
    plane_start(p, zhi, h, sa, prcv.at[0], ps_send.at[0], ps_recv.at[0])
    a_copies[2].wait()
    above = jnp.exp(logits - jnp.max(logits, axis=1, keepdims=True))
    comb[...] = above / jnp.sum(above, axis=1, keepdims=True)
    sb[...] = rounded_slots(comb[...].astype(BF), out_grad[...])
    plane_start(p, zhi, h, sb, prcv.at[1], ps_send.at[1], ps_recv.at[1])

    def gather(t):
        plane_arrived(prcv.at[t], ps_recv.at[t])
        prcv[t, p] = sends[t][p]
        for c in range(LANES):
            lanes = slice(c * 128, (c + 1) * 128)
            fs[c] = prcv[t, :, :, lanes].astype(F32).reshape(COLS, 128)
            for s in range(4):
                piece = slice(s * PLANE, (s + 1) * PLANE)
                mine = fs[c, pl.ds(zhi * 4 + s, PLANE, stride=8), :]
                rows[t, z, piece, lanes] = mine.astype(BF)
                other = fs[c, pl.ds((1 - zhi) * 4 + s, PLANE, stride=8), :]
                tout[t, piece, lanes] = other.astype(BF)

    def out_last(t):
        def finish(chains, table):
            for e in (0, 1):
                chains.finish(2 * t + e)

        both(finish)
        for c in range(LANES):
            lanes = slice(c * 128, (c + 1) * 128)
            for s in range(4):
                piece = slice(s * PLANE, (s + 1) * PLANE)
                fs[c, pl.ds(zhi * 4 + s, PLANE, stride=8), :] = part[t, z, piece, lanes].astype(F32)
                fs[c, pl.ds((1 - zhi) * 4 + s, PLANE, stride=8), :] = ofin[t, piece, lanes].astype(F32)
            psend[t, :, :, lanes] = fs[c].reshape(PLANE, 8, 128).astype(BF)
        plane_start(p, zhi, h, psend.at[t], prcv2.at[t], po_send.at[t], po_recv.at[t])


    def expert_rows(t, e):
        return rows[t, :, e * HALF : (e + 1) * HALF, :].reshape(RING * HALF, D)

    def collect(t, e, f, more):
        if f == 0:
            acc[...] = more
        elif f == 1:
            acc[...] += more
        else:
            total = (acc[...] + more).astype(BF)
            part[t, :, e * HALF : (e + 1) * HALF, :] = total.reshape(RING, HALF, D)

    def forward_piece(e, f):
        span = slice(f * COLS, (f + 1) * COLS)
        pre = jnp.dot(expert_rows(0, e), w_in[e, :, span], preferred_element_type=F32)
        half = 0.5 * (1.0 + lax.erf(pre * 0.7071067811865476))
        value = (pre * half).astype(BF)
        act[e, :, span] = value
        slope[e, :, span] = half + pre * jnp.exp(-0.5 * pre * pre) * 0.3989422804014327
        more = jnp.dot(value, w_out[e, span, :], preferred_element_type=F32)
        collect(0, e, f, more)

    def backward_piece(e, f):
        span = slice(f * COLS, (f + 1) * COLS)
        d_act = lax.dot_general(
            expert_rows(1, e), w_out[e, span, :], (((1,), (1,)), ((), ())), preferred_element_type=F32
        )
        value = (d_act * slope[e, :, span]).astype(BF)
        dpre[e, :, span] = value
        more = lax.dot_general(
            value, w_in[e, :, span], (((1,), (1,)), ((), ())), preferred_element_type=F32
        )
        collect(1, e, f, more)

    def weight_piece(e, f):
        span = slice(f * COLS, (f + 1) * COLS)
        g_out[e, span, :] = lax.dot_general(
            act[e, :, span], expert_rows(1, e), (((0,), (0,)), ((), ())), preferred_element_type=F32
        ).astype(BF)
        g_in[e, :, span] = lax.dot_general(
            expert_rows(0, e), dpre[e, :, span], (((0,), (0,)), ((), ())), preferred_element_type=F32
        ).astype(BF)

    def segment(n):
        def body(chains, table):
            for item in table[n]:
                chains.emit(*item)

        both(body)

    gather(0)
    for n, event in enumerate(EVENTS):
        segment(n)
        kind, which = event[0], event[1:]
        if kind == "gather":
            gather(1)
        elif kind in ("fwd", "bwd"):
            e, f = which
            q = e if kind == "fwd" else 2 + e
            if f == 0:
                both(lambda chains, table, q=q: chains.all_rows(q))
            if (q, f) == (0, 0):
                for copy in w_copies:
                    copy.wait()
            (forward_piece if kind == "fwd" else backward_piece)(e, f)
        elif kind == "wg":
            weight_piece(*which)
        else:
            out_last(which[0])
    segment(len(EVENTS))
    plane_arrived(prcv2.at[0], po_recv.at[0])
    prcv2[0, p] = psend[0, p]
    slot_out = prcv2[0].astype(F32).reshape(COLS, D).astype(BF)
    d_combine = across(out_grad[...], slot_out)
    mixed = comb[...] * d_combine
    d_log[...] = mixed - comb[...] * jnp.sum(mixed, axis=1, keepdims=True)
    plane_arrived(prcv2.at[1], po_recv.at[1])
    prcv2[1, p] = psend[1, p]
    slot_in_grad = prcv2[1].astype(F32).reshape(COLS, D).astype(BF)
    d_dispatch = across(tokens[...], slot_in_grad)
    mixed = disp[...] * d_dispatch
    d_logits = (d_log[...] + (mixed - disp[...] * jnp.sum(mixed, axis=0, keepdims=True))).astype(BF)
    rs[...] = rounded_slots(d_logits, tokens[...])
    plane_start(p, zhi, h, rs, rrcv, pr_send, pr_recv)
    token_grad[...] = (
        jnp.dot(disp[...].astype(BF), slot_in_grad, preferred_element_type=F32) + across(d_logits, rt[...])
    ).astype(BF)
    for t in (0, 1):
        plane_sent(prcv.at[t], ps_send.at[t])
        plane_sent(psend.at[t], po_send.at[t])
    both(lambda chains, table: chains.drain())
    plane_arrived(rrcv, pr_recv)
    rrcv[p] = rs[p]
    zs[...] = jnp.sum(rrcv[...].astype(F32), axis=0)
    zr[z] = zs[:, pl.ds(window(h), COLS)]

    def ring_copy(j, arrival):
        to = lax.rem(z + j, RING)
        slot = to if arrival else z
        return remote(
            zs.at[:, pl.ds(window(lax.rem(to, 4)), COLS)],
            zr.at[slot],
            rz_send.at[to],
            rz_recv.at[slot],
            ring_device(p, to),
        )

    for j in (4, 3, 5, 2, 6, 1, 7):
        ring_copy(j, False).start()
    for j in range(1, RING):
        ring_copy(j, True).wait_recv()
    total = jnp.sum(zr[...], axis=0)
    total = jnp.where(zhi == 0, total[:4], total[4:])
    router_out[...] = jnp.where(lax.rem(h, 2) == 0, total[:, :192], total[:, 64:])

    plane_sent(rrcv, pr_send)
    for j in range(1, RING):
        ring_copy(j, False).wait_send()


def rounded_slots(weights, values):
    sums = lax.dot_general(weights, values, (((0,), (0,)), ((), ())), preferred_element_type=F32)
    return sums.reshape(PLANE, 8, D).astype(BF)


def across(left, right):
    return lax.dot_general(left, right, (((1,), (1,)), ((), ())), preferred_element_type=F32)


def window(h):
    return pl.multiple_of((h + lax.div(h, 2)) * 128, 128)


def far(k):
    return min(k, 4 - k)


OFFSETS = sorted(
    ((dy, dx, dc) for dy in range(4) for dx in range(4) for dc in (0, 1) if (dy, dx, dc) != (0, 0, 0)),
    key=lambda o: (-far(o[0]) - far(o[1]), o[2], (o[0] + o[1]) % 2, o),
)


def plane_start(p, zhi, h, src, dst, send, recv):
    y, x, core = lax.div(p, 8), lax.rem(lax.div(p, 2), 4), lax.rem(p, 2)
    for dy, dx, dc in OFFSETS:
        to_y, to_x = lax.rem(y + dy, 4), lax.rem(x + dx, 4)
        to_core = 1 - core if dc else core
        q = to_y * 8 + to_x * 2 + to_core
        device = (to_y * 16 + zhi * 8 + to_x * 2 + to_core, h)
        remote(src.at[q], dst.at[p], send, recv, device).start()


def plane_arrived(dst, recv):
    many = dst.at[pl.ds(0, PLANE - 1)]
    pltpu.make_async_copy(many, many, recv).wait()


def plane_sent(src, send):
    many = src.at[pl.ds(0, PLANE - 1)]
    pltpu.make_async_copy(many, many, send).wait()


def layer(tokens, out_grad, slot_router, weight_in, weight_out):
    vmem = pl.BlockSpec(memory_space=pltpu.VMEM)
    dma = pltpu.SemaphoreType.DMA
    experts = weight_in.shape[0]
    width = weight_in.shape[2]
    return pl.pallas_call(
        exchange_kernel,
        out_shape=(
            pltpu.VMEM(tokens.shape, BF),
            pltpu.VMEM((4, 192), F32),
            pltpu.VMEM(weight_in.shape, BF),
            pltpu.VMEM(weight_out.shape, BF),
        ),
        in_specs=[pl.BlockSpec(memory_space=pltpu.HBM)] * 5,
        out_specs=(vmem,) * 4,
        scratch_shapes=[
            pltpu.VMEM(tokens.shape, BF),
            pltpu.VMEM(out_grad.shape, BF),
            pltpu.VMEM(slot_router.shape, BF),
            pltpu.VMEM(slot_router.shape, BF),
            pltpu.VMEM((TOK, COLS), F32),
            pltpu.VMEM((TOK, COLS), F32),
            pltpu.VMEM((TOK, COLS), F32),
            pltpu.VMEM((PLANE, 8, D), BF),
            pltpu.VMEM((PLANE, 8, D), BF),
            pltpu.VMEM((PLANE, 8, D), BF),
            pltpu.VMEM((PLANE, 8, D), BF),
            pltpu.VMEM((8, D), F32),
            pltpu.VMEM((RING, 8, COLS), F32),
            pltpu.VMEM((2, PLANE, 8, D), BF),
            pltpu.VMEM((LANES, COLS, 128), F32),
            pltpu.VMEM((2, RING, ROWS, D), BF),
            pltpu.VMEM((2, ROWS, D), BF),
            pltpu.VMEM((2, ROWS, D), BF),
            pltpu.VMEM((2, RING, ROWS, D), BF),
            pltpu.VMEM((2, RING + 1, ROWS, D), BF),
            pltpu.VMEM((2, ROWS, D), BF),
            pltpu.VMEM((2, ROWS, D), BF),
            pltpu.VMEM((2, PLANE, 8, D), BF),
            pltpu.VMEM((2, PLANE, 8, D), BF),
            pltpu.VMEM(weight_in.shape, BF),
            pltpu.VMEM(weight_out.shape, BF),
            pltpu.VMEM((experts, RING * HALF, width), BF),
            pltpu.VMEM((experts, RING * HALF, width), F32),
            pltpu.VMEM((experts, RING * HALF, width), BF),
            pltpu.VMEM((RING * HALF, D), F32),
            dma((3,)),
            dma((2,)),
            dma((2,)),
            dma((2,)),
            dma((2,)),
            dma((2,)),
            dma((COPIES,)),
            dma((4, RING)),
            dma((4,)),
            dma((4, RING + 1)),
            dma((4, 2)),
            dma(()),
            dma(()),
            dma((RING,)),
            dma((RING,)),
        ],
        compiler_params=pltpu.CompilerParams(
            collective_id=0, has_side_effects=True, vmem_limit_bytes=61900000
        ),
        name="layer",
    )(tokens, out_grad, slot_router, weight_in, weight_out)


def store_kernel(*refs):
    count = len(refs) // 2
    sems = refs[-1]
    copies = [
        pltpu.make_async_copy(refs[n], refs[count + n], sems.at[n]) for n in range(count)
    ]
    for copy in copies:
        copy.start()
    for copy in copies:
        copy.wait()


def store(*arrays):
    return pl.pallas_call(
        store_kernel,
        out_shape=tuple(jax.ShapeDtypeStruct(a.shape, a.dtype) for a in arrays),
        in_specs=[pl.BlockSpec(memory_space=pl.ANY)] * len(arrays),
        out_specs=(pl.BlockSpec(memory_space=pltpu.HBM),) * len(arrays),
        scratch_shapes=[pltpu.SemaphoreType.DMA((len(arrays),))],
        compiler_params=pltpu.CompilerParams(vmem_limit_bytes=1024 * 1024),
        name="store",
    )(*arrays)


def per_device(tokens, out_grad, slot_router, weight_in, weight_out):
    token_grad, router_grad, grad_first, grad_second = store(
        *layer(tokens, out_grad, slot_router, weight_in, weight_out)
    )
    return (token_grad, router_grad.T, grad_first, grad_second)


def solution(mesh):
    return jax.shard_map(
        per_device,
        mesh=mesh,
        in_specs=(
            P(("expert", "hidden"), None),
            P(("expert", "hidden"), None),
            P(),
            P("expert", None, "hidden"),
            P("expert", "hidden", None),
        ),
        out_specs=(
            P(("expert", "hidden"), None),
            P("hidden", "expert"),
            P("expert", None, "hidden"),
            P("expert", "hidden", None),
        ),
        check_vma=False,
    )
```

```python
import jax
import jax.numpy as jnp
from jax import lax
from jax.experimental import pallas as pl
from jax.experimental.pallas import tpu as pltpu
from jax.sharding import PartitionSpec as P

D = 768
TOK = 196
PLANE = 32
RING = 8
ROWS = 128
COLS = 256
HALF = 64
COPIES = 80
FIRST = 3
LANES = 6
MESH = pl.DeviceIdType.MESH
BF = jnp.bfloat16
F32 = jnp.float32


def place():
    expert = lax.axis_index("expert")
    h = lax.axis_index("hidden")
    p = lax.div(expert, 16) * 8 + lax.rem(expert, 8)
    zhi = lax.rem(lax.div(expert, 8), 2)
    return p, zhi, h


def plane_device(q, zhi, h):
    return (lax.div(q, 8) * 16 + zhi * 8 + lax.rem(q, 8), h)


def ring_device(p, z):
    return (lax.div(p, 8) * 16 + lax.div(z, 4) * 8 + lax.rem(p, 8), lax.rem(z, 4))


def met():
    pl.semaphore_wait(pltpu.get_barrier_semaphore(), PLANE + RING - 2)


def remote(src, dst, send, recv, device):
    return pltpu.make_async_remote_copy(
        src_ref=src, dst_ref=dst, send_sem=send, recv_sem=recv, device_id=device, device_id_type=MESH
    )


def greet(p, zhi, h, ring_offsets):
    barrier = pltpu.get_barrier_semaphore()
    z = zhi * 4 + h

    def one(j, carry):
        pl.semaphore_signal(
            barrier, inc=1, device_id=plane_device(lax.rem(p + j, PLANE), zhi, h), device_id_type=MESH
        )
        return carry

    lax.fori_loop(1, PLANE, one, 0)
    for offset in ring_offsets:
        pl.semaphore_signal(
            barrier, inc=1, device_id=ring_device(p, lax.rem(z + offset, RING)), device_id_type=MESH
        )


EVENTS = (
    ("gather",),
    ("fwd", 0, 0),
    ("fwd", 0, 1),
    ("fwd", 0, 2),
    ("fwd", 1, 0),
    ("fwd", 1, 1),
    ("fwd", 1, 2),
    ("bwd", 0, 0),
    ("bwd", 0, 1),
    ("bwd", 0, 2),
    ("wg", 0, 0),
    ("wg", 0, 1),
    ("wg", 0, 2),
    ("bwd", 1, 0),
    ("bwd", 1, 1),
    ("bwd", 1, 2),
    ("wg", 1, 0),
    ("wg", 1, 1),
    ("wg", 1, 2),
    ("last", 0),
    ("last", 1),
)
EDGE = (
    (("io", 0, "l", 0), ("io", 1, "l", 0), ("iO", 0, "h", 3), ("iO", 1, "h", 3), ("ix", 0, "h", 2), ("iX", 0, "l", 3), ("ix", 1, "h", 2), ("iX", 1, "l", 3), ("iX", 0, "l", 2)),
    (("iO", 2, "h", 3), ("io", 3, "l", 0), ("iX", 1, "l", 2), ("iO", 3, "h", 3), ("ix", 2, "h", 2), ("io", 2, "l", 0), ("iX", 2, "l", 3), ("iX", 2, "l", 2), ("iX", 3, "l", 3)),
    (),
    (),
    (("oX", 0, "h", 3), ("oo", 0, "h", 2), ("ix", 3, "h", 2), ("oX", 0, "h", 2), ("iX", 3, "l", 2), ("oo", 0, "h", 0)),
    (("oo", 0, "h", 1),),
    (),
    (("oX", 1, "h", 2), ("oo", 1, "h", 1), ("oo", 1, "h", 0), ("oX", 1, "h", 3)),
    (),
    (),
    (("oX", 2, "h", 3), ("oo", 2, "h", 0)),
    (("oX", 0, "l", 2), ("oX", 2, "h", 2)),
    (("oo", 1, "h", 2), ("oo", 2, "h", 1)),
    (("oT", 0, "h", 2),),
    (),
    (),
    (("oX", 3, "h", 2),),
    (("oX", 3, "h", 3), ("oX", 1, "l", 2), ("oo", 3, "h", 0)),
    (("oX", 1, "l", 3), ("oX", 0, "l", 3), ("oT", 1, "h", 2), ("oo", 2, "h", 2), ("oo", 3, "h", 2), ("oX", 2, "l", 2), ("oo", 3, "h", 1), ("oX", 2, "l", 3), ("oX", 3, "l", 2)),
    (("oT", 2, "h", 2), ("oX", 3, "l", 3), ("oT", 3, "h", 2)),
    (),
    (),
)
INNER = (
    (("iy", 0, "h", 2), ("iy", 1, "h", 2), ("io", 0, "l", 1), ("io", 0, "l", 0), ("io", 1, "h", 2), ("io", 0, "h", 2), ("io", 1, "l", 0), ("io", 1, "l", 1)),
    (("io", 0, "h", 1), ("iy", 2, "h", 2), ("iX", 0, "l", 3), ("io", 0, "h", 0), ("iX", 0, "l", 2), ("io", 3, "l", 1), ("iX", 0, "h", 3), ("io", 2, "l", 1), ("iX", 0, "h", 2)),
    (("iy", 3, "h", 2), ("iX", 1, "l", 2), ("iX", 1, "l", 3)),
    (("io", 2, "l", 0), ("io", 1, "h", 1), ("iX", 2, "l", 3)),
    (("iX", 1, "h", 2), ("iX", 2, "l", 2), ("io", 1, "h", 0), ("iX", 1, "h", 3), ("io", 2, "h", 2)),
    (("io", 3, "l", 0),),
    (("io", 2, "h", 1), ("oX", 0, "h", 3)),
    (("io", 2, "h", 0), ("iX", 2, "h", 3), ("iX", 3, "l", 2), ("oX", 0, "h", 2), ("oo", 0, "h", 0), ("iX", 3, "l", 3), ("iX", 2, "h", 2), ("io", 3, "h", 0), ("oX", 0, "l", 2)),
    (("oX", 1, "h", 2), ("oo", 0, "h", 1)),
    (("io", 3, "h", 1),),
    (("iX", 3, "h", 2), ("iX", 3, "h", 3)),
    (("oX", 1, "h", 3),),
    (("io", 3, "h", 2), ("oo", 1, "h", 0), ("oX", 2, "h", 3), ("oX", 1, "l", 2)),
    (("oX", 2, "h", 2), ("oX", 1, "l", 3)),
    (("oo", 2, "h", 0), ("oX", 0, "l", 3), ("oo", 2, "h", 1), ("oX", 2, "l", 2), ("oo", 1, "h", 1)),
    (),
    (),
    (("oX", 2, "l", 3), ("oX", 3, "h", 2)),
    (("oo", 0, "l", 0), ("oX", 3, "h", 3), ("oX", 3, "l", 2), ("oo", 3, "h", 0)),
    (("oX", 3, "l", 3), ("oo", 1, "l", 0)),
    (("oo", 3, "l", 0), ("oo", 2, "l", 0), ("oo", 3, "h", 1)),
    (),
)

class Chains:
    def __init__(self, edge, at, refs):
        self.lam = {"h": 3, "l": 0} if edge else {"h": 2, "l": 1}
        self.at = at
        self.refs = refs
        self.sent = 0
        self.seen = set()

    def zpos(self, d, j, own):
        up, zhi = self.at["up"], self.at["zhi"]
        towards = up if d == "h" else 1 - up
        return (zhi if own else 1 - zhi) * 4 + jnp.where(towards == 1, j, 3 - j)

    def last_slot(self, d):
        towards = self.at["up"] if d == "h" else 1 - self.at["up"]
        return jnp.where(towards == 1, self.at["z"], RING)

    def block(self, name, q, slot=None):
        t, e = q // 2, q % 2
        rows = pl.ds(e * HALF, HALF)
        ref = self.refs[name]
        return ref.at[t, rows] if slot is None else ref.at[t, slot, rows]

    def copy(self, src, dst, recv, device):
        remote(src, dst, self.refs["z_send"].at[self.sent], recv, device).start()
        self.sent += 1

    def drain(self):
        for n in range(self.sent):
            one = self.block("tout", 0)
            remote(one, one, self.refs["z_send"].at[n], self.refs["t_recv"].at[0], self.at["h"]).wait_send()

    def arrive(self, dst, recv):
        remote(dst, dst, self.refs["z_send"].at[0], recv, self.at["h"]).wait_recv()

    def arrive_rows(self, q, d, j, own):
        if (q, d, j, own) in self.seen:
            return
        self.seen.add((q, d, j, own))
        zs = self.zpos(d, j, own)
        self.arrive(self.block("rows", q, zs), self.refs["in_recv"].at[q, zs])

    def all_rows(self, q):
        for d in ("h", "l"):
            for j in range(self.lam[d] - 1, -1, -1):
                self.arrive_rows(q, d, j, True)
            for j in (3, 2):
                self.arrive_rows(q, d, j, False)

    def add(self, q, zs, slot):
        self.arrive(self.block("rr", q, slot), self.refs["out_recv"].at[q, slot])
        part, rr = self.block("part", q, zs), self.block("rr", q, slot)
        part[...] = (part[...].astype(F32) + rr[...].astype(F32)).astype(BF)

    def finish(self, q):
        for d in ("h", "l"):
            if self.lam[d] < 3:
                self.add(q, self.at["z"], self.last_slot(d))
        self.arrive(self.block("ofin", q), self.refs["ot_recv"].at[q, 1])

    def emit(self, code, q, d, j):
        lam = self.lam[d]
        other = "l" if d == "h" else "h"
        in_recv, out_recv = self.refs["in_recv"], self.refs["out_recv"]
        if code in ("io", "iX"):
            own = code == "io"
            zs = self.zpos(d, j, own)
            if not own or j < lam:
                self.arrive_rows(q, d, j, own)
            rows = self.block("rows", q, zs)
            self.copy(rows, rows, in_recv.at[q, zs], self.at[d])
        elif code == "iO":
            z = self.at["z"]
            self.copy(self.block("tout", q), self.block("rows", q, z), in_recv.at[q, z], self.at[d])
        elif code == "iy":
            self.copy(self.block("tout", q), self.block("ttr", q), self.refs["t_recv"].at[q], self.at[d])
        elif code == "ix":
            ttr = self.block("ttr", q)
            self.arrive(ttr, self.refs["t_recv"].at[q])
            zs = self.zpos(d, 2, True)
            self.copy(ttr, self.block("rows", q, zs), in_recv.at[q, zs], self.at[d])
        elif code in ("oo", "oX"):
            own = code == "oo"
            zs = self.zpos(d, j, own)
            if lam < 3:
                self.add(q, zs, zs)
            part = self.block("part", q, zs)
            if lam > 0:
                slot = self.last_slot_of(d, zs) if own and j == lam - 1 else zs
                self.copy(part, self.block("rr", q, slot), out_recv.at[q, slot], self.at[other])
            elif j == 2:
                self.copy(part, self.block("otr", q), self.refs["ot_recv"].at[q, 0], self.at[other])
            else:
                self.copy(part, self.block("ofin", q), self.refs["ot_recv"].at[q, 1], self.at[other])
        else:
            otr = self.block("otr", q)
            self.arrive(otr, self.refs["ot_recv"].at[q, 0])
            self.copy(otr, self.block("ofin", q), self.refs["ot_recv"].at[q, 1], self.at[other])

    def last_slot_of(self, d, zs):
        towards = self.at["up"] if d == "h" else 1 - self.at["up"]
        return jnp.where(towards == 1, zs, RING)


def exchange_kernel(
    tokens_in, out_grad_in, router_in, win, wout,
    token_grad, router_out, g_in, g_out,
    tokens, out_grad, router,
    rt, disp, comb, d_log, sa, sb, rs, rrcv, zs, zr,
    prcv, fs, rows, tout, ttr, part, rr, ofin, otr, psend, prcv2,
    w_in, w_out, act, slope, dpre, acc,
    a_sem, w_sem, ps_send, ps_recv, po_send, po_recv,
    z_send, in_recv, t_recv, out_recv, ot_recv,
    pr_send, pr_recv, rz_send, rz_recv,
):
    p, zhi, h = place()
    z = zhi * 4 + h
    up = jnp.where(h >= 2, 1, 0)
    step = 2 * up - 1
    at = {
        "z": z,
        "zhi": zhi,
        "up": up,
        "h": ring_device(p, lax.rem(z + step + RING, RING)),
        "l": ring_device(p, lax.rem(z - step + RING, RING)),
    }
    refs = {
        "rows": rows, "tout": tout, "ttr": ttr, "part": part, "rr": rr, "ofin": ofin, "otr": otr,
        "z_send": z_send, "in_recv": in_recv, "t_recv": t_recv, "out_recv": out_recv, "ot_recv": ot_recv,
    }
    edge, inner = Chains(True, at, refs), Chains(False, at, refs)
    at_edge = jnp.logical_or(h == 0, h == 3)

    def both(body):
        @pl.when(at_edge)
        def _():
            body(edge, EDGE)

        @pl.when(jnp.logical_not(at_edge))
        def _():
            body(inner, INNER)

    a_copies = [
        pltpu.make_async_copy(src, dst, a_sem.at[n])
        for n, (src, dst) in enumerate(
            ((router_in, router), (tokens_in, tokens), (out_grad_in, out_grad))
        )
    ]
    for copy in a_copies:
        copy.start()
    w_copies = [
        pltpu.make_async_copy(win, w_in, w_sem.at[0]),
        pltpu.make_async_copy(wout, w_out, w_sem.at[1]),
    ]
    for copy in w_copies:
        copy.start()
    greet(p, zhi, h, tuple(range(1, RING)))

    natural = lax.broadcasted_iota(jnp.int32, (COLS, COLS), 0)
    placed = lax.broadcasted_iota(jnp.int32, (COLS, COLS), 1)
    source = (placed & 192) + ((placed & 4) << 3) + ((placed & 56) >> 1) + (placed & 3)
    pick = jnp.where(natural == source, 1.0, 0.0).astype(BF)
    a_copies[0].wait()
    rt[...] = jnp.dot(router[...], pick, preferred_element_type=F32).astype(BF)
    a_copies[1].wait()
    logits = jnp.dot(tokens[...], rt[...], preferred_element_type=F32)
    above = jnp.exp(logits - jnp.max(logits, axis=0, keepdims=True))
    disp[...] = above / jnp.sum(above, axis=0, keepdims=True)
    sa[...] = rounded_slots(disp[...].astype(BF), tokens[...])
    met()
    sends = (sa, sb)
    plane_start(p, zhi, h, sa, prcv.at[0], ps_send.at[0], ps_recv.at[0])
    a_copies[2].wait()
    above = jnp.exp(logits - jnp.max(logits, axis=1, keepdims=True))
    comb[...] = above / jnp.sum(above, axis=1, keepdims=True)
    sb[...] = rounded_slots(comb[...].astype(BF), out_grad[...])

    def gather(t):
        plane_arrived(prcv.at[t], ps_recv.at[t])
        prcv[t, p] = sends[t][p]
        for c in range(LANES):
            lanes = slice(c * 128, (c + 1) * 128)
            fs[c] = prcv[t, :, :, lanes].astype(F32).reshape(COLS, 128)
            for s in range(4):
                piece = slice(s * PLANE, (s + 1) * PLANE)
                mine = fs[c, pl.ds(zhi * 4 + s, PLANE, stride=8), :]
                rows[t, z, piece, lanes] = mine.astype(BF)
                other = fs[c, pl.ds((1 - zhi) * 4 + s, PLANE, stride=8), :]
                tout[t, piece, lanes] = other.astype(BF)

    def out_last(t):
        for e in (0, 1):
            both(lambda chains, table, e=e: chains.finish(2 * t + e))
            for c in range(LANES):
                lanes = slice(c * 128, (c + 1) * 128)
                for s in (2 * e, 2 * e + 1):
                    piece = slice(s * PLANE, (s + 1) * PLANE)
                    fs[c, pl.ds(zhi * 4 + s, PLANE, stride=8), :] = part[t, z, piece, lanes].astype(F32)
                    fs[c, pl.ds((1 - zhi) * 4 + s, PLANE, stride=8), :] = ofin[t, piece, lanes].astype(F32)
        for c in range(LANES):
            psend[t, :, :, c * 128 : (c + 1) * 128] = fs[c].reshape(PLANE, 8, 128).astype(BF)
        plane_start(p, zhi, h, psend.at[t], prcv2.at[t], po_send.at[t], po_recv.at[t])


    def expert_rows(t, e):
        return rows[t, :, e * HALF : (e + 1) * HALF, :].reshape(RING * HALF, D)

    def collect(t, e, f, more):
        if f == 0:
            acc[...] = more
        elif f == 1:
            acc[...] += more
        else:
            total = (acc[...] + more).astype(BF)
            part[t, :, e * HALF : (e + 1) * HALF, :] = total.reshape(RING, HALF, D)

    def forward_piece(e, f):
        span = slice(f * COLS, (f + 1) * COLS)
        pre = jnp.dot(expert_rows(0, e), w_in[e, :, span], preferred_element_type=F32)
        half = 0.5 * (1.0 + lax.erf(pre * 0.7071067811865476))
        value = (pre * half).astype(BF)
        act[e, :, span] = value
        slope[e, :, span] = half + pre * jnp.exp(-0.5 * pre * pre) * 0.3989422804014327
        more = jnp.dot(value, w_out[e, span, :], preferred_element_type=F32)
        collect(0, e, f, more)

    def backward_piece(e, f):
        span = slice(f * COLS, (f + 1) * COLS)
        d_act = lax.dot_general(
            expert_rows(1, e), w_out[e, span, :], (((1,), (1,)), ((), ())), preferred_element_type=F32
        )
        value = (d_act * slope[e, :, span]).astype(BF)
        dpre[e, :, span] = value
        more = lax.dot_general(
            value, w_in[e, :, span], (((1,), (1,)), ((), ())), preferred_element_type=F32
        )
        collect(1, e, f, more)

    def weight_piece(e, f):
        span = slice(f * COLS, (f + 1) * COLS)
        g_out[e, span, :] = lax.dot_general(
            act[e, :, span], expert_rows(1, e), (((0,), (0,)), ((), ())), preferred_element_type=F32
        ).astype(BF)
        g_in[e, :, span] = lax.dot_general(
            expert_rows(0, e), dpre[e, :, span], (((0,), (0,)), ((), ())), preferred_element_type=F32
        ).astype(BF)

    def segment(n, span=slice(None)):
        def body(chains, table):
            for item in table[n][span]:
                chains.emit(*item)

        both(body)

    gather(0)
    for n, event in enumerate(EVENTS):
        if n == 0:
            segment(0, slice(0, FIRST))
            plane_start(p, zhi, h, sb, prcv.at[1], ps_send.at[1], ps_recv.at[1])
            segment(0, slice(FIRST, None))
        else:
            segment(n)
        kind, which = event[0], event[1:]
        if kind == "gather":
            gather(1)
        elif kind in ("fwd", "bwd"):
            e, f = which
            q = e if kind == "fwd" else 2 + e
            if f == 0:
                both(lambda chains, table, q=q: chains.all_rows(q))
            if (q, f) == (0, 0):
                for copy in w_copies:
                    copy.wait()
            (forward_piece if kind == "fwd" else backward_piece)(e, f)
        elif kind == "wg":
            weight_piece(*which)
        else:
            out_last(which[0])
    segment(len(EVENTS))
    plane_arrived(prcv2.at[0], po_recv.at[0])
    prcv2[0, p] = psend[0, p]
    slot_out = prcv2[0].astype(F32).reshape(COLS, D).astype(BF)
    d_combine = across(out_grad[...], slot_out)
    mixed = comb[...] * d_combine
    d_log[...] = mixed - comb[...] * jnp.sum(mixed, axis=1, keepdims=True)
    plane_arrived(prcv2.at[1], po_recv.at[1])
    prcv2[1, p] = psend[1, p]
    slot_in_grad = prcv2[1].astype(F32).reshape(COLS, D).astype(BF)
    d_dispatch = across(tokens[...], slot_in_grad)
    mixed = disp[...] * d_dispatch
    d_logits = (d_log[...] + (mixed - disp[...] * jnp.sum(mixed, axis=0, keepdims=True))).astype(BF)
    rs[...] = rounded_slots(d_logits, tokens[...])
    plane_start(p, zhi, h, rs, rrcv, pr_send, pr_recv)
    token_grad[...] = (
        jnp.dot(disp[...].astype(BF), slot_in_grad, preferred_element_type=F32) + across(d_logits, rt[...])
    ).astype(BF)
    for t in (0, 1):
        plane_sent(prcv.at[t], ps_send.at[t])
        plane_sent(psend.at[t], po_send.at[t])
    both(lambda chains, table: chains.drain())
    plane_arrived(rrcv, pr_recv)
    rrcv[p] = rs[p]
    zs[...] = jnp.sum(rrcv[...].astype(F32), axis=0)
    zr[z] = zs[:, pl.ds(window(h), COLS)]

    def ring_copy(j, arrival):
        to = lax.rem(z + j, RING)
        slot = to if arrival else z
        return remote(
            zs.at[:, pl.ds(window(lax.rem(to, 4)), COLS)],
            zr.at[slot],
            rz_send.at[to],
            rz_recv.at[slot],
            ring_device(p, to),
        )

    for j in (4, 3, 5, 2, 6, 1, 7):
        ring_copy(j, False).start()
    for j in range(1, RING):
        ring_copy(j, True).wait_recv()
    total = jnp.sum(zr[...], axis=0)
    total = jnp.where(zhi == 0, total[:4], total[4:])
    router_out[...] = jnp.where(lax.rem(h, 2) == 0, total[:, :192], total[:, 64:])

    plane_sent(rrcv, pr_send)
    for j in range(1, RING):
        ring_copy(j, False).wait_send()


def rounded_slots(weights, values):
    sums = lax.dot_general(weights, values, (((0,), (0,)), ((), ())), preferred_element_type=F32)
    return sums.reshape(PLANE, 8, D).astype(BF)


def across(left, right):
    return lax.dot_general(left, right, (((1,), (1,)), ((), ())), preferred_element_type=F32)


def window(h):
    return pl.multiple_of((h + lax.div(h, 2)) * 128, 128)


def far(k):
    return min(k, 4 - k)


OFFSETS = sorted(
    ((dy, dx, dc) for dy in range(4) for dx in range(4) for dc in (0, 1) if (dy, dx, dc) != (0, 0, 0)),
    key=lambda o: (-far(o[0]) - far(o[1]), o[2], (o[0] + o[1]) % 2, o),
)


def plane_start(p, zhi, h, src, dst, send, recv):
    y, x, core = lax.div(p, 8), lax.rem(lax.div(p, 2), 4), lax.rem(p, 2)
    for dy, dx, dc in OFFSETS:
        to_y, to_x = lax.rem(y + dy, 4), lax.rem(x + dx, 4)
        to_core = 1 - core if dc else core
        q = to_y * 8 + to_x * 2 + to_core
        device = (to_y * 16 + zhi * 8 + to_x * 2 + to_core, h)
        remote(src.at[q], dst.at[p], send, recv, device).start()


def plane_arrived(dst, recv):
    many = dst.at[pl.ds(0, PLANE - 1)]
    pltpu.make_async_copy(many, many, recv).wait()


def plane_sent(src, send):
    many = src.at[pl.ds(0, PLANE - 1)]
    pltpu.make_async_copy(many, many, send).wait()


def layer(tokens, out_grad, slot_router, weight_in, weight_out):
    vmem = pl.BlockSpec(memory_space=pltpu.VMEM)
    dma = pltpu.SemaphoreType.DMA
    experts = weight_in.shape[0]
    width = weight_in.shape[2]
    return pl.pallas_call(
        exchange_kernel,
        out_shape=(
            pltpu.VMEM(tokens.shape, BF),
            pltpu.VMEM((4, 192), F32),
            pltpu.VMEM(weight_in.shape, BF),
            pltpu.VMEM(weight_out.shape, BF),
        ),
        in_specs=[pl.BlockSpec(memory_space=pltpu.HBM)] * 5,
        out_specs=(vmem,) * 4,
        scratch_shapes=[
            pltpu.VMEM(tokens.shape, BF),
            pltpu.VMEM(out_grad.shape, BF),
            pltpu.VMEM(slot_router.shape, BF),
            pltpu.VMEM(slot_router.shape, BF),
            pltpu.VMEM((TOK, COLS), F32),
            pltpu.VMEM((TOK, COLS), F32),
            pltpu.VMEM((TOK, COLS), F32),
            pltpu.VMEM((PLANE, 8, D), BF),
            pltpu.VMEM((PLANE, 8, D), BF),
            pltpu.VMEM((PLANE, 8, D), BF),
            pltpu.VMEM((PLANE, 8, D), BF),
            pltpu.VMEM((8, D), F32),
            pltpu.VMEM((RING, 8, COLS), F32),
            pltpu.VMEM((2, PLANE, 8, D), BF),
            pltpu.VMEM((LANES, COLS, 128), F32),
            pltpu.VMEM((2, RING, ROWS, D), BF),
            pltpu.VMEM((2, ROWS, D), BF),
            pltpu.VMEM((2, ROWS, D), BF),
            pltpu.VMEM((2, RING, ROWS, D), BF),
            pltpu.VMEM((2, RING + 1, ROWS, D), BF),
            pltpu.VMEM((2, ROWS, D), BF),
            pltpu.VMEM((2, ROWS, D), BF),
            pltpu.VMEM((2, PLANE, 8, D), BF),
            pltpu.VMEM((2, PLANE, 8, D), BF),
            pltpu.VMEM(weight_in.shape, BF),
            pltpu.VMEM(weight_out.shape, BF),
            pltpu.VMEM((experts, RING * HALF, width), BF),
            pltpu.VMEM((experts, RING * HALF, width), F32),
            pltpu.VMEM((experts, RING * HALF, width), BF),
            pltpu.VMEM((RING * HALF, D), F32),
            dma((3,)),
            dma((2,)),
            dma((2,)),
            dma((2,)),
            dma((2,)),
            dma((2,)),
            dma((COPIES,)),
            dma((4, RING)),
            dma((4,)),
            dma((4, RING + 1)),
            dma((4, 2)),
            dma(()),
            dma(()),
            dma((RING,)),
            dma((RING,)),
        ],
        compiler_params=pltpu.CompilerParams(
            collective_id=0, has_side_effects=True, vmem_limit_bytes=61900000
        ),
        name="layer",
    )(tokens, out_grad, slot_router, weight_in, weight_out)


def store_kernel(*refs):
    count = len(refs) // 2
    sems = refs[-1]
    copies = [
        pltpu.make_async_copy(refs[n], refs[count + n], sems.at[n]) for n in range(count)
    ]
    for copy in copies:
        copy.start()
    for copy in copies:
        copy.wait()


def store(*arrays):
    return pl.pallas_call(
        store_kernel,
        out_shape=tuple(jax.ShapeDtypeStruct(a.shape, a.dtype) for a in arrays),
        in_specs=[pl.BlockSpec(memory_space=pl.ANY)] * len(arrays),
        out_specs=(pl.BlockSpec(memory_space=pltpu.HBM),) * len(arrays),
        scratch_shapes=[pltpu.SemaphoreType.DMA((len(arrays),))],
        compiler_params=pltpu.CompilerParams(vmem_limit_bytes=1024 * 1024),
        name="store",
    )(*arrays)


def per_device(tokens, out_grad, slot_router, weight_in, weight_out):
    token_grad, router_grad, grad_first, grad_second = store(
        *layer(tokens, out_grad, slot_router, weight_in, weight_out)
    )
    return (token_grad, router_grad.T, grad_first, grad_second)


def solution(mesh):
    return jax.shard_map(
        per_device,
        mesh=mesh,
        in_specs=(
            P(("expert", "hidden"), None),
            P(("expert", "hidden"), None),
            P(),
            P("expert", None, "hidden"),
            P("expert", "hidden", None),
        ),
        out_specs=(
            P(("expert", "hidden"), None),
            P("hidden", "expert"),
            P("expert", None, "hidden"),
            P("expert", "hidden", None),
        ),
        check_vma=False,
    )
```

```python
import jax
import jax.numpy as jnp
from jax import lax
from jax.experimental import pallas as pl
from jax.experimental.pallas import tpu as pltpu
from jax.sharding import PartitionSpec as P

D = 768
TOK = 196
PLANE = 32
RING = 8
ROWS = 128
COLS = 256
HALF = 64
COPIES = 80
FIRST = 3
LANES = 6
MESH = pl.DeviceIdType.MESH
BF = jnp.bfloat16
F32 = jnp.float32


def place():
    expert = lax.axis_index("expert")
    h = lax.axis_index("hidden")
    p = lax.div(expert, 16) * 8 + lax.rem(expert, 8)
    zhi = lax.rem(lax.div(expert, 8), 2)
    return p, zhi, h


def plane_device(q, zhi, h):
    return (lax.div(q, 8) * 16 + zhi * 8 + lax.rem(q, 8), h)


def ring_device(p, z):
    return (lax.div(p, 8) * 16 + lax.div(z, 4) * 8 + lax.rem(p, 8), lax.rem(z, 4))


def met():
    pl.semaphore_wait(pltpu.get_barrier_semaphore(), PLANE + RING - 2)


def remote(src, dst, send, recv, device):
    return pltpu.make_async_remote_copy(
        src_ref=src, dst_ref=dst, send_sem=send, recv_sem=recv, device_id=device, device_id_type=MESH
    )


def greet(p, zhi, h, ring_offsets):
    barrier = pltpu.get_barrier_semaphore()
    z = zhi * 4 + h

    def one(j, carry):
        pl.semaphore_signal(
            barrier, inc=1, device_id=plane_device(lax.rem(p + j, PLANE), zhi, h), device_id_type=MESH
        )
        return carry

    lax.fori_loop(1, PLANE, one, 0)
    for offset in ring_offsets:
        pl.semaphore_signal(
            barrier, inc=1, device_id=ring_device(p, lax.rem(z + offset, RING)), device_id_type=MESH
        )


EVENTS = (
    ("gather",),
    ("fwd", 0, 0),
    ("fwd", 0, 1),
    ("fwd", 0, 2),
    ("fwd", 1, 0),
    ("fwd", 1, 1),
    ("fwd", 1, 2),
    ("bwd", 0, 0),
    ("bwd", 0, 1),
    ("bwd", 0, 2),
    ("wg", 0, 0),
    ("wg", 0, 1),
    ("wg", 0, 2),
    ("bwd", 1, 0),
    ("bwd", 1, 1),
    ("bwd", 1, 2),
    ("wg", 1, 0),
    ("wg", 1, 1),
    ("wg", 1, 2),
    ("last", 0),
    ("last", 1),
)
EDGE = (
    (("io", 0, "l", 0), ("iO", 0, "h", 3), ("iO", 1, "h", 3), ("io", 1, "l", 0), ("ix", 0, "h", 2), ("iX", 0, "l", 3), ("iX", 1, "l", 3), ("iX", 0, "l", 2), ("ix", 1, "h", 2)),
    (("io", 2, "l", 0), ("iO", 2, "h", 3), ("iO", 3, "h", 3), ("iX", 1, "l", 2), ("iX", 2, "l", 3), ("ix", 2, "h", 2), ("iX", 3, "l", 3), ("iX", 2, "l", 2), ("io", 3, "l", 0)),
    (),
    (),
    (("oX", 0, "h", 2), ("ix", 3, "h", 2), ("oX", 0, "h", 3), ("oo", 0, "h", 1), ("oo", 0, "h", 0), ("iX", 3, "l", 2)),
    (),
    (),
    (("oo", 0, "h", 2), ("oX", 1, "h", 3), ("oX", 1, "h", 2), ("oo", 1, "h", 2), ("oo", 1, "h", 1)),
    (),
    (),
    (("oX", 2, "h", 2), ("oX", 2, "h", 3), ("oo", 1, "h", 0)),
    (),
    (("oo", 2, "h", 0),),
    (("oo", 2, "h", 1),),
    (),
    (),
    (("oX", 3, "h", 2), ("oX", 3, "h", 3), ("oX", 0, "l", 2), ("oo", 3, "h", 0), ("oX", 1, "l", 2), ("oX", 0, "l", 3), ("oT", 0, "h", 2), ("oT", 1, "h", 2), ("oo", 3, "h", 1)),
    (("oo", 3, "h", 2), ("oX", 1, "l", 3)),
    (("oo", 2, "h", 2), ("oX", 2, "l", 2), ("oX", 2, "l", 3), ("oX", 3, "l", 2)),
    (("oT", 2, "h", 2), ("oX", 3, "l", 3), ("oT", 3, "h", 2)),
    (),
    (),
)
INNER = (
    (("iy", 0, "h", 2), ("io", 1, "l", 1), ("io", 0, "h", 2), ("iy", 1, "h", 2), ("io", 0, "l", 0), ("io", 0, "l", 1), ("io", 1, "h", 2), ("io", 0, "h", 0)),
    (("iX", 0, "l", 3), ("iy", 2, "h", 2), ("io", 0, "h", 1), ("iX", 0, "l", 2), ("iX", 0, "h", 3), ("io", 2, "l", 0), ("iX", 0, "h", 2), ("iX", 1, "l", 3), ("io", 1, "h", 1), ("iy", 3, "h", 2), ("iX", 1, "l", 2), ("io", 1, "l", 0), ("iX", 1, "h", 3), ("iX", 2, "l", 2), ("iX", 3, "l", 3), ("iX", 1, "h", 2), ("io", 1, "h", 0), ("iX", 2, "l", 3), ("io", 2, "l", 1)),
    (),
    (("iX", 2, "h", 2), ("io", 2, "h", 2), ("io", 3, "l", 1)),
    (("io", 2, "h", 0),),
    (("io", 2, "h", 1), ("iX", 2, "h", 3), ("io", 3, "l", 0)),
    (("oX", 0, "h", 3), ("io", 3, "h", 2), ("oo", 0, "h", 0), ("oX", 0, "h", 2), ("io", 3, "h", 1)),
    (("iX", 3, "l", 2),),
    (("iX", 3, "h", 3),),
    (("oX", 1, "h", 3),),
    (),
    (("oX", 1, "h", 2),),
    (),
    (("io", 3, "h", 0),),
    (("iX", 3, "h", 2), ("oX", 0, "l", 2), ("oo", 1, "h", 1), ("oX", 1, "l", 2), ("oX", 2, "h", 2)),
    (("oX", 0, "l", 3), ("oo", 0, "l", 0), ("oo", 0, "h", 1), ("oX", 2, "h", 3)),
    (("oo", 1, "h", 0), ("oX", 1, "l", 3), ("oX", 3, "h", 2), ("oX", 2, "l", 2), ("oX", 2, "l", 3)),
    (("oX", 3, "h", 3),),
    (("oo", 2, "h", 1),),
    (("oo", 2, "h", 0), ("oX", 3, "l", 2), ("oo", 3, "h", 0), ("oX", 3, "l", 3), ("oo", 1, "l", 0)),
    (("oo", 2, "l", 0), ("oo", 3, "l", 0), ("oo", 3, "h", 1)),
    (),
)

class Chains:
    def __init__(self, edge, at, refs):
        self.lam = {"h": 3, "l": 0} if edge else {"h": 2, "l": 1}
        self.at = at
        self.refs = refs
        self.sent = 0
        self.seen = set()

    def zpos(self, d, j, own):
        up, zhi = self.at["up"], self.at["zhi"]
        towards = up if d == "h" else 1 - up
        return (zhi if own else 1 - zhi) * 4 + jnp.where(towards == 1, j, 3 - j)

    def last_slot(self, d):
        towards = self.at["up"] if d == "h" else 1 - self.at["up"]
        return jnp.where(towards == 1, self.at["z"], RING)

    def block(self, name, q, slot=None):
        t, e = q // 2, q % 2
        rows = pl.ds(e * HALF, HALF)
        ref = self.refs[name]
        return ref.at[t, rows] if slot is None else ref.at[t, slot, rows]

    def copy(self, src, dst, recv, device):
        remote(src, dst, self.refs["z_send"].at[self.sent], recv, device).start()
        self.sent += 1

    def drain(self):
        for n in range(self.sent):
            one = self.block("tout", 0)
            remote(one, one, self.refs["z_send"].at[n], self.refs["t_recv"].at[0], self.at["h"]).wait_send()

    def arrive(self, dst, recv):
        remote(dst, dst, self.refs["z_send"].at[0], recv, self.at["h"]).wait_recv()

    def arrive_rows(self, q, d, j, own):
        if (q, d, j, own) in self.seen:
            return
        self.seen.add((q, d, j, own))
        zs = self.zpos(d, j, own)
        self.arrive(self.block("rows", q, zs), self.refs["in_recv"].at[q, zs])

    def all_rows(self, q):
        for d in ("h", "l"):
            for j in range(self.lam[d] - 1, -1, -1):
                self.arrive_rows(q, d, j, True)
            for j in (3, 2):
                self.arrive_rows(q, d, j, False)

    def add(self, q, zs, slot):
        self.arrive(self.block("rr", q, slot), self.refs["out_recv"].at[q, slot])
        part, rr = self.block("part", q, zs), self.block("rr", q, slot)
        part[...] = (part[...].astype(F32) + rr[...].astype(F32)).astype(BF)

    def finish(self, q):
        for d in ("h", "l"):
            if self.lam[d] < 3:
                self.add(q, self.at["z"], self.last_slot(d))
        self.arrive(self.block("ofin", q), self.refs["ot_recv"].at[q, 1])

    def emit(self, code, q, d, j):
        lam = self.lam[d]
        other = "l" if d == "h" else "h"
        in_recv, out_recv = self.refs["in_recv"], self.refs["out_recv"]
        if code in ("io", "iX"):
            own = code == "io"
            zs = self.zpos(d, j, own)
            if not own or j < lam:
                self.arrive_rows(q, d, j, own)
            rows = self.block("rows", q, zs)
            self.copy(rows, rows, in_recv.at[q, zs], self.at[d])
        elif code == "iO":
            z = self.at["z"]
            self.copy(self.block("tout", q), self.block("rows", q, z), in_recv.at[q, z], self.at[d])
        elif code == "iy":
            self.copy(self.block("tout", q), self.block("ttr", q), self.refs["t_recv"].at[q], self.at[d])
        elif code == "ix":
            ttr = self.block("ttr", q)
            self.arrive(ttr, self.refs["t_recv"].at[q])
            zs = self.zpos(d, 2, True)
            self.copy(ttr, self.block("rows", q, zs), in_recv.at[q, zs], self.at[d])
        elif code in ("oo", "oX"):
            own = code == "oo"
            zs = self.zpos(d, j, own)
            if lam < 3:
                self.add(q, zs, zs)
            part = self.block("part", q, zs)
            if lam > 0:
                slot = self.last_slot_of(d, zs) if own and j == lam - 1 else zs
                self.copy(part, self.block("rr", q, slot), out_recv.at[q, slot], self.at[other])
            elif j == 2:
                self.copy(part, self.block("otr", q), self.refs["ot_recv"].at[q, 0], self.at[other])
            else:
                self.copy(part, self.block("ofin", q), self.refs["ot_recv"].at[q, 1], self.at[other])
        else:
            otr = self.block("otr", q)
            self.arrive(otr, self.refs["ot_recv"].at[q, 0])
            self.copy(otr, self.block("ofin", q), self.refs["ot_recv"].at[q, 1], self.at[other])

    def last_slot_of(self, d, zs):
        towards = self.at["up"] if d == "h" else 1 - self.at["up"]
        return jnp.where(towards == 1, zs, RING)


def exchange_kernel(
    tokens_in, out_grad_in, router_in, win, wout,
    token_grad, router_out, g_in, g_out,
    tokens, out_grad, router,
    rt, disp, comb, d_log, sa, sb, rs, rrcv, zs, zr,
    prcv, fs, rows, tout, ttr, part, rr, ofin, otr, psend, prcv2,
    w_in, w_out, act, slope, dpre, acc,
    a_sem, w_sem, ps_send, ps_recv, po_send, po_recv,
    z_send, in_recv, t_recv, out_recv, ot_recv,
    pr_send, pr_recv, rz_send, rz_recv,
):
    p, zhi, h = place()
    z = zhi * 4 + h
    up = jnp.where(h >= 2, 1, 0)
    step = 2 * up - 1
    at = {
        "z": z,
        "zhi": zhi,
        "up": up,
        "h": ring_device(p, lax.rem(z + step + RING, RING)),
        "l": ring_device(p, lax.rem(z - step + RING, RING)),
    }
    refs = {
        "rows": rows, "tout": tout, "ttr": ttr, "part": part, "rr": rr, "ofin": ofin, "otr": otr,
        "z_send": z_send, "in_recv": in_recv, "t_recv": t_recv, "out_recv": out_recv, "ot_recv": ot_recv,
    }
    edge, inner = Chains(True, at, refs), Chains(False, at, refs)
    at_edge = jnp.logical_or(h == 0, h == 3)

    def both(body):
        @pl.when(at_edge)
        def _():
            body(edge, EDGE)

        @pl.when(jnp.logical_not(at_edge))
        def _():
            body(inner, INNER)

    a_copies = [
        pltpu.make_async_copy(src, dst, a_sem.at[n])
        for n, (src, dst) in enumerate(
            ((router_in, router), (tokens_in, tokens), (out_grad_in, out_grad))
        )
    ]
    for copy in a_copies:
        copy.start()
    w_copies = [
        pltpu.make_async_copy(win, w_in, w_sem.at[0]),
        pltpu.make_async_copy(wout, w_out, w_sem.at[1]),
    ]
    for copy in w_copies:
        copy.start()
    greet(p, zhi, h, tuple(range(1, RING)))

    natural = lax.broadcasted_iota(jnp.int32, (COLS, COLS), 0)
    placed = lax.broadcasted_iota(jnp.int32, (COLS, COLS), 1)
    source = (placed & 192) + ((placed & 4) << 3) + ((placed & 56) >> 1) + (placed & 3)
    pick = jnp.where(natural == source, 1.0, 0.0).astype(BF)
    a_copies[0].wait()
    rt[...] = jnp.dot(router[...], pick, preferred_element_type=F32).astype(BF)
    a_copies[1].wait()
    logits = jnp.dot(tokens[...], rt[...], preferred_element_type=F32)
    above = jnp.exp(logits - jnp.max(logits, axis=0, keepdims=True))
    disp[...] = above / jnp.sum(above, axis=0, keepdims=True)
    sa[...] = rounded_slots(disp[...].astype(BF), tokens[...])
    met()
    sends = (sa, sb)
    plane_start(p, zhi, h, sa, prcv.at[0], ps_send.at[0], ps_recv.at[0])
    a_copies[2].wait()
    above = jnp.exp(logits - jnp.max(logits, axis=1, keepdims=True))
    comb[...] = above / jnp.sum(above, axis=1, keepdims=True)
    sb[...] = rounded_slots(comb[...].astype(BF), out_grad[...])

    def gather(t):
        plane_arrived(prcv.at[t], ps_recv.at[t])
        prcv[t, p] = sends[t][p]
        for c in range(LANES):
            lanes = slice(c * 128, (c + 1) * 128)
            fs[c] = prcv[t, :, :, lanes].astype(F32).reshape(COLS, 128)
            for s in range(4):
                piece = slice(s * PLANE, (s + 1) * PLANE)
                mine = fs[c, pl.ds(zhi * 4 + s, PLANE, stride=8), :]
                rows[t, z, piece, lanes] = mine.astype(BF)
                other = fs[c, pl.ds((1 - zhi) * 4 + s, PLANE, stride=8), :]
                tout[t, piece, lanes] = other.astype(BF)

    def out_last(t):
        for e in (0, 1):
            both(lambda chains, table, e=e: chains.finish(2 * t + e))
            for c in range(LANES):
                lanes = slice(c * 128, (c + 1) * 128)
                for s in (2 * e, 2 * e + 1):
                    piece = slice(s * PLANE, (s + 1) * PLANE)
                    fs[c, pl.ds(zhi * 4 + s, PLANE, stride=8), :] = part[t, z, piece, lanes].astype(F32)
                    fs[c, pl.ds((1 - zhi) * 4 + s, PLANE, stride=8), :] = ofin[t, piece, lanes].astype(F32)
        for c in range(LANES):
            psend[t, :, :, c * 128 : (c + 1) * 128] = fs[c].reshape(PLANE, 8, 128).astype(BF)
        plane_start(p, zhi, h, psend.at[t], prcv2.at[t], po_send.at[t], po_recv.at[t])


    def expert_rows(t, e):
        return rows[t, :, e * HALF : (e + 1) * HALF, :].reshape(RING * HALF, D)

    def collect(t, e, f, more):
        if f == 0:
            acc[...] = more
        elif f == 1:
            acc[...] += more
        else:
            total = (acc[...] + more).astype(BF)
            part[t, :, e * HALF : (e + 1) * HALF, :] = total.reshape(RING, HALF, D)

    def forward_piece(e, f):
        span = slice(f * COLS, (f + 1) * COLS)
        pre = jnp.dot(expert_rows(0, e), w_in[e, :, span], preferred_element_type=F32)
        half = 0.5 * (1.0 + lax.erf(pre * 0.7071067811865476))
        value = (pre * half).astype(BF)
        act[e, :, span] = value
        slope[e, :, span] = half + pre * jnp.exp(-0.5 * pre * pre) * 0.3989422804014327
        more = jnp.dot(value, w_out[e, span, :], preferred_element_type=F32)
        collect(0, e, f, more)

    def backward_piece(e, f):
        span = slice(f * COLS, (f + 1) * COLS)
        d_act = lax.dot_general(
            expert_rows(1, e), w_out[e, span, :], (((1,), (1,)), ((), ())), preferred_element_type=F32
        )
        value = (d_act * slope[e, :, span]).astype(BF)
        dpre[e, :, span] = value
        more = lax.dot_general(
            value, w_in[e, :, span], (((1,), (1,)), ((), ())), preferred_element_type=F32
        )
        collect(1, e, f, more)

    def weight_piece(e, f):
        span = slice(f * COLS, (f + 1) * COLS)
        g_out[e, span, :] = lax.dot_general(
            act[e, :, span], expert_rows(1, e), (((0,), (0,)), ((), ())), preferred_element_type=F32
        ).astype(BF)
        g_in[e, :, span] = lax.dot_general(
            expert_rows(0, e), dpre[e, :, span], (((0,), (0,)), ((), ())), preferred_element_type=F32
        ).astype(BF)

    def segment(n, span=slice(None)):
        def body(chains, table):
            for item in table[n][span]:
                chains.emit(*item)

        both(body)

    gather(0)
    for n, event in enumerate(EVENTS):
        if n == 0:
            segment(0, slice(0, FIRST))
            plane_start(p, zhi, h, sb, prcv.at[1], ps_send.at[1], ps_recv.at[1])
            segment(0, slice(FIRST, None))
        else:
            segment(n)
        kind, which = event[0], event[1:]
        if kind == "gather":
            gather(1)
        elif kind in ("fwd", "bwd"):
            e, f = which
            q = e if kind == "fwd" else 2 + e
            if f == 0:
                both(lambda chains, table, q=q: chains.all_rows(q))
            if (q, f) == (0, 0):
                for copy in w_copies:
                    copy.wait()
            (forward_piece if kind == "fwd" else backward_piece)(e, f)
        elif kind == "wg":
            weight_piece(*which)
        else:
            out_last(which[0])
    segment(len(EVENTS))
    plane_arrived(prcv2.at[0], po_recv.at[0])
    prcv2[0, p] = psend[0, p]
    slot_out = prcv2[0].astype(F32).reshape(COLS, D).astype(BF)
    d_combine = across(out_grad[...], slot_out)
    mixed = comb[...] * d_combine
    d_log[...] = mixed - comb[...] * jnp.sum(mixed, axis=1, keepdims=True)
    plane_arrived(prcv2.at[1], po_recv.at[1])
    prcv2[1, p] = psend[1, p]
    slot_in_grad = prcv2[1].astype(F32).reshape(COLS, D).astype(BF)
    d_dispatch = across(tokens[...], slot_in_grad)
    mixed = disp[...] * d_dispatch
    d_logits = (d_log[...] + (mixed - disp[...] * jnp.sum(mixed, axis=0, keepdims=True))).astype(BF)
    rs[...] = rounded_slots(d_logits, tokens[...])
    plane_start(p, zhi, h, rs, rrcv, pr_send, pr_recv)
    token_grad[...] = (
        jnp.dot(disp[...].astype(BF), slot_in_grad, preferred_element_type=F32) + across(d_logits, rt[...])
    ).astype(BF)
    for t in (0, 1):
        plane_sent(prcv.at[t], ps_send.at[t])
        plane_sent(psend.at[t], po_send.at[t])
    both(lambda chains, table: chains.drain())
    plane_arrived(rrcv, pr_recv)
    rrcv[p] = rs[p]
    zs[...] = jnp.sum(rrcv[...].astype(F32), axis=0)
    zr[z] = zs[:, pl.ds(window(h), COLS)]

    def ring_copy(j, arrival):
        to = lax.rem(z + j, RING)
        slot = to if arrival else z
        return remote(
            zs.at[:, pl.ds(window(lax.rem(to, 4)), COLS)],
            zr.at[slot],
            rz_send.at[to],
            rz_recv.at[slot],
            ring_device(p, to),
        )

    for j in (4, 3, 5, 2, 6, 1, 7):
        ring_copy(j, False).start()
    for j in range(1, RING):
        ring_copy(j, True).wait_recv()
    total = jnp.sum(zr[...], axis=0)
    total = jnp.where(zhi == 0, total[:4], total[4:])
    router_out[...] = jnp.where(lax.rem(h, 2) == 0, total[:, :192], total[:, 64:])

    plane_sent(rrcv, pr_send)
    for j in range(1, RING):
        ring_copy(j, False).wait_send()


def rounded_slots(weights, values):
    sums = lax.dot_general(weights, values, (((0,), (0,)), ((), ())), preferred_element_type=F32)
    return sums.reshape(PLANE, 8, D).astype(BF)


def across(left, right):
    return lax.dot_general(left, right, (((1,), (1,)), ((), ())), preferred_element_type=F32)


def window(h):
    return pl.multiple_of((h + lax.div(h, 2)) * 128, 128)


def far(k):
    return min(k, 4 - k)


OFFSETS = sorted(
    ((dy, dx, dc) for dy in range(4) for dx in range(4) for dc in (0, 1) if (dy, dx, dc) != (0, 0, 0)),
    key=lambda o: (-far(o[0]) - far(o[1]), o[2], (o[0] + o[1]) % 2, o),
)


def plane_start(p, zhi, h, src, dst, send, recv):
    y, x, core = lax.div(p, 8), lax.rem(lax.div(p, 2), 4), lax.rem(p, 2)
    for dy, dx, dc in OFFSETS:
        to_y, to_x = lax.rem(y + dy, 4), lax.rem(x + dx, 4)
        to_core = 1 - core if dc else core
        q = to_y * 8 + to_x * 2 + to_core
        device = (to_y * 16 + zhi * 8 + to_x * 2 + to_core, h)
        remote(src.at[q], dst.at[p], send, recv, device).start()


def plane_arrived(dst, recv):
    many = dst.at[pl.ds(0, PLANE - 1)]
    pltpu.make_async_copy(many, many, recv).wait()


def plane_sent(src, send):
    many = src.at[pl.ds(0, PLANE - 1)]
    pltpu.make_async_copy(many, many, send).wait()


def layer(tokens, out_grad, slot_router, weight_in, weight_out):
    vmem = pl.BlockSpec(memory_space=pltpu.VMEM)
    dma = pltpu.SemaphoreType.DMA
    experts = weight_in.shape[0]
    width = weight_in.shape[2]
    return pl.pallas_call(
        exchange_kernel,
        out_shape=(
            pltpu.VMEM(tokens.shape, BF),
            pltpu.VMEM((4, 192), F32),
            pltpu.VMEM(weight_in.shape, BF),
            pltpu.VMEM(weight_out.shape, BF),
        ),
        in_specs=[pl.BlockSpec(memory_space=pltpu.HBM)] * 5,
        out_specs=(vmem,) * 4,
        scratch_shapes=[
            pltpu.VMEM(tokens.shape, BF),
            pltpu.VMEM(out_grad.shape, BF),
            pltpu.VMEM(slot_router.shape, BF),
            pltpu.VMEM(slot_router.shape, BF),
            pltpu.VMEM((TOK, COLS), F32),
            pltpu.VMEM((TOK, COLS), F32),
            pltpu.VMEM((TOK, COLS), F32),
            pltpu.VMEM((PLANE, 8, D), BF),
            pltpu.VMEM((PLANE, 8, D), BF),
            pltpu.VMEM((PLANE, 8, D), BF),
            pltpu.VMEM((PLANE, 8, D), BF),
            pltpu.VMEM((8, D), F32),
            pltpu.VMEM((RING, 8, COLS), F32),
            pltpu.VMEM((2, PLANE, 8, D), BF),
            pltpu.VMEM((LANES, COLS, 128), F32),
            pltpu.VMEM((2, RING, ROWS, D), BF),
            pltpu.VMEM((2, ROWS, D), BF),
            pltpu.VMEM((2, ROWS, D), BF),
            pltpu.VMEM((2, RING, ROWS, D), BF),
            pltpu.VMEM((2, RING + 1, ROWS, D), BF),
            pltpu.VMEM((2, ROWS, D), BF),
            pltpu.VMEM((2, ROWS, D), BF),
            pltpu.VMEM((2, PLANE, 8, D), BF),
            pltpu.VMEM((2, PLANE, 8, D), BF),
            pltpu.VMEM(weight_in.shape, BF),
            pltpu.VMEM(weight_out.shape, BF),
            pltpu.VMEM((experts, RING * HALF, width), BF),
            pltpu.VMEM((experts, RING * HALF, width), F32),
            pltpu.VMEM((experts, RING * HALF, width), BF),
            pltpu.VMEM((RING * HALF, D), F32),
            dma((3,)),
            dma((2,)),
            dma((2,)),
            dma((2,)),
            dma((2,)),
            dma((2,)),
            dma((COPIES,)),
            dma((4, RING)),
            dma((4,)),
            dma((4, RING + 1)),
            dma((4, 2)),
            dma(()),
            dma(()),
            dma((RING,)),
            dma((RING,)),
        ],
        compiler_params=pltpu.CompilerParams(
            collective_id=0, has_side_effects=True, vmem_limit_bytes=61900000
        ),
        name="layer",
    )(tokens, out_grad, slot_router, weight_in, weight_out)


def store_kernel(*refs):
    count = len(refs) // 2
    sems = refs[-1]
    copies = [
        pltpu.make_async_copy(refs[n], refs[count + n], sems.at[n]) for n in range(count)
    ]
    for copy in copies:
        copy.start()
    for copy in copies:
        copy.wait()


def store(*arrays):
    return pl.pallas_call(
        store_kernel,
        out_shape=tuple(jax.ShapeDtypeStruct(a.shape, a.dtype) for a in arrays),
        in_specs=[pl.BlockSpec(memory_space=pl.ANY)] * len(arrays),
        out_specs=(pl.BlockSpec(memory_space=pltpu.HBM),) * len(arrays),
        scratch_shapes=[pltpu.SemaphoreType.DMA((len(arrays),))],
        compiler_params=pltpu.CompilerParams(vmem_limit_bytes=1024 * 1024),
        name="store",
    )(*arrays)


def per_device(tokens, out_grad, slot_router, weight_in, weight_out):
    token_grad, router_grad, grad_first, grad_second = store(
        *layer(tokens, out_grad, slot_router, weight_in, weight_out)
    )
    return (token_grad, router_grad.T, grad_first, grad_second)


def solution(mesh):
    return jax.shard_map(
        per_device,
        mesh=mesh,
        in_specs=(
            P(("expert", "hidden"), None),
            P(("expert", "hidden"), None),
            P(),
            P("expert", None, "hidden"),
            P("expert", "hidden", None),
        ),
        out_specs=(
            P(("expert", "hidden"), None),
            P("hidden", "expert"),
            P("expert", None, "hidden"),
            P("expert", "hidden", None),
        ),
        check_vma=False,
    )
```
